32 devices in a mesh: member: 8 (over y, x, core), region: 4 (over z).
Axes of the slice: x: 2, y: 2, z: 4, core: 2. Of those that a mesh axis runs over, the one named last changes fastest.
Arguments:
- state: bfloat16 [16, 64, 4096], P('member', 'region'), may hold values from -6 to 6
- diffusivity: float32 [64, 4096], P('region'), may hold values from 0.05 to 0.45
- model_perturbation: bfloat16 [2, 16, 64, 4096], P(None, 'member', 'region'), may hold values from -3 to 3
- obs_values: float32 [2, 128, 16], P(None, 'region'), may hold values from -14 to 14
- obs_prec: float32 [128, 16], P('region'), may hold values from 0.5 to 2
- obs_tile: int32 [128], P('region'), may hold values from 0 to 15
- obs_cell: int32 [128, 16], P('region'), may hold values from 0 to 4095
- pattern: int32 [64, 6], P('region'), may hold values from 0 to 31
- loc_weight: float32 [64, 6], P('region'), may hold values from 0.02 to 0.2
- anc_member: int32 [2, 4, 16, 16, 1], P(None, 'region', 'member'), may hold values from 0 to 7; in each aligned block of 32 rows (0 to 31, 32 to 63, ..., all dimensions but the last counted through in order) at most 8 rows name the same one
- anc_slot: int32 [2, 4, 16, 16], P(None, 'region', 'member'), may hold values from 0 to 1
Outputs:
- analysis: bfloat16 [16, 64, 4096], P('member', 'region')
- analysis_mean: float32 [2, 64, 4096], P(None, 'region', 'member')
The draws below stay inside these ranges and needn't reach their ends.
Inputs may be any that keep to these rules, and one draw needn't show every extreme that they name: `anc_member`: within one cycle, among the 32 particle tiles of one device (one member index, one region), at most 8 ancestors lie on the same member index.
All inputs are finite; a program needn't handle non-finite values.
Results may differ from the reference program's by a relative error of at most 0.0046.
Values may be sent and summed in bfloat16 or wider, within the bound.
No kernel may reach another device: no remote copies, remote signals or barrier semaphores. Data moves between devices by JAX's collectives and lax.ppermute only.
A program may use at most 64 MiB of HBM per device.

```python
import math
import jax
import jax.numpy as jnp
import numpy as np
from jax import lax

POINTS_PER_PATCH = 4096
PART_DEV = 2
PATCHES_PER_AREA = 16
CYCLES = 2
STEPS = 2
OB = 16
NEAR = 6
BLK_DEV = 32
MOST = 8
ENSEMBLE_SIZE = 16
PATCHES_OVERALL = 64
NB = 128
NREG = 4
N_MEMBER = 8
N_REGION = 4


def draw_obs_values(key, part):
    first = jax.random.fold_in(key, 0)
    return jnp.clip(jax.random.normal(first, (CYCLES, NB, OB), jnp.float32), -4.0, 4.0)


def block_roles(key):
    base = jax.random.fold_in(key, 7)
    roles = jax.random.randint(jax.random.fold_in(base, 1), (NB,), 0, 4)
    spots = jax.random.randint(jax.random.fold_in(base, 2), (NB,), 0, PATCHES_PER_AREA)
    return (base, roles, spots)


def draw_obs_tile(key, part):
    base, roles, spots = block_roles(key)
    placed = jnp.where(roles == 0, 0, jnp.where(roles == 1, PATCHES_PER_AREA - 1, spots))
    return placed.astype(jnp.int32)


def draw_obs_cell(key, part):
    base, roles, spots = block_roles(key)
    nearby = jax.random.randint(jax.random.fold_in(base, 3), (NB, OB), 0, 2)
    anywhere = jax.random.randint(jax.random.fold_in(base, 4), (NB, OB), 0, POINTS_PER_PATCH)
    cells = jnp.where(roles[:, None] == 0, nearby, jnp.where(roles[:, None] == 1, POINTS_PER_PATCH - 1 - nearby, anywhere))
    return cells.astype(jnp.int32)


def plant(array, stream_key, least, top_value):
    place = [jax.random.randint(jax.random.fold_in(stream_key, axis), (), 0, length) for axis, length in enumerate(array.shape)]
    widest = array.shape.index(max(array.shape))
    beside = place[:widest] + [(place[widest] + 1) % array.shape[widest]] + place[widest + 1:]
    return array.at[tuple(place)].set(least).at[tuple(beside)].set(top_value)


def block_scale(own_key, dims, cuts, low, top_value):
    def one(position, parts):
        heights = jax.random.uniform(jax.random.fold_in(jax.random.fold_in(own_key, 6), position), (parts,), jnp.float32, low / len(cuts), top_value / len(cuts))
        return jnp.repeat(jnp.exp(heights), dims[position] // parts).reshape((-1,) + (1,) * (len(dims) - position - 1))

    level = one(*cuts[0])
    for cut in cuts[1:]:
        level = level * one(*cut)
    return level


def assign_block(own_key, own, number, rows, amount, top, most, lean):
    ranking = jax.random.permutation(own_key, amount)
    packed, common = portions_of(amount, rows * top, most, lean, True), portions_of(amount, rows * top, most, lean, False)
    places = jnp.arange(amount)

    def named(tallies, offset_by):
        used = int((tallies > 0).sum())
        fixed = max(1, used // 4)
        moved = fixed + (places - fixed + offset_by * (used - fixed)) % max(1, amount - fixed)
        return jnp.zeros((amount,), jnp.int32).at[ranking[jnp.where(places < fixed, places, moved)]].set(jnp.asarray(tallies, jnp.int32))

    tallies = jnp.where(number % 4 == 0, named(packed, number // 4), named(common, number - number // 4 - 1))
    mixed = jax.random.permutation(jax.random.fold_in(own, 3), amount)
    giver, sink = mixed[0:amount // 2 * 2:2], mixed[1:amount // 2 * 2:2]
    margin = jnp.minimum(tallies[giver] - 1, most - tallies[sink]) // 2
    margin = jnp.where((giver == ranking[0]) | (sink == ranking[0]) | (tallies[sink] == 0), 0, jnp.maximum(margin, 0))
    moved = jax.random.randint(jax.random.fold_in(own, 4), (amount // 2,), 0, 1 << 20) % (margin + 1)
    tallies = tallies.at[giver].add(-moved).at[sink].add(moved)
    members = jnp.searchsorted(jnp.cumsum(tallies), jnp.arange(rows * top), side="right").astype(jnp.int32)
    table = members.reshape(top, rows).T
    table = table[jax.random.permutation(jax.random.fold_in(own, 1), rows)]
    offset_by = jax.random.randint(jax.random.fold_in(own, 2), (rows, 1), 0, top)
    return jnp.take_along_axis(table, (jnp.arange(top)[None, :] + offset_by) % top, axis=1)


def portions_of(amount, total, most, slope, full):
    weights = [(1 << 20) // math.isqrt(rank ** slope) + 1 for rank in range(1, amount + 1)]
    largest = most if full else min(most, max(-(-total // amount), total * weights[0] // sum(weights)))
    least = 1 if total - largest >= amount - 1 else 0
    counts, rest = [largest] + [least] * (amount - 1), total - largest - least * (amount - 1)
    while rest > 0:
        candidates = [i for i in range(1, amount) if counts[i] < largest] or [i for i in range(1, amount) if counts[i] < most]
        mass, budget = sum([weights[i] for i in candidates]), rest
        for i in candidates:
            more = min(most - counts[i], max(1, budget * weights[i] // mass), rest)
            counts[i] = counts[i] + more
            rest = rest - more
    return np.array(counts)


def noise(key, shape, scale, most, shards=(), kind=jnp.bfloat16):
    result = jax.random.normal(key, shape, jnp.float32) * scale
    if len(shards) > 0:
        result = block_scale(key, shape, shards, -0.22, 0.18) * result
    return jnp.clip(result, min=-most, max=most).astype(kind)


def setup_inputs(seed: int = 0) -> dict:
    streams_of = jax.random.split(jax.random.key(seed), 12)
    state = noise(streams_of[0], (ENSEMBLE_SIZE, PATCHES_OVERALL, POINTS_PER_PATCH), 1.0, 6.0, ((0, 8), (1, 4)))
    diffusivity = jnp.clip(jnp.exp(math.log(0.45) - 2.1972245 * jax.random.uniform(streams_of[1], (PATCHES_OVERALL, POINTS_PER_PATCH), jnp.float32) ** block_scale(streams_of[1], (PATCHES_OVERALL, POINTS_PER_PATCH), ((0, 4),), -0.2, 0.2)), 0.05, 0.45)
    model_perturbation = noise(streams_of[2], (CYCLES, ENSEMBLE_SIZE, PATCHES_OVERALL, POINTS_PER_PATCH), 0.5, 3.0, ((1, 8), (2, 4)))
    obs_values = draw_obs_values(jax.random.fold_in(streams_of[11], 71), 0)
    obs_prec = jnp.clip(jnp.exp(math.log(2.0) - 1.3862944 * jax.random.uniform(streams_of[4], (NB, OB), jnp.float32) ** block_scale(streams_of[4], (NB, OB), ((0, 4),), -0.2, 0.2)), 0.5, 2.0)
    obs_tile = draw_obs_tile(jax.random.fold_in(streams_of[11], 71), 0)
    obs_cell = draw_obs_cell(jax.random.fold_in(streams_of[11], 71), 0)
    pattern = plant(jax.random.randint(streams_of[7], (PATCHES_OVERALL, NEAR), 0, BLK_DEV), jax.random.fold_in(streams_of[7], 1), 0, BLK_DEV - 1).astype(jnp.int32)
    loc_weight = jnp.clip(jnp.exp(math.log(0.2) - 2.3025851 * jax.random.uniform(streams_of[8], (PATCHES_OVERALL, NEAR), jnp.float32) ** block_scale(streams_of[8], (PATCHES_OVERALL, NEAR), ((0, 4),), -0.2, 0.2)), 0.02, 0.2)
    anc_member_keys = jax.random.split(jax.random.fold_in(streams_of[9], 1), CYCLES * NREG * ENSEMBLE_SIZE * PATCHES_PER_AREA // (PART_DEV * PATCHES_PER_AREA))
    anc_member_turns = jax.random.permutation(jax.random.fold_in(streams_of[9], 3), CYCLES * NREG * ENSEMBLE_SIZE * PATCHES_PER_AREA // (PART_DEV * PATCHES_PER_AREA))
    anc_member = jax.vmap(lambda own, number: assign_block(jax.random.fold_in(streams_of[9], 2), own, number, PART_DEV * PATCHES_PER_AREA, N_MEMBER, 1, MOST, 2))(anc_member_keys, anc_member_turns).reshape((CYCLES, NREG, ENSEMBLE_SIZE, PATCHES_PER_AREA, 1))
    anc_slot = plant(jax.random.randint(streams_of[10], (CYCLES, NREG, ENSEMBLE_SIZE, PATCHES_PER_AREA), 0, PART_DEV), jax.random.fold_in(streams_of[10], 1), 0, PART_DEV - 1).astype(jnp.int32)
    return {"state": state, "diffusivity": diffusivity, "model_perturbation": model_perturbation, "obs_values": obs_values, "obs_prec": obs_prec, "obs_tile": obs_tile, "obs_cell": obs_cell, "pattern": pattern, "loc_weight": loc_weight, "anc_member": anc_member, "anc_slot": anc_slot}


def prior_member_strip(seawater_grid, smoothed_strip, perturbation_strip):
    for repeat in range(STEPS):
        padded = jnp.pad(seawater_grid, ((0, 0), (1, 1)))
        seawater_grid = seawater_grid + smoothed_strip * (padded[:, :-2] - 2.0 * seawater_grid + padded[:, 2:])
    return (seawater_grid + perturbation_strip.astype(jnp.float32)).astype(jnp.bfloat16)


def reference(state, diffusivity, model_perturbation, obs_values, obs_prec, obs_tile, obs_cell, pattern, loc_weight, anc_member, anc_slot):
    strip_extent = PATCHES_OVERALL * POINTS_PER_PATCH
    smoothed_strip = diffusivity.reshape(1, strip_extent)
    block_region = jnp.arange(NB, dtype=jnp.int32) // BLK_DEV
    measured_vector = ((block_region * PATCHES_PER_AREA + obs_tile)[:, None] * POINTS_PER_PATCH + obs_cell).astype(jnp.int32)
    patch_labels = jnp.arange(PATCHES_OVERALL, dtype=jnp.int32)
    pattern_glob = ((patch_labels // PATCHES_PER_AREA) * BLK_DEV)[:, None] + pattern
    seawater_grid = state.reshape(ENSEMBLE_SIZE, strip_extent).astype(jnp.float32)
    mean_list = []
    for update_ordinal in range(CYCLES):
        prior_ensemble = prior_member_strip(seawater_grid, smoothed_strip, model_perturbation[update_ordinal].reshape(ENSEMBLE_SIZE, strip_extent))
        modelled_readings = prior_ensemble[:, measured_vector].astype(jnp.float32)
        misses = obs_values[update_ordinal] - modelled_readings
        misfit = 0.5 * jnp.sum(obs_prec * misses * misses, axis=-1)
        loglik = jnp.sum(loc_weight * misfit[:, pattern_glob], axis=-1)
        lowest = jnp.min(loglik, axis=0)
        unscaled = jnp.exp(lowest - loglik)
        totals = jnp.sum(unscaled, axis=0)
        sorted_into_areas = prior_ensemble.reshape(ENSEMBLE_SIZE, N_REGION, PATCHES_PER_AREA, POINTS_PER_PATCH)
        weights_region = unscaled.reshape(ENSEMBLE_SIZE, N_REGION, PATCHES_PER_AREA)

        def region_sum(region_index):
            cells = lax.dynamic_index_in_dim(sorted_into_areas, region_index, 1, keepdims=False).astype(jnp.float32)
            scales = lax.dynamic_index_in_dim(weights_region, region_index, 1, keepdims=False)
            return jnp.einsum('pt,ptc->tc', scales, cells)

        numerator = lax.map(region_sum, jnp.arange(N_REGION, dtype=jnp.int32)).reshape(PATCHES_OVERALL, POINTS_PER_PATCH)
        mean_list.append(numerator / totals[:, None])
        ancestor_member = anc_member[update_ordinal, :, :, :, 0] * PART_DEV + anc_slot[update_ordinal]
        ancestor_member = jnp.transpose(ancestor_member, (1, 0, 2)).reshape(ENSEMBLE_SIZE, PATCHES_OVERALL)
        redrawn_ensemble = prior_ensemble.reshape(ENSEMBLE_SIZE, PATCHES_OVERALL, POINTS_PER_PATCH)[ancestor_member, patch_labels[None, :]]
        seawater_grid = redrawn_ensemble.reshape(ENSEMBLE_SIZE, strip_extent).astype(jnp.float32)
    return redrawn_ensemble, jnp.stack(mean_list)
```

```python
import jax
import jax.numpy as jnp
from jax import lax
from jax.experimental import pallas as pl
from jax.experimental.pallas import tpu as pltpu
from jax.sharding import PartitionSpec as P

CYCLES = 2
STEPS = 2
LANES = 128
F32 = jnp.float32
BF16 = jnp.bfloat16
I32 = jnp.int32
PARAMS = pltpu.CompilerParams(vmem_limit_bytes=48 * 1024 * 1024)


def iota(shape, dim):
    return lax.broadcasted_iota(I32, shape, dim)


def whole_spec(shape):
    zeros = (0,) * len(shape)
    return pl.BlockSpec(shape, lambda i: zeros)


def call(kernel, outs, args, specs=None, name=None):
    specs = specs or [whole_spec(a.shape) for a in args]
    return pl.pallas_call(
        kernel,
        out_shape=[jax.ShapeDtypeStruct(s, d) for s, d in outs],
        grid=(1,),
        in_specs=specs,
        out_specs=[whole_spec(s) for s, _ in outs],
        compiler_params=PARAMS,
        name=name,
    )(*args)


def column_of(row):
    n = row.shape[1]
    square = jnp.broadcast_to(row, (n, n))
    return jnp.sum(jnp.where(iota((n, n), 0) == iota((n, n), 1), square, 0), axis=1, keepdims=True)


def make_prepare(members, capacity, parts, tiles):
    def kernel(st0, st1, df0, df1, pb0, pb1, am, slot, up, down, req, keys):
        for ref, st, df, pb, t in ((up, st1, df1, pb1, tiles - 1), (down, st0, df0, pb0, 0)):
            rows = [st[p, t:t + 1, :].astype(F32) for p in range(parts)]
            rows += [df[t:t + 1, :]]
            rows += [pb[0, p, t:t + 1, :].astype(F32) for p in range(parts)]
            for p in range(parts):
                code = am[0, p:p + 1, t:t + 1] * capacity + slot[0, p:p + 1, t:t + 1]
                rows.append(jnp.broadcast_to(code.astype(F32), (1, LANES)))
            for i, row in enumerate(rows):
                ref[i:i + 1, :] = row
            for i in range(len(rows), ref.shape[0]):
                ref[i:i + 1, :] = jnp.zeros((1, LANES), F32)
        before = (iota((tiles, tiles), 0) < iota((tiles, tiles), 1)).astype(F32)
        slots = members * capacity
        for c in range(CYCLES):
            seen = jnp.zeros((members, 1), F32)
            wanted = jnp.full((slots, 1), -1, I32)
            for p in range(parts):
                source = am[c, p:p + 1, :]
                named = (iota((members, tiles), 0) == source).astype(F32)
                earlier = seen + jnp.dot(named, before, preferred_element_type=F32)
                rank = jnp.sum(named * earlier, axis=0, keepdims=True).astype(I32)
                seen = seen + jnp.sum(named, axis=1, keepdims=True)
                key = source * capacity + rank
                code = slot[c, p:p + 1, :] * tiles + iota((1, tiles), 1)
                hit = jnp.where(iota((slots, tiles), 0) == key, code, -1)
                wanted = jnp.maximum(wanted, jnp.max(hit, axis=1, keepdims=True))
                keys[c, p * tiles:(p + 1) * tiles, :] = jnp.broadcast_to(column_of(key), (tiles, LANES))
            wide = jnp.broadcast_to(wanted, (slots, LANES))
            req[:, c * capacity:(c + 1) * capacity, :] = wide.reshape(members, capacity, LANES)

    return kernel


def widen(x, left, right):
    tiles = x.shape[0]
    row = iota((tiles, LANES), 0)
    before = jnp.where(row == 0, left, pltpu.roll(x[:, -LANES:], 1, 0))
    after = jnp.where(row == tiles - 1, right, pltpu.roll(x[:, :LANES], tiles - 1, 0))
    return jnp.concatenate([before, x, after], axis=1)


def diffuse(x, d):
    n = x.shape[1]
    for _ in range(STEPS):
        x = x + d * (pltpu.roll(x, 1, 1) - 2.0 * x + pltpu.roll(x, n - 1, 1))
    return x


def pick_rows(wanted, rows):
    m = rows.shape[0]
    n = wanted.shape[0]
    choice = (wanted[:, :m] == iota((n, m), 1)).astype(F32).astype(BF16)
    return jnp.dot(choice, rows, preferred_element_type=F32)


def send_rows(req, prior, out, first, capacity, cells):
    members = req.shape[0]
    wanted = req[:, first:first + capacity, :].reshape(members * capacity, LANES)
    sent = pick_rows(wanted, prior)
    out[:, :, :cells] = sent.reshape(members, capacity, cells).astype(BF16)


def assess(prior, obs_i, terms, pattern, weight, parts, tiles, cells):
    blocks = cells // LANES
    rows = tiles * blocks
    count = obs_i.shape[1]
    stacked = jnp.concatenate(
        [jnp.concatenate([x[:, k * LANES:(k + 1) * LANES] for k in range(blocks)], axis=0) for x in prior],
        axis=1,
    )
    choice = (iota((rows, count), 0) == obs_i[0:1, :]).astype(F32).astype(BF16)
    lines = lax.dot_general(stacked, choice, (((0,), (0,)), ((), ())), preferred_element_type=F32)
    lane = (iota((LANES, count), 0) == obs_i[1:2, :])
    prec, value, group = terms
    local = jnp.zeros((tiles, count), F32)
    for k in range(pattern.shape[1]):
        local = local + jnp.where(pattern[:, k:k + 1] == group, weight[:, k:k + 1], 0.0)
    score = []
    for p in range(parts):
        predicted = jnp.sum(jnp.where(lane, lines[p * LANES:(p + 1) * LANES, :], 0.0), axis=0, keepdims=True)
        miss = value - predicted
        term = 0.5 * (prec * miss * miss)
        score.append(jnp.sum(local * term, axis=1, keepdims=True))
    least = score[0]
    for s in score[1:]:
        least = jnp.minimum(least, s)
    scale = [jnp.exp(least - s) for s in score]
    total = scale[0]
    for s in scale[1:]:
        total = total + s
    weighted = scale[0] * prior[0].astype(F32)
    for s, x in zip(scale[1:], prior[1:]):
        weighted = weighted + s * x.astype(F32)
    return least, total, weighted


def pieces(x):
    high = x.astype(BF16).astype(F32)
    middle = (x - high).astype(BF16).astype(F32)
    low = (x - high - middle).astype(BF16).astype(F32)
    return high, middle, low


def make_first(capacity, parts, tiles, cells):
    def kernel(state, diff, pert, below, above, req, send, prior_out):
        d = widen(diff[...], below[parts:parts + 1, :], above[parts:parts + 1, :])
        edge = []
        prior = []
        for p in range(parts):
            x = widen(state[p].astype(F32), below[p:p + 1, :], above[p:p + 1, :])
            x = diffuse(x, d)
            now = (x[:, LANES:LANES + cells] + pert[0, p].astype(F32)).astype(BF16)
            prior.append(now)
            prior_out[p] = now
            q = parts + 1 + p
            low = x[0:1, :LANES] + below[q:q + 1, :]
            high = x[tiles - 1:tiles, LANES + cells:] + above[q:q + 1, :]
            edge.append(jnp.where(iota((1, LANES), 1) < LANES // 2, high, low))
        send_rows(req, jnp.concatenate(prior, axis=0), send, 0, capacity, cells)
        row = iota((capacity, LANES), 0)
        misc = jnp.zeros((capacity, LANES), F32)
        for p in range(parts):
            misc = jnp.where(row == p, edge[p], misc)
        members = send.shape[0]
        send[:, :, cells:] = jnp.broadcast_to(misc.astype(BF16)[None], (members, capacity, LANES))

    return kernel


def make_assess(parts, tiles, cells):
    def kernel(prior, obs_i, obs_f, pattern, weight, part, stats):
        terms = (obs_f[0:1, :], obs_f[1:2, :], obs_i[2:3, :])
        least, total, weighted = assess(
            [prior[p] for p in range(parts)], obs_i, terms, pattern[...], weight[...], parts, tiles, cells
        )
        part[...] = weighted.astype(BF16)
        lane = iota((tiles, LANES), 1)
        stats[...] = jnp.where(lane == 0, least, total)

    return kernel


def make_second(members, capacity, parts, tiles, cells):
    share = cells // members
    groups = tiles // capacity

    def kernel(got, keys, diff, pert, below, above, req, part1, stats1, obs_i, obs_f, pattern, weight, send):
        slots = members * capacity
        arrived = got[...].reshape(slots, cells + LANES)
        field = pick_rows(keys[0], arrived[:, :cells])
        lines = arrived[:, cells:]
        q = 2 * parts + 1
        first = pick_rows(below[q:q + parts, :].astype(I32), lines)
        last = pick_rows(above[q:q + parts, :].astype(I32), lines)
        d = widen(diff[...], below[parts:parts + 1, :], above[parts:parts + 1, :])
        prior = []
        for p in range(parts):
            x = widen(field[p * tiles:(p + 1) * tiles, :], first[p:p + 1, :], last[p:p + 1, :])
            x = diffuse(x, d)[:, LANES:LANES + cells]
            prior.append((x + pert[0, p].astype(F32)).astype(BF16))
        send_rows(req, jnp.concatenate(prior, axis=0), send, capacity, capacity, cells)
        terms = (obs_f[0:1, :], obs_f[2:3, :], obs_i[2:3, :])
        least, total, weighted = assess(prior, obs_i, terms, pattern[...], weight[...], parts, tiles, cells)
        kept = (part1[...].astype(F32), weighted)
        for c in range(CYCLES):
            for m in range(members):
                for g in range(groups):
                    at = cells + (c * groups + g) * share
                    block = kept[c][g * capacity:(g + 1) * capacity, m * share:(m + 1) * share]
                    send[m, :, at:at + share] = block.astype(BF16)
        lane = iota((capacity, LANES), 1)
        misc = jnp.zeros((capacity, LANES), F32)
        spot = 0
        for x in (stats1[:, 0:1], stats1[:, 1:2], least, total):
            for piece in pieces(x):
                for g in range(groups):
                    misc = jnp.where(lane == spot, piece[g * capacity:(g + 1) * capacity, :], misc)
                    spot += 1
        at = cells + CYCLES * groups * share
        send[:, :, at:] = jnp.broadcast_to(misc.astype(BF16)[None], (members, capacity, LANES))

    return kernel


def make_last(members, capacity, parts, tiles, cells):
    share = cells // members
    groups = tiles // capacity

    def kernel(got, keys, analysis, mean):
        slots = members * capacity
        rows = got[:, :, :cells].reshape(slots, cells)
        picked = pick_rows(keys[1], rows)
        for p in range(parts):
            analysis[p] = picked[p * tiles:(p + 1) * tiles, :].astype(BF16)
        at = cells + CYCLES * groups * share
        misc = got[:, :, at:].astype(F32)
        for c in range(CYCLES):
            for g in range(groups):
                pair = []
                for kind in range(2):
                    spot = (c * 2 + kind) * 3 * groups + g
                    x = misc[:, :, spot:spot + 1]
                    for piece in range(1, 3):
                        x = x + misc[:, :, spot + piece * groups:spot + piece * groups + 1]
                    pair.append(x)
                least, total = pair
                scale = jnp.exp(jnp.min(least, axis=0, keepdims=True) - least)
                start = cells + (c * groups + g) * share
                part = got[:, :, start:start + share].astype(F32)
                top = jnp.sum(scale * part, axis=0)
                mean[c, g * capacity:(g + 1) * capacity, :] = top / jnp.sum(scale * total, axis=0)

    return kernel


def body(
    state,
    diffusivity,
    model_perturbation,
    obs_values,
    obs_prec,
    obs_tile,
    obs_cell,
    pattern,
    loc_weight,
    anc_member,
    anc_slot,
):
    parts, tiles, cells = state.shape
    members = lax.axis_size("member")
    regions = lax.axis_size("region")
    capacity = max(2, 2 * parts * tiles // members)
    share = cells // members
    groups = tiles // capacity
    blocks, per_block = obs_cell.shape
    count = blocks * per_block
    member_of = anc_member.reshape(CYCLES, parts, tiles)
    slot_of = anc_slot.reshape(CYCLES, parts, tiles)

    ends = cells // LANES - 1

    def block(shape, at):
        lead = (0,) * (len(shape) - 1)
        return pl.BlockSpec(shape, lambda i: lead + (at,))

    up, down, req, keys = call(
        make_prepare(members, capacity, parts, tiles),
        [((8, LANES), F32), ((8, LANES), F32), ((members, CYCLES * capacity, LANES), I32), ((CYCLES, parts * tiles, LANES), I32)],
        [state, state, diffusivity, diffusivity, model_perturbation, model_perturbation, member_of, slot_of],
        [
            block((parts, tiles, LANES), 0),
            block((parts, tiles, LANES), ends),
            block((tiles, LANES), 0),
            block((tiles, LANES), ends),
            block((1, parts, tiles, LANES), 0),
            block((1, parts, tiles, LANES), ends),
            whole_spec(member_of.shape),
            whole_spec(slot_of.shape),
        ],
        name="prepare",
    )
    forward = [(i, i + 1) for i in range(regions - 1)]
    below = lax.ppermute(up, "region", forward)
    above = lax.ppermute(down, "region", [(j, i) for i, j in forward])
    asked = lax.all_to_all(req, "member", split_axis=0, concat_axis=0, tiled=True)

    cell_block = (obs_cell // LANES) * tiles + obs_tile[:, None]
    group = jnp.broadcast_to(jnp.arange(blocks, dtype=I32)[:, None], obs_cell.shape)
    obs_i = jnp.stack([cell_block, obs_cell % LANES, group]).reshape(3, count)
    obs_f = jnp.concatenate([obs_prec[None], obs_values]).reshape(1 + CYCLES, count)

    def noise_spec(c):
        return pl.BlockSpec((1, parts, tiles, cells), lambda i: (c, 0, 0, 0))

    send, prior = call(
        make_first(capacity, parts, tiles, cells),
        [((members, capacity, cells + LANES), BF16), ((parts, tiles, cells), BF16)],
        [state, diffusivity, model_perturbation, below, above, asked],
        [
            whole_spec(state.shape),
            whole_spec(diffusivity.shape),
            noise_spec(0),
            whole_spec(below.shape),
            whole_spec(above.shape),
            whole_spec(asked.shape),
        ],
        name="forecast_first",
    )
    got = lax.all_to_all(send, "member", split_axis=0, concat_axis=0, tiled=True)
    part, stats = call(
        make_assess(parts, tiles, cells),
        [((tiles, cells), BF16), ((tiles, LANES), F32)],
        [prior, obs_i, obs_f, pattern, loc_weight],
        name="assess_first",
    )
    width = cells + CYCLES * groups * share + LANES
    args = [got, keys, diffusivity, model_perturbation, below, above, asked, part, stats, obs_i, obs_f, pattern, loc_weight]
    specs = [whole_spec(a.shape) for a in args]
    specs[3] = noise_spec(1)
    (send,) = call(
        make_second(members, capacity, parts, tiles, cells),
        [((members, capacity, width), BF16)],
        args,
        specs,
        name="forecast_second",
    )
    got = lax.all_to_all(send, "member", split_axis=0, concat_axis=0, tiled=True)
    return tuple(
        call(
            make_last(members, capacity, parts, tiles, cells),
            [(state.shape, BF16), ((CYCLES, tiles, share), F32)],
            [got, keys],
            name="finish",
        )
    )


def solution(mesh):
    in_specs = (
        P("member", "region", None),
        P("region", None),
        P(None, "member", "region", None),
        P(None, "region", None),
        P("region", None),
        P("region"),
        P("region", None),
        P("region", None),
        P("region", None),
        P(None, "region", "member", None, None),
        P(None, "region", "member", None),
    )
    out_specs = (P("member", "region", None), P(None, "region", "member"))
    return jax.shard_map(body, mesh=mesh, in_specs=in_specs, out_specs=out_specs, check_vma=False)
```

```python
import jax
import jax.numpy as jnp
from jax import lax
from jax.experimental import pallas as pl
from jax.experimental.pallas import tpu as pltpu
from jax.sharding import PartitionSpec as P

CYCLES = 2
STEPS = 2
LANES = 128
F32 = jnp.float32
BF16 = jnp.bfloat16
I32 = jnp.int32
PARAMS = pltpu.CompilerParams(vmem_limit_bytes=48 * 1024 * 1024)


def iota(shape, dim):
    return lax.broadcasted_iota(I32, shape, dim)


def whole_spec(shape):
    zeros = (0,) * len(shape)
    return pl.BlockSpec(shape, lambda i: zeros)


def call(kernel, outs, args, specs=None, name=None):
    specs = specs or [whole_spec(a.shape) for a in args]
    return pl.pallas_call(
        kernel,
        out_shape=[jax.ShapeDtypeStruct(s, d) for s, d in outs],
        grid=(1,),
        in_specs=specs,
        out_specs=[whole_spec(s) for s, _ in outs],
        compiler_params=PARAMS,
        name=name,
    )(*args)


def column_of(row):
    n = row.shape[1]
    square = jnp.broadcast_to(row, (n, n))
    return jnp.sum(jnp.where(iota((n, n), 0) == iota((n, n), 1), square, 0), axis=1, keepdims=True)


def here():
    return lax.axis_index("region"), lax.axis_index("member")


def make_prepare(regions, members, capacity, parts, tiles):
    width = 2 * STEPS

    def kernel(st0, st1, df0, df1, pb0, pb1, am, slot, note, keys):
        r, m = here()
        lane = iota((1, LANES), 1)
        halo = []
        for st, df, pb, t in ((st1, df1, pb1, tiles - 1), (st0, df0, pb0, 0)):
            top = t > 0
            rows = [st[p, t:t + 1, :].astype(F32) for p in range(parts)]
            rows += [df[t:t + 1, :]]
            rows += [pb[0, p, t:t + 1, :].astype(F32) for p in range(parts)]
            out = jnp.zeros((1, LANES), F32)
            for i, row in enumerate(rows):
                shift = (LANES - 8 * i) % LANES if top else 8 * i
                first = LANES - 8 * i - width if top else 8 * i
                moved = pltpu.roll(row, shift, 1) if shift else row
                out = jnp.where((lane >= first) & (lane < first + width), moved, out)
            for p in range(parts):
                code = am[0, p:p + 1, t:t + 1] * capacity + slot[0, p:p + 1, t:t + 1]
                out = jnp.where(lane == (p if top else LANES - 1 - p), code.astype(F32), out)
            halo.append(out)
        before = (iota((tiles, tiles), 0) < iota((tiles, tiles), 1)).astype(F32)
        asked = jnp.full((members, LANES), -1.0, F32)
        for c in range(CYCLES):
            seen = jnp.zeros((members, 1), F32)
            for p in range(parts):
                source = am[c, p:p + 1, :]
                named = (iota((members, tiles), 0) == source).astype(F32)
                earlier = seen + jnp.dot(named, before, preferred_element_type=F32)
                rank = jnp.sum(named * earlier, axis=0, keepdims=True).astype(I32)
                seen = seen + jnp.sum(named, axis=1, keepdims=True)
                code = slot[c, p:p + 1, :] * tiles + iota((1, tiles), 1)
                spot = (iota((LANES, tiles), 0) == c * capacity + rank).astype(F32)
                asked = asked + lax.dot_general(
                    named * (code + 1).astype(F32), spot, (((1,), (1,)), ((), ())), preferred_element_type=F32
                )
                column = column_of(source * capacity + rank)
                keys[c, p * tiles:(p + 1) * tiles, :] = jnp.broadcast_to(column, (tiles, LANES))
        mine = iota((members, LANES), 0) == m
        for q in range(regions):
            edge = jnp.where(q == r + 1, halo[0], halo[1])
            note[q] = jnp.where(q == r, asked, jnp.where(mine, edge, 0.0))

    return kernel


def halo_rows(note, regions, parts):
    r, m = here()
    low = note[jnp.maximum(r - 1, 0), pl.ds(m, 1), :]
    high = note[jnp.minimum(r + 1, regions - 1), pl.ds(m, 1), :]
    low = jnp.where(r > 0, low, 0.0)
    high = jnp.where(r < regions - 1, high, 0.0)

    def field(i):
        if i == 0:
            return low, high
        return pltpu.roll(low, 8 * i, 1), pltpu.roll(high, LANES - 8 * i, 1)

    def code():
        row = iota((parts, LANES), 0)
        below = jnp.zeros((parts, LANES), I32)
        above = jnp.zeros((parts, LANES), I32)
        for p in range(parts):
            below = jnp.where(row == p, low[:, p:p + 1].astype(I32), below)
            above = jnp.where(row == p, high[:, LANES - 1 - p:LANES - p].astype(I32), above)
        return below, above

    return field, code


def widen(x, left, right):
    tiles = x.shape[0]
    row = iota((tiles, LANES), 0)
    before = jnp.where(row == 0, left, pltpu.roll(x[:, -LANES:], 1, 0))
    after = jnp.where(row == tiles - 1, right, pltpu.roll(x[:, :LANES], tiles - 1, 0))
    return jnp.concatenate([before, x, after], axis=1)


def diffuse(x, d):
    n = x.shape[1]
    for _ in range(STEPS):
        x = x + d * (pltpu.roll(x, 1, 1) - 2.0 * x + pltpu.roll(x, n - 1, 1))
    return x


def pick_rows(wanted, rows):
    m = rows.shape[0]
    n = wanted.shape[0]
    choice = (wanted[:, :m] == iota((n, m), 1)).astype(F32).astype(BF16)
    return jnp.dot(choice, rows, preferred_element_type=F32)


def send_rows(note, prior, out, cycle, capacity, cells):
    r, _ = here()
    asked = note[r]
    members = asked.shape[0]
    slots = members * capacity
    spread = jnp.broadcast_to(asked[:, None, :], (members, capacity, LANES)).reshape(slots, LANES)
    mine = iota((slots, LANES), 1) == cycle * capacity + iota((slots, LANES), 0) % capacity
    wanted = jnp.sum(jnp.where(mine, spread, 0.0), axis=1, keepdims=True).astype(I32)
    sent = pick_rows(jnp.broadcast_to(wanted, (slots, LANES)), prior)
    out[:, :, :cells] = sent.reshape(members, capacity, cells).astype(BF16)


def make_observe(blocks, per_block, tiles, near):
    count = blocks * per_block

    def kernel(tile, cell, prec, value, pattern, weight, where, terms, local):
        def line(x):
            wide = jnp.concatenate([x] * per_block, axis=1)
            own = iota((per_block, count), 1) // blocks == iota((per_block, count), 0)
            return jnp.sum(jnp.where(own, wide, 0), axis=0, keepdims=True)

        at = line(cell[...])
        row = (at // LANES) * tiles + jnp.concatenate([tile[...]] * per_block, axis=1)
        pick = iota((2, count), 0) == 0
        where[...] = jnp.where(pick, row, at % LANES)
        terms[0:1, :] = line(prec[...])
        for c in range(CYCLES):
            terms[c + 1:c + 2, :] = line(value[c])
        group = iota((tiles, count), 1) % blocks
        total = jnp.zeros((tiles, count), F32)
        for k in range(near):
            total = total + jnp.where(column_of(pattern[k:k + 1, :]) == group, column_of(weight[k:k + 1, :]), 0.0)
        local[...] = total

    return kernel


def assess(prior, where, prec, value, local, parts, tiles, cells):
    blocks = cells // LANES
    rows = tiles * blocks
    count = where.shape[1]
    stacked = jnp.concatenate(
        [jnp.concatenate([x[:, k * LANES:(k + 1) * LANES] for k in range(blocks)], axis=0) for x in prior],
        axis=1,
    )
    choice = (iota((rows, count), 0) == where[0:1, :]).astype(F32).astype(BF16)
    lines = lax.dot_general(stacked, choice, (((0,), (0,)), ((), ())), preferred_element_type=F32)
    lane = iota((LANES, count), 0) == where[1:2, :]
    score = []
    for p in range(parts):
        predicted = jnp.sum(jnp.where(lane, lines[p * LANES:(p + 1) * LANES, :], 0.0), axis=0, keepdims=True)
        miss = value - predicted
        term = 0.5 * (prec * miss * miss)
        score.append(jnp.sum(local * term, axis=1, keepdims=True))
    least = score[0]
    for s in score[1:]:
        least = jnp.minimum(least, s)
    scale = [jnp.exp(least - s) for s in score]
    total = scale[0]
    for s in scale[1:]:
        total = total + s
    weighted = scale[0] * prior[0].astype(F32)
    for s, x in zip(scale[1:], prior[1:]):
        weighted = weighted + s * x.astype(F32)
    return least, total, weighted


def pieces(x):
    high = x.astype(BF16).astype(F32)
    middle = (x - high).astype(BF16).astype(F32)
    low = (x - high - middle).astype(BF16).astype(F32)
    return high, middle, low


def pack_mean(out, at, least, total, weighted):
    members, capacity, _ = out.shape
    tiles, cells = weighted.shape
    share = cells // members
    groups = tiles // capacity
    weighted = weighted.astype(BF16)
    for g in range(groups):
        rows = weighted[g * capacity:(g + 1) * capacity, :]
        for m in range(members):
            out[m, :, at + g * share:at + (g + 1) * share] = rows[:, m * share:(m + 1) * share]
    lane = iota((capacity, LANES), 1)
    misc = jnp.zeros((capacity, LANES), F32)
    spot = 0
    for x in (least, total):
        for piece in pieces(x):
            for g in range(groups):
                misc = jnp.where(lane == spot, piece[g * capacity:(g + 1) * capacity, :], misc)
                spot += 1
    out[:, :, at + groups * share:at + groups * share + LANES] = jnp.broadcast_to(misc.astype(BF16)[None], (members, capacity, LANES))


def unpack_mean(got, at, tiles, share):
    _, capacity, _ = got.shape
    groups = tiles // capacity
    misc = got[:, :, at + groups * share:at + groups * share + LANES].astype(F32)
    means = []
    for g in range(groups):
        pair = []
        for kind in range(2):
            spot = [(kind * 3 + piece) * groups + g for piece in range(3)]
            high, middle, low = [misc[:, :, i:i + 1] for i in spot]
            pair.append(high + middle + low)
        least, total = pair
        scale = jnp.exp(jnp.min(least, axis=0, keepdims=True) - least)
        part = got[:, :, at + g * share:at + (g + 1) * share].astype(F32)
        means.append(jnp.sum(scale * part, axis=0) / jnp.sum(scale * total, axis=0))
    return means


def make_first(regions, capacity, parts, tiles, cells):
    def kernel(state, diff, pert, note, send, prior_out):
        field, _ = halo_rows(note, regions, parts)
        d = widen(diff[...], *field(parts))
        edge = []
        prior = []
        for p in range(parts):
            x = widen(state[p].astype(F32), *field(p))
            x = diffuse(x, d)
            now = (x[:, LANES:LANES + cells] + pert[0, p].astype(F32)).astype(BF16)
            prior.append(now)
            prior_out[p] = now
            low, high = field(parts + 1 + p)
            low = low + x[0:1, :LANES]
            high = high + x[tiles - 1:tiles, LANES + cells:]
            edge.append(jnp.where(iota((1, LANES), 1) < LANES // 2, high, low))
        send_rows(note, jnp.concatenate(prior, axis=0), send, 0, capacity, cells)
        row = iota((capacity, LANES), 0)
        misc = jnp.zeros((capacity, LANES), F32)
        for p in range(parts):
            misc = jnp.where(row == p, edge[p], misc)
        members = send.shape[0]
        send[:, :, cells:] = jnp.broadcast_to(misc.astype(BF16)[None], (members, capacity, LANES))

    return kernel


def make_assess(parts, tiles, cells):
    def kernel(prior, where, terms, local, out):
        pack_mean(
            out,
            0,
            *assess(
                [prior[p] for p in range(parts)],
                where[...], terms[0:1, :], terms[1:2, :], local[...], parts, tiles, cells,
            ),
        )

    return kernel


def make_second(regions, capacity, parts, tiles, cells):
    def kernel(got, keys, diff, pert, note, where, terms, local, part, send):
        slots = got.shape[0] * capacity
        arrived = got[...].reshape(slots, cells + LANES)
        moved = pick_rows(keys[0], arrived[:, :cells])
        lines = arrived[:, cells:]
        field, code = halo_rows(note, regions, parts)
        first, last = [pick_rows(x, lines) for x in code()]
        d = widen(diff[...], *field(parts))
        prior = []
        for p in range(parts):
            x = widen(moved[p * tiles:(p + 1) * tiles, :], first[p:p + 1, :], last[p:p + 1, :])
            x = diffuse(x, d)[:, LANES:LANES + cells]
            prior.append((x + pert[0, p].astype(F32)).astype(BF16))
        send_rows(note, jnp.concatenate(prior, axis=0), send, 1, capacity, cells)
        extra = part.shape[2]
        send[:, :, cells:cells + extra] = part[...]
        pack_mean(
            send,
            cells + extra,
            *assess(prior, where[...], terms[0:1, :], terms[2:3, :], local[...], parts, tiles, cells),
        )

    return kernel


def make_last(capacity, parts, tiles, cells):
    def kernel(got, keys, analysis, mean):
        slots = got.shape[0] * capacity
        rows = got[:, :, :cells].reshape(slots, cells)
        picked = pick_rows(keys[1], rows)
        for p in range(parts):
            analysis[p] = picked[p * tiles:(p + 1) * tiles, :].astype(BF16)
        share = mean.shape[2]
        extra = tiles // capacity * share + LANES
        for c in range(CYCLES):
            for g, x in enumerate(unpack_mean(got, cells + c * extra, tiles, share)):
                mean[c, g * capacity:(g + 1) * capacity, :] = x

    return kernel


def body(
    state,
    diffusivity,
    model_perturbation,
    obs_values,
    obs_prec,
    obs_tile,
    obs_cell,
    pattern,
    loc_weight,
    anc_member,
    anc_slot,
):
    parts, tiles, cells = state.shape
    members = lax.axis_size("member")
    regions = lax.axis_size("region")
    capacity = max(2, 2 * parts * tiles // members)
    share = cells // members
    groups = tiles // capacity
    blocks, per_block = obs_cell.shape
    count = blocks * per_block
    member_of = anc_member.reshape(CYCLES, parts, tiles)
    slot_of = anc_slot.reshape(CYCLES, parts, tiles)
    near = pattern.shape[1]
    ends = cells // LANES - 1

    def block(shape, at):
        lead = (0,) * (len(shape) - 1)
        return pl.BlockSpec(shape, lambda i: lead + (at,))

    edges = [state, state, diffusivity, diffusivity, model_perturbation, model_perturbation, member_of, slot_of]
    note, keys = call(
        make_prepare(regions, members, capacity, parts, tiles),
        [((regions, members, LANES), F32), ((CYCLES, parts * tiles, LANES), I32)],
        [pltpu.with_memory_space_constraint(x, pltpu.HBM) for x in edges],
        [
            block((parts, tiles, LANES), 0),
            block((parts, tiles, LANES), ends),
            block((tiles, LANES), 0),
            block((tiles, LANES), ends),
            block((1, parts, tiles, LANES), 0),
            block((1, parts, tiles, LANES), ends),
            whole_spec(member_of.shape),
            whole_spec(slot_of.shape),
        ],
        name="prepare",
    )
    note = lax.all_to_all(
        note.reshape(regions * members, LANES), ("region", "member"), split_axis=0, concat_axis=0, tiled=True
    ).reshape(regions, members, LANES)

    where, terms, local = call(
        make_observe(blocks, per_block, tiles, near),
        [((2, count), I32), ((1 + CYCLES, count), F32), ((tiles, count), F32)],
        [obs_tile[None, :], obs_cell.T, obs_prec.T, jnp.swapaxes(obs_values, 1, 2), pattern.T, loc_weight.T],
        name="observe",
    )

    def noise_spec(c):
        return pl.BlockSpec((1, parts, tiles, cells), lambda i: (c, 0, 0, 0))

    args = [state, diffusivity, model_perturbation, note]
    specs = [whole_spec(a.shape) for a in args]
    specs[2] = noise_spec(0)
    send, prior = call(
        make_first(regions, capacity, parts, tiles, cells),
        [((members, capacity, cells + LANES), BF16), ((parts, tiles, cells), BF16)],
        args,
        specs,
        name="forecast_first",
    )
    got = lax.all_to_all(send, "member", split_axis=0, concat_axis=0, tiled=True)
    extra = groups * share + LANES
    (part,) = call(
        make_assess(parts, tiles, cells),
        [((members, capacity, extra), BF16)],
        [prior, where, terms, local],
        name="assess_first",
    )
    args = [got, keys, diffusivity, model_perturbation, note, where, terms, local, part]
    specs = [whole_spec(a.shape) for a in args]
    specs[3] = noise_spec(1)
    (send,) = call(
        make_second(regions, capacity, parts, tiles, cells),
        [((members, capacity, cells + CYCLES * extra), BF16)],
        args,
        specs,
        name="forecast_second",
    )
    got = lax.all_to_all(send, "member", split_axis=0, concat_axis=0, tiled=True)
    return tuple(
        call(
            make_last(capacity, parts, tiles, cells),
            [(state.shape, BF16), ((CYCLES, tiles, share), F32)],
            [got, keys],
            name="finish",
        )
    )


def solution(mesh):
    in_specs = (
        P("member", "region", None),
        P("region", None),
        P(None, "member", "region", None),
        P(None, "region", None),
        P("region", None),
        P("region"),
        P("region", None),
        P("region", None),
        P("region", None),
        P(None, "region", "member", None, None),
        P(None, "region", "member", None),
    )
    out_specs = (P("member", "region", None), P(None, "region", "member"))
    return jax.shard_map(body, mesh=mesh, in_specs=in_specs, out_specs=out_specs, check_vma=False)
```

```python
import jax
import jax.numpy as jnp
from jax import lax
from jax.experimental import pallas as pl
from jax.experimental.pallas import tpu as pltpu
from jax.sharding import PartitionSpec as P

CYCLES = 2
STEPS = 2
LANES = 128
F32 = jnp.float32
BF16 = jnp.bfloat16
I32 = jnp.int32
PARAMS = pltpu.CompilerParams(vmem_limit_bytes=48 * 1024 * 1024)


def iota(shape, dim):
    return lax.broadcasted_iota(I32, shape, dim)


def whole_spec(shape):
    zeros = (0,) * len(shape)
    return pl.BlockSpec(shape, lambda i: zeros)


def call(kernel, outs, args, specs=None, name=None):
    specs = specs or [whole_spec(a.shape) for a in args]
    return pl.pallas_call(
        kernel,
        out_shape=[jax.ShapeDtypeStruct(s, d) for s, d in outs],
        grid=(1,),
        in_specs=specs,
        out_specs=[whole_spec(s) for s, _ in outs],
        compiler_params=PARAMS,
        name=name,
    )(*args)


def column_of(row):
    n = row.shape[1]
    square = jnp.broadcast_to(row, (n, n))
    return jnp.sum(jnp.where(iota((n, n), 0) == iota((n, n), 1), square, 0), axis=1, keepdims=True)


def here():
    return lax.axis_index("member")


EDGE_AT = 32
STRIDE = 8


def make_prepare(members, capacity, parts, tiles):
    width = 2 * STEPS

    def kernel(st0, st1, df0, df1, pb0, pb1, am, slot, note, trail, keys):
        lane = iota((1, LANES), 1)
        last = tiles - 1
        trail[...] = jnp.zeros(trail.shape, F32)
        trail[0:1, :] = df1[last:last + 1, :]
        trail[1:2, :] = df0[0:1, :]
        edge = jnp.zeros((1, LANES), F32)
        for p in range(parts):
            for i, t in enumerate((last, 0)):
                code = slot[0, p:p + 1, t:t + 1] * members + am[0, p:p + 1, t:t + 1]
                row = 2 + i * parts + p
                trail[row:row + 1, :] = jnp.broadcast_to(code.astype(F32), (1, LANES))
            fields = (st1[p, last:last + 1, :], st0[p, 0:1, :], pb1[0, p, last:last + 1, :], pb0[0, p, 0:1, :])
            for i, x in enumerate(fields):
                to = EDGE_AT + STRIDE * (4 * p + i)
                start = 0 if i % 2 else LANES - width
                moved = pltpu.roll(x.astype(F32), (to - start) % LANES, 1)
                edge = jnp.where((lane >= to) & (lane < to + width), moved, edge)
        before = (iota((tiles, tiles), 0) < iota((tiles, tiles), 1)).astype(F32)
        asked = jnp.zeros((members, LANES), F32)
        for c in range(CYCLES):
            seen = jnp.zeros((members, 1), F32)
            for p in range(parts):
                source = am[c, p:p + 1, :]
                named = (iota((members, tiles), 0) == source).astype(F32)
                earlier = seen + jnp.dot(named, before, preferred_element_type=F32)
                rank = jnp.sum(named * earlier, axis=0, keepdims=True).astype(I32)
                seen = seen + jnp.sum(named, axis=1, keepdims=True)
                code = slot[c, p:p + 1, :] * tiles + iota((1, tiles), 1)
                spot = (iota((LANES, tiles), 0) == c * capacity + rank).astype(F32)
                asked = asked + lax.dot_general(
                    named * (code + 1).astype(F32), spot, (((1,), (1,)), ((), ())), preferred_element_type=F32
                )
                column = column_of(source * capacity + rank)
                keys[c, p * tiles:(p + 1) * tiles, :] = jnp.broadcast_to(column, (tiles, LANES))
        note[...] = jnp.where(iota((members, LANES), 1) < EDGE_AT, asked - 1.0, edge)

    return kernel


def edge_windows(own, below, above, members, parts):
    width = 2 * STEPS

    def field(note, p, i):
        at = EDGE_AT + STRIDE * (4 * p + i)
        start = 0 if i % 2 else LANES - width
        return pltpu.roll(note[:members, :], (start - at) % LANES, 1)

    low, high = [], []
    for out, before, after in ((low, below, own), (high, own, above)):
        d = jnp.concatenate([before[members:members + 1, :], after[members + 1:members + 2, :]], axis=1)
        for p in range(parts):
            x = jnp.concatenate([field(before, p, 0), field(after, p, 1)], axis=1)
            x = diffuse(x, d) + jnp.concatenate([field(before, p, 2), field(after, p, 3)], axis=1)
            out.append(x.astype(BF16).astype(F32))
    return jnp.concatenate(low, axis=0), jnp.concatenate(high, axis=0)


def patch(x, first, last):
    tiles = x.shape[0]
    row, lane = iota((tiles, LANES), 0), iota((tiles, LANES), 1)
    head = jnp.where((row == 0) & (lane < STEPS), first, x[:, :LANES])
    tail = jnp.where((row == tiles - 1) & (lane >= LANES - STEPS), last, x[:, -LANES:])
    return jnp.concatenate([head, x[:, LANES:-LANES], tail], axis=1)


def widen(x, left, right):
    tiles = x.shape[0]
    row = iota((tiles, LANES), 0)
    before = jnp.where(row == 0, left, pltpu.roll(x[:, -LANES:], 1, 0))
    after = jnp.where(row == tiles - 1, right, pltpu.roll(x[:, :LANES], tiles - 1, 0))
    return jnp.concatenate([before, x, after], axis=1)


def diffuse(x, d):
    n = x.shape[1]
    for _ in range(STEPS):
        x = x + d * (pltpu.roll(x, 1, 1) - 2.0 * x + pltpu.roll(x, n - 1, 1))
    return x


def pick_rows(wanted, rows):
    m = rows.shape[0]
    n = wanted.shape[0]
    choice = (wanted[:, :m] == iota((n, m), 1)).astype(F32).astype(BF16)
    return jnp.dot(choice, rows, preferred_element_type=F32)


def send_rows(asked, prior, out, cycle, capacity, cells):
    members = asked.shape[0]
    slots = members * capacity
    spread = jnp.broadcast_to(asked[:, None, :], (members, capacity, LANES)).reshape(slots, LANES)
    mine = iota((slots, LANES), 1) == cycle * capacity + iota((slots, LANES), 0) % capacity
    wanted = jnp.sum(jnp.where(mine, spread, 0.0), axis=1, keepdims=True).astype(I32)
    sent = pick_rows(jnp.broadcast_to(wanted, (slots, LANES)), prior)
    out[:, :, :cells] = sent.reshape(members, capacity, cells).astype(BF16)


def make_observe(blocks, per_block, tiles, near):
    count = blocks * per_block

    def kernel(tile, cell, prec, value, pattern, weight, where, terms, local):
        def line(x):
            wide = jnp.concatenate([x] * per_block, axis=1)
            own = iota((per_block, count), 1) // blocks == iota((per_block, count), 0)
            return jnp.sum(jnp.where(own, wide, 0), axis=0, keepdims=True)

        at = line(cell[...])
        row = (at // LANES) * tiles + jnp.concatenate([tile[...]] * per_block, axis=1)
        pick = iota((2, count), 0) == 0
        where[...] = jnp.where(pick, row, at % LANES)
        terms[0:1, :] = line(prec[...])
        for c in range(CYCLES):
            terms[c + 1:c + 2, :] = line(value[c])
        group = iota((tiles, count), 1) % blocks
        total = jnp.zeros((tiles, count), F32)
        for k in range(near):
            total = total + jnp.where(column_of(pattern[k:k + 1, :]) == group, column_of(weight[k:k + 1, :]), 0.0)
        local[...] = total

    return kernel


def assess(prior, where, prec, value, local, parts, tiles, cells):
    blocks = cells // LANES
    rows = tiles * blocks
    count = where.shape[1]
    stacked = jnp.concatenate(
        [jnp.concatenate([x[:, k * LANES:(k + 1) * LANES] for k in range(blocks)], axis=0) for x in prior],
        axis=1,
    )
    choice = (iota((rows, count), 0) == where[0:1, :]).astype(F32).astype(BF16)
    lines = lax.dot_general(stacked, choice, (((0,), (0,)), ((), ())), preferred_element_type=F32)
    lane = iota((LANES, count), 0) == where[1:2, :]
    score = []
    for p in range(parts):
        predicted = jnp.sum(jnp.where(lane, lines[p * LANES:(p + 1) * LANES, :], 0.0), axis=0, keepdims=True)
        miss = value - predicted
        term = 0.5 * (prec * miss * miss)
        score.append(jnp.sum(local * term, axis=1, keepdims=True))
    least = score[0]
    for s in score[1:]:
        least = jnp.minimum(least, s)
    scale = [jnp.exp(least - s) for s in score]
    total = scale[0]
    for s in scale[1:]:
        total = total + s
    weighted = scale[0] * prior[0].astype(F32)
    for s, x in zip(scale[1:], prior[1:]):
        weighted = weighted + s * x.astype(F32)
    return least, total, weighted


def pieces(x):
    high = x.astype(BF16).astype(F32)
    middle = (x - high).astype(BF16).astype(F32)
    low = (x - high - middle).astype(BF16).astype(F32)
    return high, middle, low


def pack_mean(out, at, least, total, weighted):
    members, capacity, _ = out.shape
    tiles, cells = weighted.shape
    share = cells // members
    groups = tiles // capacity
    weighted = weighted.astype(BF16)
    for g in range(groups):
        rows = weighted[g * capacity:(g + 1) * capacity, :]
        for m in range(members):
            out[m, :, at + g * share:at + (g + 1) * share] = rows[:, m * share:(m + 1) * share]
    lane = iota((capacity, LANES), 1)
    misc = jnp.zeros((capacity, LANES), F32)
    spot = 0
    for x in (least, total):
        for piece in pieces(x):
            for g in range(groups):
                misc = jnp.where(lane == spot, piece[g * capacity:(g + 1) * capacity, :], misc)
                spot += 1
    out[:, :, at + groups * share:at + groups * share + LANES] = jnp.broadcast_to(misc.astype(BF16)[None], (members, capacity, LANES))


def unpack_mean(got, at, tiles, share):
    _, capacity, _ = got.shape
    groups = tiles // capacity
    misc = got[:, :, at + groups * share:at + groups * share + LANES].astype(F32)
    means = []
    for g in range(groups):
        pair = []
        for kind in range(2):
            spot = [(kind * 3 + piece) * groups + g for piece in range(3)]
            high, middle, low = [misc[:, :, i:i + 1] for i in spot]
            pair.append(high + middle + low)
        least, total = pair
        scale = jnp.exp(jnp.min(least, axis=0, keepdims=True) - least)
        part = got[:, :, at + g * share:at + (g + 1) * share].astype(F32)
        means.append(jnp.sum(scale * part, axis=0) / jnp.sum(scale * total, axis=0))
    return means


def make_first(parts, tiles, cells):
    def kernel(state, diff, pert, prior):
        nothing = jnp.zeros((1, LANES), F32)
        d = widen(diff[...], nothing, nothing)
        for p in range(parts):
            x = diffuse(widen(state[p].astype(F32), nothing, nothing), d)
            now = x[:, LANES:LANES + cells] + pert[0, p].astype(F32)
            prior[p * tiles:(p + 1) * tiles, :] = now.astype(BF16)

    return kernel


def make_send(capacity, cells):
    def kernel(prior, note, trail, send, message):
        members = note.shape[0]
        send_rows(note[...], prior[...], send, 0, capacity, cells)
        message[:members, :] = note[...]
        message[members:, :] = trail[...]

    return kernel


def make_assess(members, parts, tiles, cells):
    def kernel(prior, own, below, above, where, terms, local, part, low_out, high_out):
        low, high = edge_windows(own[...], below[...], above[...], members, parts)
        low_out[...] = low
        high_out[...] = high
        m = here()
        fixed = []
        for p in range(parts):
            mine = iota(low.shape, 0) == p * members + m
            start = jnp.sum(jnp.where(mine, low, 0.0), axis=0, keepdims=True)
            end = jnp.sum(jnp.where(mine, high, 0.0), axis=0, keepdims=True)
            x = patch(prior[p * tiles:(p + 1) * tiles, :].astype(F32), start[:, LANES:], end[:, :LANES])
            fixed.append(x.astype(BF16))
        pack_mean(
            part,
            0,
            *assess(fixed, where[...], terms[0:1, :], terms[1:2, :], local[...], parts, tiles, cells),
        )

    return kernel


def make_second(members, capacity, parts, tiles, cells):
    def kernel(got, keys, diff, pert, own, below, above, low, high, where, terms, local, part, send):
        arrived = got[...].reshape(members * capacity, cells)
        moved = pick_rows(keys[0], arrived)
        at = members + 2
        mine = own[at:at + 2 * parts, :].astype(I32)
        codes = jnp.concatenate([mine[parts:], below[at:at + parts, :].astype(I32)], axis=0)
        start = pick_rows(codes, low[...].astype(BF16))
        codes = jnp.concatenate([mine[:parts], above[at + parts:at + 2 * parts, :].astype(I32)], axis=0)
        end = pick_rows(codes, high[...].astype(BF16))
        d = widen(diff[...], below[members:members + 1, :], above[members + 1:members + 2, :])
        prior = []
        for p in range(parts):
            x = patch(moved[p * tiles:(p + 1) * tiles, :], start[p:p + 1, LANES:], end[p:p + 1, :LANES])
            q = parts + p
            x = widen(x, start[q:q + 1, :LANES], end[q:q + 1, LANES:])
            x = diffuse(x, d)[:, LANES:LANES + cells]
            prior.append((x + pert[0, p].astype(F32)).astype(BF16))
        send_rows(own[:members, :], jnp.concatenate(prior, axis=0), send, 1, capacity, cells)
        extra = part.shape[2]
        send[:, :, cells:cells + extra] = part[...]
        pack_mean(
            send,
            cells + extra,
            *assess(prior, where[...], terms[0:1, :], terms[2:3, :], local[...], parts, tiles, cells),
        )

    return kernel


def make_last(capacity, parts, tiles, cells):
    def kernel(got, keys, analysis, mean):
        slots = got.shape[0] * capacity
        rows = got[:, :, :cells].reshape(slots, cells)
        picked = pick_rows(keys[1], rows)
        for p in range(parts):
            analysis[p] = picked[p * tiles:(p + 1) * tiles, :].astype(BF16)
        share = mean.shape[2]
        extra = tiles // capacity * share + LANES
        for c in range(CYCLES):
            for g, x in enumerate(unpack_mean(got, cells + c * extra, tiles, share)):
                mean[c, g * capacity:(g + 1) * capacity, :] = x

    return kernel


def body(
    state,
    diffusivity,
    model_perturbation,
    obs_values,
    obs_prec,
    obs_tile,
    obs_cell,
    pattern,
    loc_weight,
    anc_member,
    anc_slot,
):
    parts, tiles, cells = state.shape
    members = lax.axis_size("member")
    regions = lax.axis_size("region")
    capacity = max(2, 2 * parts * tiles // members)
    share = cells // members
    groups = tiles // capacity
    blocks, per_block = obs_cell.shape
    count = blocks * per_block
    member_of = anc_member.reshape(CYCLES, parts, tiles)
    slot_of = anc_slot.reshape(CYCLES, parts, tiles)
    near = pattern.shape[1]
    ends = cells // LANES - 1

    def block(shape, at):
        lead = (0,) * (len(shape) - 1)
        return pl.BlockSpec(shape, lambda i: lead + (at,))

    edges = [state, state, diffusivity, diffusivity, model_perturbation, model_perturbation, member_of, slot_of]
    note, trail, keys = call(
        make_prepare(members, capacity, parts, tiles),
        [((members, LANES), F32), ((8, LANES), F32), ((CYCLES, parts * tiles, LANES), I32)],
        [pltpu.with_memory_space_constraint(x, pltpu.HBM) for x in edges],
        [
            block((parts, tiles, LANES), 0),
            block((parts, tiles, LANES), ends),
            block((tiles, LANES), 0),
            block((tiles, LANES), ends),
            block((1, parts, tiles, LANES), 0),
            block((1, parts, tiles, LANES), ends),
            whole_spec(member_of.shape),
            whole_spec(slot_of.shape),
        ],
        name="prepare",
    )
    note = lax.all_to_all(note, "member", split_axis=0, concat_axis=0, tiled=True)

    where, terms, local = call(
        make_observe(blocks, per_block, tiles, near),
        [((2, count), I32), ((1 + CYCLES, count), F32), ((tiles, count), F32)],
        [obs_tile[None, :], obs_cell.T, obs_prec.T, jnp.swapaxes(obs_values, 1, 2), pattern.T, loc_weight.T],
        name="observe",
    )

    def noise_spec(c):
        return pl.BlockSpec((1, parts, tiles, cells), lambda i: (c, 0, 0, 0))

    args = [state, diffusivity, model_perturbation]
    specs = [whole_spec(a.shape) for a in args]
    specs[2] = noise_spec(0)
    (prior,) = call(
        make_first(parts, tiles, cells), [((parts * tiles, cells), BF16)], args, specs, name="forecast_first"
    )
    send, message = call(
        make_send(capacity, cells),
        [((members, capacity, cells), BF16), ((members + trail.shape[0], LANES), F32)],
        [prior, note, trail],
        name="send_first",
    )
    got = lax.all_to_all(send, "member", split_axis=0, concat_axis=0, tiled=True)
    forward = [(i, i + 1) for i in range(regions - 1)]
    below = lax.ppermute(message, "region", forward)
    above = lax.ppermute(message, "region", [(j, i) for i, j in forward])
    extra = groups * share + LANES
    window = ((parts * members, 2 * LANES), F32)
    part, low, high = call(
        make_assess(members, parts, tiles, cells),
        [((members, capacity, extra), BF16), window, window],
        [prior, message, below, above, where, terms, local],
        name="assess_first",
    )
    args = [got, keys, diffusivity, model_perturbation, message, below, above, low, high, where, terms, local, part]
    specs = [whole_spec(a.shape) for a in args]
    specs[3] = noise_spec(1)
    (send,) = call(
        make_second(members, capacity, parts, tiles, cells),
        [((members, capacity, cells + CYCLES * extra), BF16)],
        args,
        specs,
        name="forecast_second",
    )
    got = lax.all_to_all(send, "member", split_axis=0, concat_axis=0, tiled=True)
    return tuple(
        call(
            make_last(capacity, parts, tiles, cells),
            [(state.shape, BF16), ((CYCLES, tiles, share), F32)],
            [got, keys],
            name="finish",
        )
    )


def solution(mesh):
    in_specs = (
        P("member", "region", None),
        P("region", None),
        P(None, "member", "region", None),
        P(None, "region", None),
        P("region", None),
        P("region"),
        P("region", None),
        P("region", None),
        P("region", None),
        P(None, "region", "member", None, None),
        P(None, "region", "member", None),
    )
    out_specs = (P("member", "region", None), P(None, "region", "member"))
    return jax.shard_map(body, mesh=mesh, in_specs=in_specs, out_specs=out_specs, check_vma=False)
```

```python
import jax
import jax.numpy as jnp
from jax import lax
from jax.experimental import pallas as pl
from jax.experimental.pallas import tpu as pltpu
from jax.sharding import PartitionSpec as P

CYCLES = 2
STEPS = 2
LANES = 128
F32 = jnp.float32
BF16 = jnp.bfloat16
I32 = jnp.int32
PARAMS = pltpu.CompilerParams(vmem_limit_bytes=48 * 1024 * 1024)


def iota(shape, dim):
    return lax.broadcasted_iota(I32, shape, dim)


def whole_spec(shape):
    zeros = (0,) * len(shape)
    return pl.BlockSpec(shape, lambda i: zeros)


def call(kernel, outs, args, specs=None, scratch=(), name=None):
    specs = specs or [whole_spec(a.shape) for a in args]
    return pl.pallas_call(
        kernel,
        out_shape=[jax.ShapeDtypeStruct(s, d) for s, d in outs],
        grid=(1,),
        in_specs=specs,
        out_specs=[whole_spec(s) for s, _ in outs],
        scratch_shapes=[pltpu.VMEM(s, d) for s, d in scratch],
        compiler_params=PARAMS,
        name=name,
    )(*args)


def column_of(row):
    n = row.shape[1]
    square = jnp.broadcast_to(row, (n, n))
    return jnp.sum(jnp.where(iota((n, n), 0) == iota((n, n), 1), square, 0), axis=1, keepdims=True)


def here():
    return lax.axis_index("member")


EDGE_AT = 32
STRIDE = 8


def padded(pairs):
    return max(8, pairs)


def make_prepare(members, capacity, parts, tiles):
    width = 2 * STEPS
    pairs = members // 2
    rows = parts * tiles

    def kernel(st0, st1, df0, df1, pb0, pb1, am, slot, *outs):
        notes, trail, keys = outs[:pairs], outs[pairs], outs[pairs + 1]
        m = here()
        lane = iota((1, LANES), 1)
        last = tiles - 1
        trail[...] = jnp.zeros(trail.shape, F32)
        trail[0:1, :] = df1[last:last + 1, :]
        trail[1:2, :] = df0[0:1, :]
        edge = jnp.zeros((1, LANES), F32)
        for p in range(parts):
            for i, t in enumerate((last, 0)):
                source = am[0, p:p + 1, t:t + 1] ^ m
                code = (slot[0, p:p + 1, t:t + 1] * 2 + source % 2) * padded(pairs) + source // 2
                row = 2 + i * parts + p
                trail[row:row + 1, :] = jnp.broadcast_to(code.astype(F32), (1, LANES))
            fields = (st1[p, last:last + 1, :], st0[p, 0:1, :], pb1[0, p, last:last + 1, :], pb0[0, p, 0:1, :])
            for i, x in enumerate(fields):
                to = EDGE_AT + STRIDE * (4 * p + i)
                start = 0 if i % 2 else LANES - width
                moved = pltpu.roll(x.astype(F32), (to - start) % LANES, 1)
                edge = jnp.where((lane >= to) & (lane < to + width), moved, edge)
        before = (iota((tiles, tiles), 0) < iota((tiles, tiles), 1)).astype(F32)
        asked = jnp.zeros((pairs, LANES), F32)
        for c in range(CYCLES):
            seen = jnp.zeros((members, 1), F32)
            for p in range(parts):
                source = am[c, p:p + 1, :] ^ m
                named = (iota((members, tiles), 0) == source).astype(F32)
                earlier = seen + jnp.dot(named, before, preferred_element_type=F32)
                rank = jnp.sum(named * earlier, axis=0, keepdims=True).astype(I32)
                seen = seen + jnp.sum(named, axis=1, keepdims=True)
                half = source % 2
                code = half * rows + slot[c, p:p + 1, :] * tiles + iota((1, tiles), 1)
                spot = (iota((LANES, tiles), 0) == (2 * c + half) * capacity + rank).astype(F32)
                pair = jnp.where(iota((pairs, tiles), 0) == source // 2, (code + 1).astype(F32), 0.0)
                asked = asked + lax.dot_general(pair, spot, (((1,), (1,)), ((), ())), preferred_element_type=F32)
                column = column_of(source * capacity + rank)
                keys[c, p * tiles:(p + 1) * tiles, :] = jnp.broadcast_to(column, (tiles, LANES))
        for k in range(pairs):
            notes[k][...] = jnp.where(lane < EDGE_AT, asked[k:k + 1, :] - 1.0, edge)

    return kernel


def edge_windows(own, below, above, size, parts):
    width = 2 * STEPS

    def field(note, p, i):
        at = EDGE_AT + STRIDE * (4 * p + i)
        start = 0 if i % 2 else LANES - width
        both = jnp.concatenate([note[:size, :], note[size + 8:, :]], axis=0)
        return pltpu.roll(both, (start - at) % LANES, 1)

    low, high = [], []
    for out, before, after in ((low, below, own), (high, own, above)):
        d = jnp.concatenate([before[size:size + 1, :], after[size + 1:size + 2, :]], axis=1)
        for p in range(parts):
            x = jnp.concatenate([field(before, p, 0), field(after, p, 1)], axis=1)
            x = diffuse(x, d) + jnp.concatenate([field(before, p, 2), field(after, p, 3)], axis=1)
            out.append(x.astype(BF16).astype(F32))
    return jnp.concatenate(low, axis=0), jnp.concatenate(high, axis=0)


def patch(x, first, last):
    tiles = x.shape[0]
    row, lane = iota((tiles, LANES), 0), iota((tiles, LANES), 1)
    head = jnp.where((row == 0) & (lane < STEPS), first, x[:, :LANES])
    tail = jnp.where((row == tiles - 1) & (lane >= LANES - STEPS), last, x[:, -LANES:])
    return jnp.concatenate([head, x[:, LANES:-LANES], tail], axis=1)


def widen(x, left, right):
    tiles = x.shape[0]
    row = iota((tiles, LANES), 0)
    before = jnp.where(row == 0, left, pltpu.roll(x[:, -LANES:], 1, 0))
    after = jnp.where(row == tiles - 1, right, pltpu.roll(x[:, :LANES], tiles - 1, 0))
    return jnp.concatenate([before, x, after], axis=1)


def diffuse(x, d):
    n = x.shape[1]
    for _ in range(STEPS):
        x = x + d * (pltpu.roll(x, 1, 1) - 2.0 * x + pltpu.roll(x, n - 1, 1))
    return x


def pick_rows(wanted, rows):
    m = rows.shape[0]
    n = wanted.shape[0]
    choice = (wanted[:, :m] == iota((n, m), 1)).astype(F32).astype(BF16)
    return jnp.dot(choice, rows, preferred_element_type=F32)


def requested(notes, prior, cycle, rows):
    pairs = len(notes)
    total = pairs * rows
    asked = jnp.concatenate(notes, axis=0)
    spread = jnp.broadcast_to(asked[:, None, :], (pairs, rows, LANES)).reshape(total, LANES)
    mine = iota((total, LANES), 1) == cycle * rows + iota((total, LANES), 0) % rows
    wanted = jnp.sum(jnp.where(mine, spread, 0.0), axis=1, keepdims=True).astype(I32)
    return pick_rows(jnp.broadcast_to(wanted, (total, LANES)), prior)


def make_observe(blocks, per_block, tiles, near):
    count = blocks * per_block

    def kernel(tile, cell, prec, value, pattern, weight, where, terms, local):
        def line(x):
            wide = jnp.concatenate([x] * per_block, axis=1)
            own = iota((per_block, count), 1) // blocks == iota((per_block, count), 0)
            return jnp.sum(jnp.where(own, wide, 0), axis=0, keepdims=True)

        at = line(cell[...])
        row = (at // LANES) * tiles + jnp.concatenate([tile[...]] * per_block, axis=1)
        pick = iota((2, count), 0) == 0
        where[...] = jnp.where(pick, row, at % LANES)
        terms[0:1, :] = line(prec[...])
        for c in range(CYCLES):
            terms[c + 1:c + 2, :] = line(value[c])
        group = iota((tiles, count), 1) % blocks
        total = jnp.zeros((tiles, count), F32)
        for k in range(near):
            total = total + jnp.where(column_of(pattern[k:k + 1, :]) == group, column_of(weight[k:k + 1, :]), 0.0)
        local[...] = total

    return kernel


def assess(prior, where, prec, value, local, parts, tiles, cells):
    blocks = cells // LANES
    rows = tiles * blocks
    count = where.shape[1]
    stacked = jnp.concatenate(
        [jnp.concatenate([x[:, k * LANES:(k + 1) * LANES] for k in range(blocks)], axis=0) for x in prior],
        axis=1,
    )
    choice = (iota((rows, count), 0) == where[0:1, :]).astype(F32).astype(BF16)
    lines = lax.dot_general(stacked, choice, (((0,), (0,)), ((), ())), preferred_element_type=F32)
    lane = iota((LANES, count), 0) == where[1:2, :]
    score = []
    for p in range(parts):
        predicted = jnp.sum(jnp.where(lane, lines[p * LANES:(p + 1) * LANES, :], 0.0), axis=0, keepdims=True)
        miss = value - predicted
        term = 0.5 * (prec * miss * miss)
        score.append(jnp.sum(local * term, axis=1, keepdims=True))
    least = score[0]
    for s in score[1:]:
        least = jnp.minimum(least, s)
    scale = [jnp.exp(least - s) for s in score]
    total = scale[0]
    for s in scale[1:]:
        total = total + s
    weighted = scale[0] * prior[0].astype(F32)
    for s, x in zip(scale[1:], prior[1:]):
        weighted = weighted + s * x.astype(F32)
    return least, total, weighted


def pieces(x):
    high = x.astype(BF16).astype(F32)
    middle = (x - high).astype(BF16).astype(F32)
    low = (x - high - middle).astype(BF16).astype(F32)
    return high, middle, low


def share_of(ref, member, share):
    if share % LANES == 0:
        return ref[:, pl.ds(pl.multiple_of(member * share, LANES), share)]
    return pltpu.roll(ref[...], ref.shape[1] - member * share, 1)[:, :share]


def pack_mean(outs, at, least, total, sums, share):
    rows = outs[0].shape[0]
    tiles = sums.shape[0]
    groups = tiles // rows
    m = here()
    lane = iota((rows, LANES), 1)
    misc = jnp.zeros((rows, LANES), F32)
    spot = 0
    for x in (least, total):
        for piece in pieces(x):
            for g in range(groups):
                misc = jnp.where(lane == spot, piece[g * rows:(g + 1) * rows, :], misc)
                spot += 1
    end = at + groups * share
    for k, out in enumerate(outs):
        block = share_of(sums, m ^ (2 * k), share)
        for g in range(groups):
            out[:, at + g * share:at + (g + 1) * share] = block[g * rows:(g + 1) * rows, :].astype(BF16)
        out[:, end:end + LANES] = misc.astype(BF16)


def unpack_mean(got, at, tiles, share):
    rows = got[0].shape[0]
    groups = tiles // rows
    end = at + groups * share
    misc = [x[:, end:end + LANES].astype(F32) for x in got]
    means = []
    for g in range(groups):
        stats = []
        for x in misc:
            pair = []
            for kind in range(2):
                spot = [(kind * 3 + piece) * groups + g for piece in range(3)]
                high, middle, low = [x[:, i:i + 1] for i in spot]
                pair.append(high + middle + low)
            stats.append(pair)
        lowest = stats[0][0]
        for least, _ in stats[1:]:
            lowest = jnp.minimum(lowest, least)
        top, bottom = 0.0, 0.0
        for x, (least, total) in zip(got, stats):
            scale = jnp.exp(lowest - least)
            top = top + scale * x[:, at + g * share:at + (g + 1) * share].astype(F32)
            bottom = bottom + scale * total
        means.append(top / bottom)
    return means


def make_first(parts, tiles, cells):
    def kernel(state, diff, pert, after, prior):
        nothing = jnp.zeros((1, LANES), F32)
        d = widen(diff[...], nothing, nothing)
        for p in range(parts):
            x = diffuse(widen(state[p].astype(F32), nothing, nothing), d)
            now = x[:, LANES:LANES + cells] + pert[0, p].astype(F32)
            prior[p * tiles:(p + 1) * tiles, :] = now.astype(BF16)

    return kernel


def make_send(pairs, rows):
    def kernel(own, other, trail, *refs):
        notes, sends, half = refs[:pairs], refs[pairs:2 * pairs], refs[2 * pairs]
        prior = jnp.concatenate([own[...], other[...]], axis=0)
        sent = requested([x[...] for x in notes], prior, 0, rows)
        for k in range(pairs):
            sends[k][...] = sent[k * rows:(k + 1) * rows, :].astype(BF16)
        size = padded(pairs)
        half[...] = jnp.zeros(half.shape, F32)
        for k in range(pairs):
            half[k:k + 1, :] = notes[k][...]
        half[size:, :] = trail[...]

    return kernel


def make_assess(pairs, parts, tiles, cells, share):
    size = padded(pairs)

    def kernel(own, other, message, below, above, where, terms, local, *refs):
        outs, low_out, high_out, sums = refs[:pairs], refs[pairs], refs[pairs + 1], refs[pairs + 2]
        low, high = edge_windows(message[...], below[...], above[...], size, parts)
        low_out[...] = low.astype(BF16)
        high_out[...] = high.astype(BF16)
        fixed = []
        for h, prior in enumerate((own, other)):
            for p in range(parts):
                row = (2 * p + h) * size
                x = prior[p * tiles:(p + 1) * tiles, :].astype(F32)
                x = patch(x, low[row:row + 1, LANES:], high[row:row + 1, :LANES])
                fixed.append(x.astype(BF16))
        least, total, weighted = assess(
            fixed, where[...], terms[0:1, :], terms[1:2, :], local[...], 2 * parts, tiles, cells
        )
        sums[...] = weighted
        pack_mean(outs, 0, least, total, sums, share)

    return kernel


def make_second(pairs, parts, tiles, cells):
    size = padded(pairs)

    def kernel(keys, diff, pert, message, below, above, low, high, *refs):
        got, prior = refs[:pairs], refs[pairs]
        arrived = jnp.concatenate([x[...] for x in got], axis=0)
        moved = pick_rows(keys[0], arrived)
        at = size + 2
        mine = message[at:at + 2 * parts, :].astype(I32)
        codes = jnp.concatenate([mine[parts:], below[at:at + parts, :].astype(I32)], axis=0)
        start = pick_rows(codes, low[...])
        codes = jnp.concatenate([mine[:parts], above[at + parts:at + 2 * parts, :].astype(I32)], axis=0)
        end = pick_rows(codes, high[...])
        d = widen(diff[...], below[size:size + 1, :], above[size + 1:size + 2, :])
        for p in range(parts):
            x = patch(moved[p * tiles:(p + 1) * tiles, :], start[p:p + 1, LANES:], end[p:p + 1, :LANES])
            q = parts + p
            x = widen(x, start[q:q + 1, :LANES], end[q:q + 1, LANES:])
            x = diffuse(x, d)[:, LANES:LANES + cells]
            prior[p * tiles:(p + 1) * tiles, :] = (x + pert[0, p].astype(F32)).astype(BF16)

    return kernel


def make_send_second(pairs, rows, parts, tiles, cells, share):
    def kernel(own, other, where, terms, local, *refs):
        notes, kept, outs, sums = refs[:pairs], refs[pairs:2 * pairs], refs[2 * pairs:3 * pairs], refs[3 * pairs]
        prior = jnp.concatenate([own[...], other[...]], axis=0)
        sent = requested([x[...] for x in notes], prior, 1, rows)
        extra = kept[0].shape[1]
        for k in range(pairs):
            outs[k][:, :cells] = sent[k * rows:(k + 1) * rows, :].astype(BF16)
            outs[k][:, cells:cells + extra] = kept[k][...]
        least, total, weighted = assess(
            [x[p * tiles:(p + 1) * tiles, :] for x in (own, other) for p in range(parts)],
            where[...], terms[0:1, :], terms[2:3, :], local[...], 2 * parts, tiles, cells,
        )
        sums[...] = weighted
        pack_mean(outs, cells + extra, least, total, sums, share)

    return kernel


def make_last(pairs, rows, parts, tiles, cells):
    def kernel(keys, *refs):
        got, analysis, mean = refs[:pairs], refs[pairs], refs[pairs + 1]
        arrived = jnp.concatenate([x[:, :cells] for x in got], axis=0)
        picked = pick_rows(keys[1], arrived)
        for p in range(parts):
            analysis[p] = picked[p * tiles:(p + 1) * tiles, :].astype(BF16)
        share = mean.shape[2]
        extra = tiles // rows * share + LANES
        for c in range(CYCLES):
            for g, x in enumerate(unpack_mean(got, cells + c * extra, tiles, share)):
                mean[c, g * rows:(g + 1) * rows, :] = x

    return kernel


def body(
    state,
    diffusivity,
    model_perturbation,
    obs_values,
    obs_prec,
    obs_tile,
    obs_cell,
    pattern,
    loc_weight,
    anc_member,
    anc_slot,
):
    parts, tiles, cells = state.shape
    members = lax.axis_size("member")
    regions = lax.axis_size("region")
    capacity = max(2, 2 * parts * tiles // members)
    share = cells // members
    pairs = members // 2
    rows = 2 * capacity
    extra = tiles // rows * share + LANES
    blocks, per_block = obs_cell.shape
    count = blocks * per_block
    member_of = anc_member.reshape(CYCLES, parts, tiles)
    slot_of = anc_slot.reshape(CYCLES, parts, tiles)
    near = pattern.shape[1]
    ends = cells // LANES - 1

    def block(shape, at):
        lead = (0,) * (len(shape) - 1)
        return pl.BlockSpec(shape, lambda i: lead + (at,))

    edges = [state, state, diffusivity, diffusivity, model_perturbation, model_perturbation, member_of, slot_of]
    *notes, trail, keys = call(
        make_prepare(members, capacity, parts, tiles),
        [((1, LANES), F32)] * pairs + [((8, LANES), F32), ((CYCLES, parts * tiles, LANES), I32)],
        [pltpu.with_memory_space_constraint(x, pltpu.HBM) for x in edges],
        [
            block((parts, tiles, LANES), 0),
            block((parts, tiles, LANES), ends),
            block((tiles, LANES), 0),
            block((tiles, LANES), ends),
            block((1, parts, tiles, LANES), 0),
            block((1, parts, tiles, LANES), ends),
            whole_spec(member_of.shape),
            whole_spec(slot_of.shape),
        ],
        name="prepare",
    )

    def trade(x, k):
        return lax.ppermute(x, "member", [(i, i ^ k) for i in range(members)])

    notes = notes[:1] + [trade(notes[k], 2 * k) for k in range(1, pairs)]

    where, terms, local = call(
        make_observe(blocks, per_block, tiles, near),
        [((2, count), I32), ((1 + CYCLES, count), F32), ((tiles, count), F32)],
        [obs_tile[None, :], obs_cell.T, obs_prec.T, jnp.swapaxes(obs_values, 1, 2), pattern.T, loc_weight.T],
        name="observe",
    )

    def noise_spec(c):
        return pl.BlockSpec((1, parts, tiles, cells), lambda i: (c, 0, 0, 0))

    args = [state, diffusivity, model_perturbation, trail]
    specs = [whole_spec(a.shape) for a in args]
    specs[2] = noise_spec(0)
    (prior,) = call(
        make_first(parts, tiles, cells), [((parts * tiles, cells), BF16)], args, specs, name="forecast_first"
    )
    other = trade(prior, 1)
    size = padded(pairs)
    *sends, half = call(
        make_send(pairs, rows),
        [((rows, cells), BF16)] * pairs + [((size + trail.shape[0], LANES), F32)],
        [prior, other, trail, *notes],
        name="send_first",
    )
    got = [sends[0]] + [trade(sends[k], 2 * k) for k in range(1, pairs)]
    message = jnp.concatenate([half, trade(half, 1)[:size]], axis=0)
    forward = [(i, i + 1) for i in range(regions - 1)]
    below = lax.ppermute(message, "region", forward)
    above = lax.ppermute(message, "region", [(j, i) for i, j in forward])
    window = ((parts * 2 * size, 2 * LANES), BF16)
    sums = [((tiles, cells), F32)]
    *kept, low, high = call(
        make_assess(pairs, parts, tiles, cells, share),
        [((rows, extra), BF16)] * pairs + [window, window],
        [prior, other, message, below, above, where, terms, local],
        scratch=sums,
        name="assess_first",
    )
    args = [keys, diffusivity, model_perturbation, message, below, above, low, high, *got]
    specs = [whole_spec(a.shape) for a in args]
    specs[2] = noise_spec(1)
    (prior,) = call(
        make_second(pairs, parts, tiles, cells),
        [((parts * tiles, cells), BF16)],
        args,
        specs,
        name="forecast_second",
    )
    sends = call(
        make_send_second(pairs, rows, parts, tiles, cells, share),
        [((rows, cells + CYCLES * extra), BF16)] * pairs,
        [prior, trade(prior, 1), where, terms, local, *notes, *kept],
        scratch=sums,
        name="send_second",
    )
    got = [sends[0]] + [trade(sends[k], 2 * k) for k in range(1, pairs)]
    return tuple(
        call(
            make_last(pairs, rows, parts, tiles, cells),
            [(state.shape, BF16), ((CYCLES, tiles, share), F32)],
            [keys, *got],
            name="finish",
        )
    )


def solution(mesh):
    in_specs = (
        P("member", "region", None),
        P("region", None),
        P(None, "member", "region", None),
        P(None, "region", None),
        P("region", None),
        P("region"),
        P("region", None),
        P("region", None),
        P("region", None),
        P(None, "region", "member", None, None),
        P(None, "region", "member", None),
    )
    out_specs = (P("member", "region", None), P(None, "region", "member"))
    return jax.shard_map(body, mesh=mesh, in_specs=in_specs, out_specs=out_specs, check_vma=False)
```

```python
import jax
import jax.numpy as jnp
from jax import lax
from jax.experimental import pallas as pl
from jax.experimental.pallas import tpu as pltpu
from jax.sharding import PartitionSpec as P

CYCLES = 2
STEPS = 2
LANES = 128
F32 = jnp.float32
BF16 = jnp.bfloat16
I32 = jnp.int32
PARAMS = pltpu.CompilerParams(vmem_limit_bytes=48 * 1024 * 1024)


def iota(shape, dim):
    return lax.broadcasted_iota(I32, shape, dim)


def whole_spec(shape):
    zeros = (0,) * len(shape)
    return pl.BlockSpec(shape, lambda i: zeros)


def call(kernel, outs, args, specs=None, scratch=(), name=None):
    specs = specs or [whole_spec(a.shape) for a in args]
    return pl.pallas_call(
        kernel,
        out_shape=[jax.ShapeDtypeStruct(s, d) for s, d in outs],
        grid=(1,),
        in_specs=specs,
        out_specs=[whole_spec(s) for s, _ in outs],
        scratch_shapes=[pltpu.VMEM(s, d) for s, d in scratch],
        compiler_params=PARAMS,
        name=name,
    )(*args)


def column_of(row):
    n = row.shape[1]
    square = jnp.broadcast_to(row, (n, n))
    return jnp.sum(jnp.where(iota((n, n), 0) == iota((n, n), 1), square, 0), axis=1, keepdims=True)


def here():
    return lax.axis_index("member")


EDGE_AT = 32
STRIDE = 8


def padded(pairs):
    return max(8, pairs)


def make_prepare(members, capacity, parts, tiles):
    width = 2 * STEPS
    pairs = members // 2
    rows = parts * tiles

    def kernel(st0, st1, df0, df1, pb0, pb1, am, slot, *outs):
        notes, trail, keys = outs[:pairs], outs[pairs], outs[pairs + 1]
        m = here()
        lane = iota((1, LANES), 1)
        last = tiles - 1
        trail[...] = jnp.zeros(trail.shape, F32)
        trail[0:1, :] = df1[last:last + 1, :]
        trail[1:2, :] = df0[0:1, :]
        edge = jnp.zeros((1, LANES), F32)
        for p in range(parts):
            for i, t in enumerate((last, 0)):
                source = am[0, p:p + 1, t:t + 1] ^ m
                code = (slot[0, p:p + 1, t:t + 1] * 2 + source % 2) * padded(pairs) + source // 2
                row = 2 + i * parts + p
                trail[row:row + 1, :] = jnp.broadcast_to(code.astype(F32), (1, LANES))
            fields = (st1[p, last:last + 1, :], st0[p, 0:1, :], pb1[0, p, last:last + 1, :], pb0[0, p, 0:1, :])
            for i, x in enumerate(fields):
                to = EDGE_AT + STRIDE * (4 * p + i)
                start = 0 if i % 2 else LANES - width
                moved = pltpu.roll(x.astype(F32), (to - start) % LANES, 1)
                edge = jnp.where((lane >= to) & (lane < to + width), moved, edge)
        before = (iota((tiles, tiles), 0) < iota((tiles, tiles), 1)).astype(F32)
        asked = jnp.zeros((pairs, LANES), F32)
        for c in range(CYCLES):
            seen = jnp.zeros((members, 1), F32)
            for p in range(parts):
                source = am[c, p:p + 1, :] ^ m
                named = (iota((members, tiles), 0) == source).astype(F32)
                earlier = seen + jnp.dot(named, before, preferred_element_type=F32)
                rank = jnp.sum(named * earlier, axis=0, keepdims=True).astype(I32)
                seen = seen + jnp.sum(named, axis=1, keepdims=True)
                half = source % 2
                code = half * rows + slot[c, p:p + 1, :] * tiles + iota((1, tiles), 1)
                spot = (iota((LANES, tiles), 0) == (2 * c + half) * capacity + rank).astype(F32)
                pair = jnp.where(iota((pairs, tiles), 0) == source // 2, (code + 1).astype(F32), 0.0)
                asked = asked + lax.dot_general(pair, spot, (((1,), (1,)), ((), ())), preferred_element_type=F32)
                column = column_of(source * capacity + rank)
                keys[c, p * tiles:(p + 1) * tiles, :] = jnp.broadcast_to(column, (tiles, LANES))
        for k in range(pairs):
            notes[k][...] = jnp.where(lane < EDGE_AT, asked[k:k + 1, :] - 1.0, edge)

    return kernel


def halves(mine, theirs):
    half = theirs.shape[0] // 2
    theirs = jnp.concatenate([theirs[half:, :], theirs[:half, :]], axis=0)
    first = jnp.broadcast_to(here() % 2, mine.shape) == 0
    return jnp.where(first, mine, theirs), jnp.where(first, theirs, mine)


def edge_windows(own, below, above, size, parts):
    width = 2 * STEPS

    def field(note, p, i):
        at = EDGE_AT + STRIDE * (4 * p + i)
        start = 0 if i % 2 else LANES - width
        both = jnp.concatenate([note[:size, :], note[size + 8:2 * size + 8, :]], axis=0)
        return pltpu.roll(both, (start - at) % LANES, 1)

    low, high = [], []
    for out, before, after in ((low, below, own), (high, own, above)):
        d = jnp.concatenate([before[size:size + 1, :], after[size + 1:size + 2, :]], axis=1)
        for p in range(parts):
            x = jnp.concatenate([field(before, p, 0), field(after, p, 1)], axis=1)
            x = diffuse(x, d) + jnp.concatenate([field(before, p, 2), field(after, p, 3)], axis=1)
            out.append(x.astype(BF16).astype(F32))
    return jnp.concatenate(low, axis=0), jnp.concatenate(high, axis=0)


def patch(x, first, last):
    tiles = x.shape[0]
    row, lane = iota((tiles, LANES), 0), iota((tiles, LANES), 1)
    head = jnp.where((row == 0) & (lane < STEPS), first, x[:, :LANES])
    tail = jnp.where((row == tiles - 1) & (lane >= LANES - STEPS), last, x[:, -LANES:])
    return jnp.concatenate([head, x[:, LANES:-LANES], tail], axis=1)


def widen(x, left, right):
    tiles = x.shape[0]
    row = iota((tiles, LANES), 0)
    before = jnp.where(row == 0, left, pltpu.roll(x[:, -LANES:], 1, 0))
    after = jnp.where(row == tiles - 1, right, pltpu.roll(x[:, :LANES], tiles - 1, 0))
    return jnp.concatenate([before, x, after], axis=1)


def diffuse(x, d):
    n = x.shape[1]
    for _ in range(STEPS):
        x = x + d * (pltpu.roll(x, 1, 1) - 2.0 * x + pltpu.roll(x, n - 1, 1))
    return x


def pick_rows(wanted, rows):
    m = rows.shape[0]
    n = wanted.shape[0]
    choice = (wanted[:, :m] == iota((n, m), 1)).astype(F32).astype(BF16)
    return jnp.dot(choice, rows, preferred_element_type=F32)


def requested(notes, prior, cycle, rows):
    pairs = len(notes)
    total = pairs * rows
    asked = jnp.concatenate(notes, axis=0)
    spread = jnp.broadcast_to(asked[:, None, :], (pairs, rows, LANES)).reshape(total, LANES)
    mine = iota((total, LANES), 1) == cycle * rows + iota((total, LANES), 0) % rows
    wanted = jnp.sum(jnp.where(mine, spread, 0.0), axis=1, keepdims=True).astype(I32)
    return pick_rows(jnp.broadcast_to(wanted, (total, LANES)), prior)


def make_observe(blocks, per_block, tiles, near):
    count = blocks * per_block

    def kernel(tile, cell, prec, value, pattern, weight, where, terms, local):
        def line(x):
            wide = jnp.concatenate([x] * per_block, axis=1)
            own = iota((per_block, count), 1) // blocks == iota((per_block, count), 0)
            return jnp.sum(jnp.where(own, wide, 0), axis=0, keepdims=True)

        at = line(cell[...])
        row = (at // LANES) * tiles + jnp.concatenate([tile[...]] * per_block, axis=1)
        pick = iota((2, count), 0) == 0
        where[...] = jnp.where(pick, row, at % LANES)
        terms[0:1, :] = line(prec[...])
        for c in range(CYCLES):
            terms[c + 1:c + 2, :] = line(value[c])
        group = iota((tiles, count), 1) % blocks
        total = jnp.zeros((tiles, count), F32)
        for k in range(near):
            total = total + jnp.where(column_of(pattern[k:k + 1, :]) == group, column_of(weight[k:k + 1, :]), 0.0)
        local[...] = total

    return kernel


def assess(prior, where, prec, value, local, parts, tiles, cells):
    blocks = cells // LANES
    rows = tiles * blocks
    count = where.shape[1]
    stacked = jnp.concatenate(
        [jnp.concatenate([x[:, k * LANES:(k + 1) * LANES] for k in range(blocks)], axis=0) for x in prior],
        axis=1,
    )
    choice = (iota((rows, count), 0) == where[0:1, :]).astype(F32).astype(BF16)
    lines = lax.dot_general(stacked, choice, (((0,), (0,)), ((), ())), preferred_element_type=F32)
    lane = iota((LANES, count), 0) == where[1:2, :]
    score = []
    for p in range(parts):
        predicted = jnp.sum(jnp.where(lane, lines[p * LANES:(p + 1) * LANES, :], 0.0), axis=0, keepdims=True)
        miss = value - predicted
        term = 0.5 * (prec * miss * miss)
        score.append(jnp.sum(local * term, axis=1, keepdims=True))
    least = score[0]
    for s in score[1:]:
        least = jnp.minimum(least, s)
    scale = [jnp.exp(least - s) for s in score]
    total = scale[0]
    for s in scale[1:]:
        total = total + s
    weighted = scale[0] * prior[0].astype(F32)
    for s, x in zip(scale[1:], prior[1:]):
        weighted = weighted + s * x.astype(F32)
    return least, total, weighted


def pieces(x):
    high = x.astype(BF16).astype(F32)
    middle = (x - high).astype(BF16).astype(F32)
    low = (x - high - middle).astype(BF16).astype(F32)
    return high, middle, low


def share_of(ref, member, share):
    if share % LANES == 0:
        return ref[:, pl.ds(pl.multiple_of(member * share, LANES), share)]
    return pltpu.roll(ref[...], ref.shape[1] - member * share, 1)[:, :share]


def pack_mean(outs, at, least, total, sums, share):
    rows = outs[0].shape[0]
    tiles = sums.shape[0]
    groups = tiles // rows
    m = here()
    lane = iota((rows, LANES), 1)
    misc = jnp.zeros((rows, LANES), F32)
    spot = 0
    for x in (least, total):
        for piece in pieces(x):
            for g in range(groups):
                misc = jnp.where(lane == spot, piece[g * rows:(g + 1) * rows, :], misc)
                spot += 1
    end = at + groups * share
    for k, out in enumerate(outs):
        block = share_of(sums, m ^ (2 * k), share)
        for g in range(groups):
            out[:, at + g * share:at + (g + 1) * share] = block[g * rows:(g + 1) * rows, :].astype(BF16)
        out[:, end:end + LANES] = misc.astype(BF16)


def unpack_mean(got, at, tiles, share):
    rows = got[0].shape[0]
    groups = tiles // rows
    end = at + groups * share
    misc = [x[:, end:end + LANES].astype(F32) for x in got]
    means = []
    for g in range(groups):
        stats = []
        for x in misc:
            pair = []
            for kind in range(2):
                spot = [(kind * 3 + piece) * groups + g for piece in range(3)]
                high, middle, low = [x[:, i:i + 1] for i in spot]
                pair.append(high + middle + low)
            stats.append(pair)
        lowest = stats[0][0]
        for least, _ in stats[1:]:
            lowest = jnp.minimum(lowest, least)
        top, bottom = 0.0, 0.0
        for x, (least, total) in zip(got, stats):
            scale = jnp.exp(lowest - least)
            top = top + scale * x[:, at + g * share:at + (g + 1) * share].astype(F32)
            bottom = bottom + scale * total
        means.append(top / bottom)
    return means


def make_first(parts, tiles, cells):
    def kernel(state, diff, pert, after, prior):
        nothing = jnp.zeros((1, LANES), F32)
        d = widen(diff[...], nothing, nothing)
        for p in range(parts):
            x = diffuse(widen(state[p].astype(F32), nothing, nothing), d)
            now = x[:, LANES:LANES + cells] + pert[0, p].astype(F32)
            prior[p * tiles:(p + 1) * tiles, :] = now.astype(BF16)

    return kernel


def make_send(pairs, rows):
    def kernel(own, other, trail, *refs):
        notes, sends, half = refs[:pairs], refs[pairs:2 * pairs], refs[2 * pairs]
        prior = jnp.concatenate([own[...], other[...]], axis=0)
        sent = requested([x[...] for x in notes], prior, 0, rows)
        for k in range(pairs):
            sends[k][...] = sent[k * rows:(k + 1) * rows, :].astype(BF16)
        size = padded(pairs)
        half[...] = jnp.zeros(half.shape, F32)
        for k in range(pairs):
            half[k:k + 1, :] = notes[k][...]
        half[size:, :] = trail[...]

    return kernel


def make_assess(pairs, parts, tiles, cells, share):
    size = padded(pairs)

    def kernel(own, other, message, mine, theirs, where, terms, local, *refs):
        outs, low_out, high_out, sums = refs[:pairs], refs[pairs], refs[pairs + 1], refs[pairs + 2]
        low, high = edge_windows(message[...], *halves(mine[...], theirs[...]), size, parts)
        low_out[...] = low.astype(BF16)
        high_out[...] = high.astype(BF16)
        fixed = []
        for h, prior in enumerate((own, other)):
            for p in range(parts):
                row = (2 * p + h) * size
                x = prior[p * tiles:(p + 1) * tiles, :].astype(F32)
                x = patch(x, low[row:row + 1, LANES:], high[row:row + 1, :LANES])
                fixed.append(x.astype(BF16))
        least, total, weighted = assess(
            fixed, where[...], terms[0:1, :], terms[1:2, :], local[...], 2 * parts, tiles, cells
        )
        sums[...] = weighted
        pack_mean(outs, 0, least, total, sums, share)

    return kernel


def make_second(pairs, parts, tiles, cells):
    size = padded(pairs)

    def kernel(keys, diff, pert, message, mine, theirs, low, high, *refs):
        got, prior = refs[:pairs], refs[pairs]
        below, above = [x[size:size + 8, :] for x in halves(mine[...], theirs[...])]
        arrived = jnp.concatenate([x[...] for x in got], axis=0)
        moved = pick_rows(keys[0], arrived)
        here_codes = message[size + 2:size + 2 + 2 * parts, :].astype(I32)
        codes = jnp.concatenate([here_codes[parts:], below[2:2 + parts, :].astype(I32)], axis=0)
        start = pick_rows(codes, low[...])
        codes = jnp.concatenate([here_codes[:parts], above[2 + parts:2 + 2 * parts, :].astype(I32)], axis=0)
        end = pick_rows(codes, high[...])
        d = widen(diff[...], below[0:1, :], above[1:2, :])
        for p in range(parts):
            x = patch(moved[p * tiles:(p + 1) * tiles, :], start[p:p + 1, LANES:], end[p:p + 1, :LANES])
            q = parts + p
            x = widen(x, start[q:q + 1, :LANES], end[q:q + 1, LANES:])
            x = diffuse(x, d)[:, LANES:LANES + cells]
            prior[p * tiles:(p + 1) * tiles, :] = (x + pert[0, p].astype(F32)).astype(BF16)

    return kernel


def make_send_second(pairs, rows, parts, tiles, cells, share):
    def kernel(own, other, where, terms, local, *refs):
        notes, kept, outs, sums = refs[:pairs], refs[pairs:2 * pairs], refs[2 * pairs:3 * pairs], refs[3 * pairs]
        prior = jnp.concatenate([own[...], other[...]], axis=0)
        sent = requested([x[...] for x in notes], prior, 1, rows)
        extra = kept[0].shape[1]
        for k in range(pairs):
            outs[k][:, :cells] = sent[k * rows:(k + 1) * rows, :].astype(BF16)
            outs[k][:, cells:cells + extra] = kept[k][...]
        least, total, weighted = assess(
            [x[p * tiles:(p + 1) * tiles, :] for x in (own, other) for p in range(parts)],
            where[...], terms[0:1, :], terms[2:3, :], local[...], 2 * parts, tiles, cells,
        )
        sums[...] = weighted
        pack_mean(outs, cells + extra, least, total, sums, share)

    return kernel


def make_last(pairs, rows, parts, tiles, cells):
    def kernel(keys, *refs):
        got, analysis, mean = refs[:pairs], refs[pairs], refs[pairs + 1]
        arrived = jnp.concatenate([x[:, :cells] for x in got], axis=0)
        picked = pick_rows(keys[1], arrived)
        for p in range(parts):
            analysis[p] = picked[p * tiles:(p + 1) * tiles, :].astype(BF16)
        share = mean.shape[2]
        extra = tiles // rows * share + LANES
        for c in range(CYCLES):
            for g, x in enumerate(unpack_mean(got, cells + c * extra, tiles, share)):
                mean[c, g * rows:(g + 1) * rows, :] = x

    return kernel


def body(
    state,
    diffusivity,
    model_perturbation,
    obs_values,
    obs_prec,
    obs_tile,
    obs_cell,
    pattern,
    loc_weight,
    anc_member,
    anc_slot,
):
    parts, tiles, cells = state.shape
    members = lax.axis_size("member")
    regions = lax.axis_size("region")
    capacity = max(2, 2 * parts * tiles // members)
    share = cells // members
    pairs = members // 2
    rows = 2 * capacity
    extra = tiles // rows * share + LANES
    blocks, per_block = obs_cell.shape
    count = blocks * per_block
    member_of = anc_member.reshape(CYCLES, parts, tiles)
    slot_of = anc_slot.reshape(CYCLES, parts, tiles)
    near = pattern.shape[1]
    ends = cells // LANES - 1

    def block(shape, at):
        lead = (0,) * (len(shape) - 1)
        return pl.BlockSpec(shape, lambda i: lead + (at,))

    edges = [state, state, diffusivity, diffusivity, model_perturbation, model_perturbation, member_of, slot_of]
    *notes, trail, keys = call(
        make_prepare(members, capacity, parts, tiles),
        [((1, LANES), F32)] * pairs + [((8, LANES), F32), ((CYCLES, parts * tiles, LANES), I32)],
        [pltpu.with_memory_space_constraint(x, pltpu.HBM) for x in edges],
        [
            block((parts, tiles, LANES), 0),
            block((parts, tiles, LANES), ends),
            block((tiles, LANES), 0),
            block((tiles, LANES), ends),
            block((1, parts, tiles, LANES), 0),
            block((1, parts, tiles, LANES), ends),
            whole_spec(member_of.shape),
            whole_spec(slot_of.shape),
        ],
        name="prepare",
    )

    def trade(x, k):
        return lax.ppermute(x, "member", [(i, i ^ k) for i in range(members)])

    def exchange(sends):
        got = {k: trade(sends[k], 2 * k) for k in range(pairs - 1, 0, -1)}
        return [sends[0]] + [got[k] for k in range(1, pairs)]

    notes = exchange(notes)

    where, terms, local = call(
        make_observe(blocks, per_block, tiles, near),
        [((2, count), I32), ((1 + CYCLES, count), F32), ((tiles, count), F32)],
        [obs_tile[None, :], obs_cell.T, obs_prec.T, jnp.swapaxes(obs_values, 1, 2), pattern.T, loc_weight.T],
        name="observe",
    )

    def noise_spec(c):
        return pl.BlockSpec((1, parts, tiles, cells), lambda i: (c, 0, 0, 0))

    args = [state, diffusivity, model_perturbation, trail]
    specs = [whole_spec(a.shape) for a in args]
    specs[2] = noise_spec(0)
    (prior,) = call(
        make_first(parts, tiles, cells), [((parts * tiles, cells), BF16)], args, specs, name="forecast_first"
    )
    other = trade(prior, 1)
    size = padded(pairs)
    *sends, half = call(
        make_send(pairs, rows),
        [((rows, cells), BF16)] * pairs + [((size + trail.shape[0], LANES), F32)],
        [prior, other, trail, *notes],
        name="send_first",
    )
    got = exchange(sends)
    message = jnp.concatenate([half, trade(half, 1)], axis=0)
    steps = []
    for i in range(members):
        first, last = (0, regions - 1) if i % 2 == 0 else (1, regions)
        steps += [(i * regions + r, i * regions + r + 1 - 2 * (i % 2)) for r in range(first, last)]
    mine = lax.ppermute(message, ("member", "region"), steps)
    theirs = trade(mine, 1)
    window = ((parts * 2 * size, 2 * LANES), BF16)
    sums = [((tiles, cells), F32)]
    *kept, low, high = call(
        make_assess(pairs, parts, tiles, cells, share),
        [((rows, extra), BF16)] * pairs + [window, window],
        [prior, other, message, mine, theirs, where, terms, local],
        scratch=sums,
        name="assess_first",
    )
    args = [keys, diffusivity, model_perturbation, message, mine, theirs, low, high, *got]
    specs = [whole_spec(a.shape) for a in args]
    specs[2] = noise_spec(1)
    (prior,) = call(
        make_second(pairs, parts, tiles, cells),
        [((parts * tiles, cells), BF16)],
        args,
        specs,
        name="forecast_second",
    )
    sends = call(
        make_send_second(pairs, rows, parts, tiles, cells, share),
        [((rows, cells + CYCLES * extra), BF16)] * pairs,
        [prior, trade(prior, 1), where, terms, local, *notes, *kept],
        scratch=sums,
        name="send_second",
    )
    got = exchange(sends)
    return tuple(
        call(
            make_last(pairs, rows, parts, tiles, cells),
            [(state.shape, BF16), ((CYCLES, tiles, share), F32)],
            [keys, *got],
            name="finish",
        )
    )


def solution(mesh):
    in_specs = (
        P("member", "region", None),
        P("region", None),
        P(None, "member", "region", None),
        P(None, "region", None),
        P("region", None),
        P("region"),
        P("region", None),
        P("region", None),
        P("region", None),
        P(None, "region", "member", None, None),
        P(None, "region", "member", None),
    )
    out_specs = (P("member", "region", None), P(None, "region", "member"))
    return jax.shard_map(body, mesh=mesh, in_specs=in_specs, out_specs=out_specs, check_vma=False)
```

```python
import jax
import jax.numpy as jnp
from jax import lax
from jax.experimental import pallas as pl
from jax.experimental.pallas import tpu as pltpu
from jax.sharding import PartitionSpec as P

CYCLES = 2
STEPS = 2
LANES = 128
F32 = jnp.float32
BF16 = jnp.bfloat16
I32 = jnp.int32
PARAMS = pltpu.CompilerParams(vmem_limit_bytes=48 * 1024 * 1024)


def iota(shape, dim):
    return lax.broadcasted_iota(I32, shape, dim)


def whole_spec(shape):
    zeros = (0,) * len(shape)
    return pl.BlockSpec(shape, lambda i: zeros)


def call(kernel, outs, args, specs=None, scratch=(), name=None):
    specs = specs or [whole_spec(a.shape) for a in args]
    return pl.pallas_call(
        kernel,
        out_shape=[jax.ShapeDtypeStruct(s, d) for s, d in outs],
        grid=(1,),
        in_specs=specs,
        out_specs=[whole_spec(s) for s, _ in outs],
        scratch_shapes=[pltpu.VMEM(s, d) for s, d in scratch],
        compiler_params=PARAMS,
        name=name,
    )(*args)


def column_of(row):
    n = row.shape[1]
    square = jnp.broadcast_to(row, (n, n))
    return jnp.sum(jnp.where(iota((n, n), 0) == iota((n, n), 1), square, 0), axis=1, keepdims=True)


def here():
    return lax.axis_index("member")


EDGE_AT = 32
STRIDE = 8


def apart(i, pairs):
    return (pairs - i) % pairs


def padded(pairs):
    return max(8, pairs)


def make_prepare(members, capacity, parts, tiles):
    width = 2 * STEPS
    pairs = members // 2
    rows = parts * tiles

    def kernel(st0, st1, df0, df1, pb0, pb1, am, slot, *outs):
        notes, trail, keys = outs[:pairs], outs[pairs], outs[pairs + 1]
        m = here()
        lane = iota((1, LANES), 1)
        last = tiles - 1
        trail[...] = jnp.zeros(trail.shape, F32)
        trail[0:1, :] = df1[last:last + 1, :]
        trail[1:2, :] = df0[0:1, :]
        edge = jnp.zeros((1, LANES), F32)
        for p in range(parts):
            for i, t in enumerate((last, 0)):
                source = am[0, p:p + 1, t:t + 1] ^ m
                code = (slot[0, p:p + 1, t:t + 1] * 2 + source % 2) * padded(pairs) + apart(source // 2, pairs)
                row = 2 + i * parts + p
                trail[row:row + 1, :] = jnp.broadcast_to(code.astype(F32), (1, LANES))
            fields = (st1[p, last:last + 1, :], st0[p, 0:1, :], pb1[0, p, last:last + 1, :], pb0[0, p, 0:1, :])
            for i, x in enumerate(fields):
                to = EDGE_AT + STRIDE * (4 * p + i)
                start = 0 if i % 2 else LANES - width
                moved = pltpu.roll(x.astype(F32), (to - start) % LANES, 1)
                edge = jnp.where((lane >= to) & (lane < to + width), moved, edge)
        before = (iota((tiles, tiles), 0) < iota((tiles, tiles), 1)).astype(F32)
        asked = jnp.zeros((pairs, LANES), F32)
        for c in range(CYCLES):
            seen = jnp.zeros((members, 1), F32)
            for p in range(parts):
                source = am[c, p:p + 1, :] ^ m
                named = (iota((members, tiles), 0) == source).astype(F32)
                earlier = seen + jnp.dot(named, before, preferred_element_type=F32)
                rank = jnp.sum(named * earlier, axis=0, keepdims=True).astype(I32)
                seen = seen + jnp.sum(named, axis=1, keepdims=True)
                half = source % 2
                code = half * rows + slot[c, p:p + 1, :] * tiles + iota((1, tiles), 1)
                spot = (iota((LANES, tiles), 0) == (2 * c + half) * capacity + rank).astype(F32)
                pair = jnp.where(iota((pairs, tiles), 0) == apart(source // 2, pairs), (code + 1).astype(F32), 0.0)
                asked = asked + lax.dot_general(pair, spot, (((1,), (1,)), ((), ())), preferred_element_type=F32)
                column = column_of((2 * apart(source // 2, pairs) + half) * capacity + rank)
                keys[c, p * tiles:(p + 1) * tiles, :] = jnp.broadcast_to(column, (tiles, LANES))
        for k in range(pairs):
            notes[k][...] = jnp.where(lane < EDGE_AT, asked[k:k + 1, :] - 1.0, edge)

    return kernel


def halves(mine, theirs):
    half = theirs.shape[0] // 2
    theirs = jnp.concatenate([theirs[half:, :], theirs[:half, :]], axis=0)
    first = jnp.broadcast_to(here() % 2, mine.shape) == 0
    return jnp.where(first, mine, theirs), jnp.where(first, theirs, mine)


def edge_windows(own, below, above, size, parts):
    width = 2 * STEPS

    def field(note, p, i):
        at = EDGE_AT + STRIDE * (4 * p + i)
        start = 0 if i % 2 else LANES - width
        both = jnp.concatenate([note[:size, :], note[size + 8:2 * size + 8, :]], axis=0)
        return pltpu.roll(both, (start - at) % LANES, 1)

    low, high = [], []
    for out, before, after in ((low, below, own), (high, own, above)):
        d = jnp.concatenate([before[size:size + 1, :], after[size + 1:size + 2, :]], axis=1)
        for p in range(parts):
            x = jnp.concatenate([field(before, p, 0), field(after, p, 1)], axis=1)
            x = diffuse(x, d) + jnp.concatenate([field(before, p, 2), field(after, p, 3)], axis=1)
            out.append(x.astype(BF16).astype(F32))
    return jnp.concatenate(low, axis=0), jnp.concatenate(high, axis=0)


def patch(x, first, last):
    tiles = x.shape[0]
    row, lane = iota((tiles, LANES), 0), iota((tiles, LANES), 1)
    head = jnp.where((row == 0) & (lane < STEPS), first, x[:, :LANES])
    tail = jnp.where((row == tiles - 1) & (lane >= LANES - STEPS), last, x[:, -LANES:])
    return jnp.concatenate([head, x[:, LANES:-LANES], tail], axis=1)


def widen(x, left, right):
    tiles = x.shape[0]
    row = iota((tiles, LANES), 0)
    before = jnp.where(row == 0, left, pltpu.roll(x[:, -LANES:], 1, 0))
    after = jnp.where(row == tiles - 1, right, pltpu.roll(x[:, :LANES], tiles - 1, 0))
    return jnp.concatenate([before, x, after], axis=1)


def diffuse(x, d):
    n = x.shape[1]
    for _ in range(STEPS):
        x = x + d * (pltpu.roll(x, 1, 1) - 2.0 * x + pltpu.roll(x, n - 1, 1))
    return x


def pick_rows(wanted, rows):
    m = rows.shape[0]
    n = wanted.shape[0]
    choice = (wanted[:, :m] == iota((n, m), 1)).astype(F32).astype(BF16)
    return jnp.dot(choice, rows, preferred_element_type=F32)


def requested(notes, prior, cycle, rows):
    pairs = len(notes)
    total = pairs * rows
    asked = jnp.concatenate(notes, axis=0)
    spread = jnp.broadcast_to(asked[:, None, :], (pairs, rows, LANES)).reshape(total, LANES)
    mine = iota((total, LANES), 1) == cycle * rows + iota((total, LANES), 0) % rows
    wanted = jnp.sum(jnp.where(mine, spread, 0.0), axis=1, keepdims=True).astype(I32)
    return pick_rows(jnp.broadcast_to(wanted, (total, LANES)), prior)


def make_observe(blocks, per_block, tiles, near):
    count = blocks * per_block

    def kernel(tile, cell, prec, value, pattern, weight, where, terms, local):
        def line(x):
            wide = jnp.concatenate([x] * per_block, axis=1)
            own = iota((per_block, count), 1) // blocks == iota((per_block, count), 0)
            return jnp.sum(jnp.where(own, wide, 0), axis=0, keepdims=True)

        at = line(cell[...])
        row = (at // LANES) * tiles + jnp.concatenate([tile[...]] * per_block, axis=1)
        pick = iota((2, count), 0) == 0
        where[...] = jnp.where(pick, row, at % LANES)
        terms[0:1, :] = line(prec[...])
        for c in range(CYCLES):
            terms[c + 1:c + 2, :] = line(value[c])
        group = iota((tiles, count), 1) % blocks
        total = jnp.zeros((tiles, count), F32)
        for k in range(near):
            total = total + jnp.where(column_of(pattern[k:k + 1, :]) == group, column_of(weight[k:k + 1, :]), 0.0)
        local[...] = total

    return kernel


def assess(prior, where, prec, value, local, parts, tiles, cells):
    blocks = cells // LANES
    rows = tiles * blocks
    count = where.shape[1]
    stacked = jnp.concatenate(
        [jnp.concatenate([x[:, k * LANES:(k + 1) * LANES] for k in range(blocks)], axis=0) for x in prior],
        axis=1,
    )
    choice = (iota((rows, count), 0) == where[0:1, :]).astype(F32).astype(BF16)
    lines = lax.dot_general(stacked, choice, (((0,), (0,)), ((), ())), preferred_element_type=F32)
    lane = iota((LANES, count), 0) == where[1:2, :]
    score = []
    for p in range(parts):
        predicted = jnp.sum(jnp.where(lane, lines[p * LANES:(p + 1) * LANES, :], 0.0), axis=0, keepdims=True)
        miss = value - predicted
        term = 0.5 * (prec * miss * miss)
        score.append(jnp.sum(local * term, axis=1, keepdims=True))
    least = score[0]
    for s in score[1:]:
        least = jnp.minimum(least, s)
    scale = [jnp.exp(least - s) for s in score]
    total = scale[0]
    for s in scale[1:]:
        total = total + s
    weighted = scale[0] * prior[0].astype(F32)
    for s, x in zip(scale[1:], prior[1:]):
        weighted = weighted + s * x.astype(F32)
    return least, total, weighted


def pieces(x):
    high = x.astype(BF16).astype(F32)
    middle = (x - high).astype(BF16).astype(F32)
    low = (x - high - middle).astype(BF16).astype(F32)
    return high, middle, low


def share_of(ref, member, share):
    if share % LANES == 0:
        return ref[:, pl.ds(pl.multiple_of(member * share, LANES), share)]
    return pltpu.roll(ref[...], ref.shape[1] - member * share, 1)[:, :share]


def pack_mean(outs, at, least, total, sums, share):
    rows = outs[0].shape[0]
    tiles = sums.shape[0]
    groups = tiles // rows
    m = here()
    lane = iota((rows, LANES), 1)
    misc = jnp.zeros((rows, LANES), F32)
    spot = 0
    for x in (least, total):
        for piece in pieces(x):
            for g in range(groups):
                misc = jnp.where(lane == spot, piece[g * rows:(g + 1) * rows, :], misc)
                spot += 1
    end = at + groups * share
    for k, out in enumerate(outs):
        block = share_of(sums, m ^ (2 * apart(k, len(outs))), share)
        for g in range(groups):
            out[:, at + g * share:at + (g + 1) * share] = block[g * rows:(g + 1) * rows, :].astype(BF16)
        out[:, end:end + LANES] = misc.astype(BF16)


def unpack_mean(got, at, tiles, share):
    rows = got[0].shape[0]
    groups = tiles // rows
    end = at + groups * share
    misc = [x[:, end:end + LANES].astype(F32) for x in got]
    means = []
    for g in range(groups):
        stats = []
        for x in misc:
            pair = []
            for kind in range(2):
                spot = [(kind * 3 + piece) * groups + g for piece in range(3)]
                high, middle, low = [x[:, i:i + 1] for i in spot]
                pair.append(high + middle + low)
            stats.append(pair)
        lowest = stats[0][0]
        for least, _ in stats[1:]:
            lowest = jnp.minimum(lowest, least)
        top, bottom = 0.0, 0.0
        for x, (least, total) in zip(got, stats):
            scale = jnp.exp(lowest - least)
            top = top + scale * x[:, at + g * share:at + (g + 1) * share].astype(F32)
            bottom = bottom + scale * total
        means.append(top / bottom)
    return means


def make_first(parts, tiles, cells):
    def kernel(state, diff, pert, after, prior):
        nothing = jnp.zeros((1, LANES), F32)
        d = widen(diff[...], nothing, nothing)
        for p in range(parts):
            x = diffuse(widen(state[p].astype(F32), nothing, nothing), d)
            now = x[:, LANES:LANES + cells] + pert[0, p].astype(F32)
            prior[p * tiles:(p + 1) * tiles, :] = now.astype(BF16)

    return kernel


def make_send(pairs, rows):
    def kernel(own, other, trail, *refs):
        notes, sends, half = refs[:pairs], refs[pairs:2 * pairs], refs[2 * pairs]
        prior = jnp.concatenate([own[...], other[...]], axis=0)
        sent = requested([x[...] for x in notes], prior, 0, rows)
        for k in range(pairs):
            sends[k][...] = sent[k * rows:(k + 1) * rows, :].astype(BF16)
        size = padded(pairs)
        half[...] = jnp.zeros(half.shape, F32)
        for k in range(pairs):
            half[k:k + 1, :] = notes[k][...]
        half[size:, :] = trail[...]

    return kernel


def make_assess(pairs, parts, tiles, cells, share):
    size = padded(pairs)

    def kernel(own, other, low, high, where, terms, local, *refs):
        outs, sums = refs[:pairs], refs[pairs]
        fixed = []
        for h, prior in enumerate((own, other)):
            for p in range(parts):
                row = (2 * p + h) * size
                x = prior[p * tiles:(p + 1) * tiles, :].astype(F32)
                x = patch(x, low[row:row + 1, LANES:], high[row:row + 1, :LANES])
                fixed.append(x.astype(BF16))
        least, total, weighted = assess(
            fixed, where[...], terms[0:1, :], terms[1:2, :], local[...], 2 * parts, tiles, cells
        )
        sums[...] = weighted
        pack_mean(outs, 0, least, total, sums, share)

    return kernel


def make_second(pairs, parts, tiles, cells):
    size = padded(pairs)

    def kernel(keys, diff, pert, message, mine, theirs, *refs):
        got, prior, low_out, high_out = refs[:pairs], refs[pairs], refs[pairs + 1], refs[pairs + 2]
        below, above = halves(mine[...], theirs[...])
        low, high = edge_windows(message[...], below, above, size, parts)
        low_out[...] = low
        high_out[...] = high
        below, above = below[size:size + 8, :], above[size:size + 8, :]
        arrived = jnp.concatenate([x[...] for x in got], axis=0)
        moved = pick_rows(keys[0], arrived)
        here_codes = message[size + 2:size + 2 + 2 * parts, :].astype(I32)
        codes = jnp.concatenate([here_codes[parts:], below[2:2 + parts, :].astype(I32)], axis=0)
        start = pick_rows(codes, low.astype(BF16))
        codes = jnp.concatenate([here_codes[:parts], above[2 + parts:2 + 2 * parts, :].astype(I32)], axis=0)
        end = pick_rows(codes, high.astype(BF16))
        d = widen(diff[...], below[0:1, :], above[1:2, :])
        for p in range(parts):
            x = patch(moved[p * tiles:(p + 1) * tiles, :], start[p:p + 1, LANES:], end[p:p + 1, :LANES])
            q = parts + p
            x = widen(x, start[q:q + 1, :LANES], end[q:q + 1, LANES:])
            x = diffuse(x, d)[:, LANES:LANES + cells]
            prior[p * tiles:(p + 1) * tiles, :] = (x + pert[0, p].astype(F32)).astype(BF16)

    return kernel


def make_send_second(pairs, rows, parts, tiles, cells, share):
    def kernel(own, other, where, terms, local, *refs):
        notes, kept, outs, sums = refs[:pairs], refs[pairs:2 * pairs], refs[2 * pairs:3 * pairs], refs[3 * pairs]
        prior = jnp.concatenate([own[...], other[...]], axis=0)
        sent = requested([x[...] for x in notes], prior, 1, rows)
        extra = kept[0].shape[1]
        for k in range(pairs):
            outs[k][:, :cells] = sent[k * rows:(k + 1) * rows, :].astype(BF16)
            outs[k][:, cells:cells + extra] = kept[k][...]
        least, total, weighted = assess(
            [x[p * tiles:(p + 1) * tiles, :] for x in (own, other) for p in range(parts)],
            where[...], terms[0:1, :], terms[2:3, :], local[...], 2 * parts, tiles, cells,
        )
        sums[...] = weighted
        pack_mean(outs, cells + extra, least, total, sums, share)

    return kernel


def make_last(pairs, rows, parts, tiles, cells):
    def kernel(keys, *refs):
        got, analysis, mean = refs[:pairs], refs[pairs], refs[pairs + 1]
        arrived = jnp.concatenate([x[:, :cells] for x in got], axis=0)
        picked = pick_rows(keys[1], arrived)
        for p in range(parts):
            analysis[p] = picked[p * tiles:(p + 1) * tiles, :].astype(BF16)
        share = mean.shape[2]
        extra = tiles // rows * share + LANES
        for c in range(CYCLES):
            for g, x in enumerate(unpack_mean(got, cells + c * extra, tiles, share)):
                mean[c, g * rows:(g + 1) * rows, :] = x

    return kernel


def body(
    state,
    diffusivity,
    model_perturbation,
    obs_values,
    obs_prec,
    obs_tile,
    obs_cell,
    pattern,
    loc_weight,
    anc_member,
    anc_slot,
):
    parts, tiles, cells = state.shape
    members = lax.axis_size("member")
    regions = lax.axis_size("region")
    capacity = max(2, 2 * parts * tiles // members)
    share = cells // members
    pairs = members // 2
    rows = 2 * capacity
    extra = tiles // rows * share + LANES
    blocks, per_block = obs_cell.shape
    count = blocks * per_block
    member_of = anc_member.reshape(CYCLES, parts, tiles)
    slot_of = anc_slot.reshape(CYCLES, parts, tiles)
    near = pattern.shape[1]
    ends = cells // LANES - 1

    def block(shape, at):
        lead = (0,) * (len(shape) - 1)
        return pl.BlockSpec(shape, lambda i: lead + (at,))

    edges = [state, state, diffusivity, diffusivity, model_perturbation, model_perturbation, member_of, slot_of]
    *notes, trail, keys = call(
        make_prepare(members, capacity, parts, tiles),
        [((1, LANES), F32)] * pairs + [((8, LANES), F32), ((CYCLES, parts * tiles, LANES), I32)],
        [pltpu.with_memory_space_constraint(x, pltpu.HBM) for x in edges],
        [
            block((parts, tiles, LANES), 0),
            block((parts, tiles, LANES), ends),
            block((tiles, LANES), 0),
            block((tiles, LANES), ends),
            block((1, parts, tiles, LANES), 0),
            block((1, parts, tiles, LANES), ends),
            whole_spec(member_of.shape),
            whole_spec(slot_of.shape),
        ],
        name="prepare",
    )

    def trade(x, k):
        return lax.ppermute(x, "member", [(i, i ^ k) for i in range(members)])

    def exchange(sends):
        return [sends[0]] + [trade(sends[k], 2 * apart(k, pairs)) for k in range(1, pairs)]

    notes = exchange(notes)

    where, terms, local = call(
        make_observe(blocks, per_block, tiles, near),
        [((2, count), I32), ((1 + CYCLES, count), F32), ((tiles, count), F32)],
        [obs_tile[None, :], obs_cell.T, obs_prec.T, jnp.swapaxes(obs_values, 1, 2), pattern.T, loc_weight.T],
        name="observe",
    )

    def noise_spec(c):
        return pl.BlockSpec((1, parts, tiles, cells), lambda i: (c, 0, 0, 0))

    args = [state, diffusivity, model_perturbation, trail]
    specs = [whole_spec(a.shape) for a in args]
    specs[2] = noise_spec(0)
    (prior,) = call(
        make_first(parts, tiles, cells), [((parts * tiles, cells), BF16)], args, specs, name="forecast_first"
    )
    other = trade(prior, 1)
    size = padded(pairs)
    *sends, half = call(
        make_send(pairs, rows),
        [((rows, cells), BF16)] * pairs + [((size + trail.shape[0], LANES), F32)],
        [prior, other, trail, *notes],
        name="send_first",
    )
    got = exchange(sends)
    message = jnp.concatenate([half, trade(half, 1)], axis=0)
    steps = []
    for i in range(members):
        first, last = (0, regions - 1) if i % 2 == 0 else (1, regions)
        steps += [(i * regions + r, i * regions + r + 1 - 2 * (i % 2)) for r in range(first, last)]
    mine = lax.ppermute(message, ("member", "region"), steps)
    theirs = trade(mine, 1)
    window = ((parts * 2 * size, 2 * LANES), F32)
    sums = [((tiles, cells), F32)]
    args = [keys, diffusivity, model_perturbation, message, mine, theirs, *got]
    specs = [whole_spec(a.shape) for a in args]
    specs[2] = noise_spec(1)
    second, low, high = call(
        make_second(pairs, parts, tiles, cells),
        [((parts * tiles, cells), BF16), window, window],
        args,
        specs,
        name="forecast_second",
    )
    kept = call(
        make_assess(pairs, parts, tiles, cells, share),
        [((rows, extra), BF16)] * pairs,
        [prior, other, low, high, where, terms, local],
        scratch=sums,
        name="assess_first",
    )
    sends = call(
        make_send_second(pairs, rows, parts, tiles, cells, share),
        [((rows, cells + CYCLES * extra), BF16)] * pairs,
        [second, trade(second, 1), where, terms, local, *notes, *kept],
        scratch=sums,
        name="send_second",
    )
    got = exchange(sends)
    return tuple(
        call(
            make_last(pairs, rows, parts, tiles, cells),
            [(state.shape, BF16), ((CYCLES, tiles, share), F32)],
            [keys, *got],
            name="finish",
        )
    )


def solution(mesh):
    in_specs = (
        P("member", "region", None),
        P("region", None),
        P(None, "member", "region", None),
        P(None, "region", None),
        P("region", None),
        P("region"),
        P("region", None),
        P("region", None),
        P("region", None),
        P(None, "region", "member", None, None),
        P(None, "region", "member", None),
    )
    out_specs = (P("member", "region", None), P(None, "region", "member"))
    return jax.shard_map(body, mesh=mesh, in_specs=in_specs, out_specs=out_specs, check_vma=False)
```

```python
import jax
import jax.numpy as jnp
from jax import lax
from jax.experimental import pallas as pl
from jax.experimental.pallas import tpu as pltpu
from jax.sharding import PartitionSpec as P

CYCLES = 2
STEPS = 2
LANES = 128
F32 = jnp.float32
BF16 = jnp.bfloat16
I32 = jnp.int32
PARAMS = pltpu.CompilerParams(vmem_limit_bytes=48 * 1024 * 1024)


def iota(shape, dim):
    return lax.broadcasted_iota(I32, shape, dim)


def whole_spec(shape):
    zeros = (0,) * len(shape)
    return pl.BlockSpec(shape, lambda i: zeros)


def call(kernel, outs, args, specs=None, scratch=(), name=None):
    specs = specs or [whole_spec(a.shape) for a in args]
    return pl.pallas_call(
        kernel,
        out_shape=[jax.ShapeDtypeStruct(s, d) for s, d in outs],
        grid=(1,),
        in_specs=specs,
        out_specs=[whole_spec(s) for s, _ in outs],
        scratch_shapes=[pltpu.VMEM(s, d) for s, d in scratch],
        compiler_params=PARAMS,
        name=name,
    )(*args)


def column_of(row):
    n = row.shape[1]
    square = jnp.broadcast_to(row, (n, n))
    return jnp.sum(jnp.where(iota((n, n), 0) == iota((n, n), 1), square, 0), axis=1, keepdims=True)


def here():
    return lax.axis_index("member")


EDGE_AT = 32
STRIDE = 8


def apart(i, pairs):
    return (pairs - i) % pairs


def padded(pairs):
    return max(8, pairs)


def make_prepare(members, capacity, parts, tiles):
    width = 2 * STEPS
    pairs = members // 2
    rows = parts * tiles

    def kernel(st0, st1, df0, df1, pb0, pb1, am, slot, *outs):
        notes, trail, keys = outs[:pairs], outs[pairs], outs[pairs + 1]
        m = here()
        lane = iota((1, LANES), 1)
        last = tiles - 1
        trail[...] = jnp.zeros(trail.shape, F32)
        trail[0:1, :] = df1[last:last + 1, :]
        trail[1:2, :] = df0[0:1, :]
        edge = jnp.zeros((1, LANES), F32)
        for p in range(parts):
            for i, t in enumerate((last, 0)):
                source = am[0, p:p + 1, t:t + 1] ^ m
                code = (slot[0, p:p + 1, t:t + 1] * 2 + source % 2) * padded(pairs) + apart(source // 2, pairs)
                row = 2 + i * parts + p
                trail[row:row + 1, :] = jnp.broadcast_to(code.astype(F32), (1, LANES))
            fields = (st1[p, last:last + 1, :], st0[p, 0:1, :], pb1[0, p, last:last + 1, :], pb0[0, p, 0:1, :])
            for i, x in enumerate(fields):
                to = EDGE_AT + STRIDE * (4 * p + i)
                start = 0 if i % 2 else LANES - width
                moved = pltpu.roll(x.astype(F32), (to - start) % LANES, 1)
                edge = jnp.where((lane >= to) & (lane < to + width), moved, edge)
        before = (iota((tiles, tiles), 0) < iota((tiles, tiles), 1)).astype(F32)
        asked = jnp.zeros((pairs, LANES), F32)
        for c in range(CYCLES):
            seen = jnp.zeros((members, 1), F32)
            for p in range(parts):
                source = am[c, p:p + 1, :] ^ m
                named = (iota((members, tiles), 0) == source).astype(F32)
                earlier = seen + jnp.dot(named, before, preferred_element_type=F32)
                rank = jnp.sum(named * earlier, axis=0, keepdims=True).astype(I32)
                seen = seen + jnp.sum(named, axis=1, keepdims=True)
                half = source % 2
                code = half * rows + slot[c, p:p + 1, :] * tiles + iota((1, tiles), 1)
                spot = (iota((LANES, tiles), 0) == (2 * c + half) * capacity + rank).astype(F32)
                pair = jnp.where(iota((pairs, tiles), 0) == apart(source // 2, pairs), (code + 1).astype(F32), 0.0)
                asked = asked + lax.dot_general(pair, spot, (((1,), (1,)), ((), ())), preferred_element_type=F32)
                column = column_of((2 * apart(source // 2, pairs) + half) * capacity + rank)
                keys[c, p * tiles:(p + 1) * tiles, :] = jnp.broadcast_to(column, (tiles, LANES))
        for k in range(pairs):
            notes[k][...] = jnp.where(lane < EDGE_AT, asked[k:k + 1, :] - 1.0, edge)

    return kernel


def halves(mine, theirs):
    half = theirs.shape[0] // 2
    theirs = jnp.concatenate([theirs[half:, :], theirs[:half, :]], axis=0)
    first = jnp.broadcast_to(here() % 2, mine.shape) == 0
    return jnp.where(first, mine, theirs), jnp.where(first, theirs, mine)


def edge_windows(own, below, above, size, parts):
    width = 2 * STEPS

    def field(note, p, i):
        at = EDGE_AT + STRIDE * (4 * p + i)
        start = 0 if i % 2 else LANES - width
        both = jnp.concatenate([note[:size, :], note[size + 8:2 * size + 8, :]], axis=0)
        return pltpu.roll(both, (start - at) % LANES, 1)

    low, high = [], []
    for out, before, after in ((low, below, own), (high, own, above)):
        d = jnp.concatenate([before[size:size + 1, :], after[size + 1:size + 2, :]], axis=1)
        for p in range(parts):
            x = jnp.concatenate([field(before, p, 0), field(after, p, 1)], axis=1)
            x = diffuse(x, d) + jnp.concatenate([field(before, p, 2), field(after, p, 3)], axis=1)
            out.append(x.astype(BF16).astype(F32))
    return jnp.concatenate(low, axis=0), jnp.concatenate(high, axis=0)


def patch(x, first, last, width):
    tiles = x.shape[0]
    row, lane = iota((tiles, LANES), 0), iota((tiles, LANES), 1)
    head = jnp.where((row == 0) & (lane < width), first, x[:, :LANES])
    tail = jnp.where((row == tiles - 1) & (lane >= LANES - width), last, x[:, -LANES:])
    return jnp.concatenate([head, x[:, LANES:-LANES], tail], axis=1)


def widen(x, left, right):
    tiles = x.shape[0]
    row = iota((tiles, LANES), 0)
    before = jnp.where(row == 0, left, pltpu.roll(x[:, -LANES:], 1, 0))
    after = jnp.where(row == tiles - 1, right, pltpu.roll(x[:, :LANES], tiles - 1, 0))
    return jnp.concatenate([before, x, after], axis=1)


def diffuse(x, d):
    n = x.shape[1]
    for _ in range(STEPS):
        x = x + d * (pltpu.roll(x, 1, 1) - 2.0 * x + pltpu.roll(x, n - 1, 1))
    return x


def pick_rows(wanted, rows):
    m = rows.shape[0]
    n = wanted.shape[0]
    choice = (wanted[:, :m] == iota((n, m), 1)).astype(F32).astype(BF16)
    return jnp.dot(choice, rows, preferred_element_type=F32)


def requested(notes, prior, cycle, rows):
    pairs = len(notes)
    total = pairs * rows
    asked = jnp.concatenate(notes, axis=0)
    spread = jnp.broadcast_to(asked[:, None, :], (pairs, rows, LANES)).reshape(total, LANES)
    mine = iota((total, LANES), 1) == cycle * rows + iota((total, LANES), 0) % rows
    wanted = jnp.sum(jnp.where(mine, spread, 0.0), axis=1, keepdims=True).astype(I32)
    return pick_rows(jnp.broadcast_to(wanted, (total, LANES)), prior)


def make_observe(blocks, per_block, tiles, near):
    count = blocks * per_block

    def kernel(tile, cell, prec, value, pattern, weight, where, terms, local):
        def line(x):
            wide = jnp.concatenate([x] * per_block, axis=1)
            own = iota((per_block, count), 1) // blocks == iota((per_block, count), 0)
            return jnp.sum(jnp.where(own, wide, 0), axis=0, keepdims=True)

        at = line(cell[...])
        row = (at // LANES) * tiles + jnp.concatenate([tile[...]] * per_block, axis=1)
        pick = iota((2, count), 0) == 0
        where[...] = jnp.where(pick, row, at % LANES)
        terms[0:1, :] = line(prec[...])
        for c in range(CYCLES):
            terms[c + 1:c + 2, :] = line(value[c])
        group = iota((tiles, count), 1) % blocks
        total = jnp.zeros((tiles, count), F32)
        for k in range(near):
            total = total + jnp.where(column_of(pattern[k:k + 1, :]) == group, column_of(weight[k:k + 1, :]), 0.0)
        local[...] = total

    return kernel


def assess(prior, where, prec, value, local, parts, tiles, cells):
    blocks = cells // LANES
    rows = tiles * blocks
    count = where.shape[1]
    stacked = jnp.concatenate(
        [jnp.concatenate([x[:, k * LANES:(k + 1) * LANES] for k in range(blocks)], axis=0) for x in prior],
        axis=1,
    )
    choice = (iota((rows, count), 0) == where[0:1, :]).astype(F32).astype(BF16)
    lines = lax.dot_general(stacked, choice, (((0,), (0,)), ((), ())), preferred_element_type=F32)
    lane = iota((LANES, count), 0) == where[1:2, :]
    score = []
    for p in range(parts):
        predicted = jnp.sum(jnp.where(lane, lines[p * LANES:(p + 1) * LANES, :], 0.0), axis=0, keepdims=True)
        miss = value - predicted
        term = 0.5 * (prec * miss * miss)
        score.append(jnp.sum(local * term, axis=1, keepdims=True))
    least = score[0]
    for s in score[1:]:
        least = jnp.minimum(least, s)
    scale = [jnp.exp(least - s) for s in score]
    total = scale[0]
    for s in scale[1:]:
        total = total + s
    weighted = scale[0] * prior[0].astype(F32)
    for s, x in zip(scale[1:], prior[1:]):
        weighted = weighted + s * x.astype(F32)
    return least, total, weighted


def pieces(x):
    high = x.astype(BF16).astype(F32)
    middle = (x - high).astype(BF16).astype(F32)
    low = (x - high - middle).astype(BF16).astype(F32)
    return high, middle, low


def share_of(ref, member, share):
    if share % LANES == 0:
        return ref[:, pl.ds(pl.multiple_of(member * share, LANES), share)]
    return pltpu.roll(ref[...], ref.shape[1] - member * share, 1)[:, :share]


def pack_mean(outs, at, least, total, sums, share):
    rows = outs[0].shape[0]
    tiles = sums.shape[0]
    groups = tiles // rows
    m = here()
    lane = iota((rows, LANES), 1)
    misc = jnp.zeros((rows, LANES), F32)
    spot = 0
    for x in (least, total):
        for piece in pieces(x):
            for g in range(groups):
                misc = jnp.where(lane == spot, piece[g * rows:(g + 1) * rows, :], misc)
                spot += 1
    end = at + groups * share
    for k, out in enumerate(outs):
        block = share_of(sums, m ^ (2 * apart(k, len(outs))), share)
        for g in range(groups):
            out[:, at + g * share:at + (g + 1) * share] = block[g * rows:(g + 1) * rows, :].astype(BF16)
        out[:, end:end + LANES] = misc.astype(BF16)


def unpack_mean(got, at, tiles, share):
    rows = got[0].shape[0]
    groups = tiles // rows
    end = at + groups * share
    misc = [x[:, end:end + LANES].astype(F32) for x in got]
    means = []
    for g in range(groups):
        stats = []
        for x in misc:
            pair = []
            for kind in range(2):
                spot = [(kind * 3 + piece) * groups + g for piece in range(3)]
                high, middle, low = [x[:, i:i + 1] for i in spot]
                pair.append(high + middle + low)
            stats.append(pair)
        lowest = stats[0][0]
        for least, _ in stats[1:]:
            lowest = jnp.minimum(lowest, least)
        top, bottom = 0.0, 0.0
        for x, (least, total) in zip(got, stats):
            scale = jnp.exp(lowest - least)
            top = top + scale * x[:, at + g * share:at + (g + 1) * share].astype(F32)
            bottom = bottom + scale * total
        means.append(top / bottom)
    return means


def make_first(parts, tiles, cells):
    def kernel(state, diff, pert, after, prior):
        nothing = jnp.zeros((1, LANES), F32)
        d = widen(diff[...], nothing, nothing)
        for p in range(parts):
            x = diffuse(widen(state[p].astype(F32), nothing, nothing), d)
            now = x[:, LANES:LANES + cells] + pert[0, p].astype(F32)
            prior[p * tiles:(p + 1) * tiles, :] = now.astype(BF16)

    return kernel


def make_send(pairs, rows):
    def kernel(own, other, trail, *refs):
        notes, sends, half = refs[:pairs], refs[pairs:2 * pairs], refs[2 * pairs]
        prior = jnp.concatenate([own[...], other[...]], axis=0)
        sent = requested([x[...] for x in notes], prior, 0, rows)
        for k in range(pairs):
            sends[k][...] = sent[k * rows:(k + 1) * rows, :].astype(BF16)
        size = padded(pairs)
        half[...] = jnp.zeros(half.shape, F32)
        for k in range(pairs):
            half[k:k + 1, :] = notes[k][...]
        half[size:, :] = trail[...]

    return kernel


def make_assess(pairs, parts, tiles, cells, share):
    size = padded(pairs)

    def kernel(own, other, message, mine, theirs, where, terms, local, *refs):
        outs, low_out, high_out, sums = refs[:pairs], refs[pairs], refs[pairs + 1], refs[pairs + 2]
        low, high = edge_windows(message[...], *halves(mine[...], theirs[...]), size, parts)
        low_out[...] = low
        high_out[...] = high
        fixed = []
        for h, prior in enumerate((own, other)):
            for p in range(parts):
                row = (2 * p + h) * size
                x = prior[p * tiles:(p + 1) * tiles, :].astype(F32)
                x = patch(x, low[row:row + 1, LANES:], high[row:row + 1, :LANES], STEPS)
                fixed.append(x.astype(BF16))
        least, total, weighted = assess(
            fixed, where[...], terms[0:1, :], terms[1:2, :], local[...], 2 * parts, tiles, cells
        )
        sums[...] = weighted
        pack_mean(outs, 0, least, total, sums, share)

    return kernel


def make_second(pairs, parts, tiles, cells):
    def kernel(keys, diff, pert, after, also, *refs):
        got, prior, rim = refs[:pairs], refs[pairs], refs[pairs + 1]
        arrived = jnp.concatenate([x[...] for x in got], axis=0)
        moved = pick_rows(keys[0], arrived)
        nothing = jnp.zeros((1, LANES), F32)
        d = widen(diff[...], nothing, nothing)
        last = tiles - 1
        for p in range(parts):
            x = moved[p * tiles:(p + 1) * tiles, :]
            noise = pert[0, p].astype(F32)
            ends = (x[0:1, :LANES], x[last:, -LANES:], noise[0:1, :LANES], noise[last:, -LANES:])
            for i, row in enumerate(ends):
                rim[i * parts + p:i * parts + p + 1, :] = row
            x = diffuse(widen(x, nothing, nothing), d)[:, LANES:LANES + cells]
            prior[p * tiles:(p + 1) * tiles, :] = (x + noise).astype(BF16)

    return kernel


def rims(own, other, message, below, above, low, high, size, parts):
    n = 2 * parts
    lane = iota((n, LANES), 1)

    def both(i):
        return jnp.concatenate([own[i * parts:(i + 1) * parts, :], other[i * parts:(i + 1) * parts, :]], axis=0)

    def codes(note, i):
        at = size + 2 + i * parts
        first = note[at:at + parts, :].astype(I32)
        at += size + 8
        return jnp.concatenate([first, note[at:at + parts, :].astype(I32) ^ size], axis=0)

    def picked(here_codes, there_codes, windows):
        x = pick_rows(jnp.concatenate([here_codes, there_codes], axis=0), windows.astype(BF16))
        return x[:n, :], x[n:, :]

    fix, halo = picked(codes(message, 1), codes(below, 0), low)
    x = jnp.concatenate([halo[:, :LANES], jnp.where(lane < STEPS, fix[:, LANES:], both(0))], axis=1)
    d = jnp.concatenate([below[size:size + 1, :], message[size + 1:size + 2, :]], axis=1)
    first = diffuse(x, d)[:, LANES:] + both(2)
    fix, halo = picked(codes(message, 0), codes(above, 1), high)
    x = jnp.concatenate([jnp.where(lane >= LANES - STEPS, fix[:, :LANES], both(1)), halo[:, LANES:]], axis=1)
    d = jnp.concatenate([message[size:size + 1, :], above[size + 1:size + 2, :]], axis=1)
    return first, diffuse(x, d)[:, :LANES] + both(3)


def make_send_second(pairs, rows, parts, tiles, cells, share):
    size = padded(pairs)

    def kernel(own, other, rim, other_rim, message, mine, theirs, low, high, where, terms, local, *refs):
        notes, kept, outs, sums = refs[:pairs], refs[pairs:2 * pairs], refs[2 * pairs:3 * pairs], refs[3 * pairs]
        below, above = halves(mine[...], theirs[...])
        first, last = rims(rim[...], other_rim[...], message[...], below, above, low[...], high[...], size, parts)
        prior = []
        for h, x in enumerate((own, other)):
            for p in range(parts):
                q = h * parts + p
                now = x[p * tiles:(p + 1) * tiles, :].astype(F32)
                now = patch(now, first[q:q + 1, :], last[q:q + 1, :], 2 * STEPS)
                prior.append(now.astype(BF16))
        sent = requested([x[...] for x in notes], jnp.concatenate(prior, axis=0), 1, rows)
        extra = kept[0].shape[1]
        for k in range(pairs):
            outs[k][:, :cells] = sent[k * rows:(k + 1) * rows, :].astype(BF16)
            outs[k][:, cells:cells + extra] = kept[k][...]
        least, total, weighted = assess(
            prior, where[...], terms[0:1, :], terms[2:3, :], local[...], 2 * parts, tiles, cells
        )
        sums[...] = weighted
        pack_mean(outs, cells + extra, least, total, sums, share)

    return kernel


def make_last(pairs, rows, parts, tiles, cells):
    def kernel(keys, *refs):
        got, analysis, mean = refs[:pairs], refs[pairs], refs[pairs + 1]
        arrived = jnp.concatenate([x[:, :cells] for x in got], axis=0)
        picked = pick_rows(keys[1], arrived)
        for p in range(parts):
            analysis[p] = picked[p * tiles:(p + 1) * tiles, :].astype(BF16)
        share = mean.shape[2]
        extra = tiles // rows * share + LANES
        for c in range(CYCLES):
            for g, x in enumerate(unpack_mean(got, cells + c * extra, tiles, share)):
                mean[c, g * rows:(g + 1) * rows, :] = x

    return kernel


def body(
    state,
    diffusivity,
    model_perturbation,
    obs_values,
    obs_prec,
    obs_tile,
    obs_cell,
    pattern,
    loc_weight,
    anc_member,
    anc_slot,
):
    parts, tiles, cells = state.shape
    members = lax.axis_size("member")
    regions = lax.axis_size("region")
    capacity = max(2, 2 * parts * tiles // members)
    share = cells // members
    pairs = members // 2
    rows = 2 * capacity
    extra = tiles // rows * share + LANES
    blocks, per_block = obs_cell.shape
    count = blocks * per_block
    member_of = anc_member.reshape(CYCLES, parts, tiles)
    slot_of = anc_slot.reshape(CYCLES, parts, tiles)
    near = pattern.shape[1]
    ends = cells // LANES - 1

    def block(shape, at):
        lead = (0,) * (len(shape) - 1)
        return pl.BlockSpec(shape, lambda i: lead + (at,))

    edges = [state, state, diffusivity, diffusivity, model_perturbation, model_perturbation, member_of, slot_of]
    *notes, trail, keys = call(
        make_prepare(members, capacity, parts, tiles),
        [((1, LANES), F32)] * pairs + [((8, LANES), F32), ((CYCLES, parts * tiles, LANES), I32)],
        [pltpu.with_memory_space_constraint(x, pltpu.HBM) for x in edges],
        [
            block((parts, tiles, LANES), 0),
            block((parts, tiles, LANES), ends),
            block((tiles, LANES), 0),
            block((tiles, LANES), ends),
            block((1, parts, tiles, LANES), 0),
            block((1, parts, tiles, LANES), ends),
            whole_spec(member_of.shape),
            whole_spec(slot_of.shape),
        ],
        name="prepare",
    )

    def trade(x, k):
        return lax.ppermute(x, "member", [(i, i ^ k) for i in range(members)])

    def exchange(sends):
        return [sends[0]] + [trade(sends[k], 2 * apart(k, pairs)) for k in range(1, pairs)]

    notes = exchange(notes)

    where, terms, local = call(
        make_observe(blocks, per_block, tiles, near),
        [((2, count), I32), ((1 + CYCLES, count), F32), ((tiles, count), F32)],
        [obs_tile[None, :], obs_cell.T, obs_prec.T, jnp.swapaxes(obs_values, 1, 2), pattern.T, loc_weight.T],
        name="observe",
    )

    def noise_spec(c):
        return pl.BlockSpec((1, parts, tiles, cells), lambda i: (c, 0, 0, 0))

    args = [state, diffusivity, model_perturbation, trail]
    specs = [whole_spec(a.shape) for a in args]
    specs[2] = noise_spec(0)
    (prior,) = call(
        make_first(parts, tiles, cells), [((parts * tiles, cells), BF16)], args, specs, name="forecast_first"
    )
    other = trade(prior, 1)
    size = padded(pairs)
    *sends, half = call(
        make_send(pairs, rows),
        [((rows, cells), BF16)] * pairs + [((size + trail.shape[0], LANES), F32)],
        [prior, other, trail, *notes],
        name="send_first",
    )
    got = exchange(sends)
    message = jnp.concatenate([half, trade(half, 1)], axis=0)
    steps = []
    for i in range(members):
        first, last = (0, regions - 1) if i % 2 == 0 else (1, regions)
        steps += [(i * regions + r, i * regions + r + 1 - 2 * (i % 2)) for r in range(first, last)]
    mine = lax.ppermute(message, ("member", "region"), steps)
    theirs = trade(mine, 1)
    window = ((parts * 2 * size, 2 * LANES), F32)
    sums = [((tiles, cells), F32)]
    args = [keys, diffusivity, model_perturbation, where, mine, *got]
    specs = [whole_spec(a.shape) for a in args]
    specs[2] = noise_spec(1)
    second, rim = call(
        make_second(pairs, parts, tiles, cells),
        [((parts * tiles, cells), BF16), ((4 * parts, LANES), F32)],
        args,
        specs,
        name="forecast_second",
    )
    *kept, low, high = call(
        make_assess(pairs, parts, tiles, cells, share),
        [((rows, extra), BF16)] * pairs + [window, window],
        [prior, other, message, mine, theirs, where, terms, local],
        scratch=sums,
        name="assess_first",
    )
    args = [second, trade(second, 1), rim, trade(rim, 1), message, mine, theirs, low, high, where, terms, local]
    sends = call(
        make_send_second(pairs, rows, parts, tiles, cells, share),
        [((rows, cells + CYCLES * extra), BF16)] * pairs,
        [*args, *notes, *kept],
        scratch=sums,
        name="send_second",
    )
    got = exchange(sends)
    return tuple(
        call(
            make_last(pairs, rows, parts, tiles, cells),
            [(state.shape, BF16), ((CYCLES, tiles, share), F32)],
            [keys, *got],
            name="finish",
        )
    )


def solution(mesh):
    in_specs = (
        P("member", "region", None),
        P("region", None),
        P(None, "member", "region", None),
        P(None, "region", None),
        P("region", None),
        P("region"),
        P("region", None),
        P("region", None),
        P("region", None),
        P(None, "region", "member", None, None),
        P(None, "region", "member", None),
    )
    out_specs = (P("member", "region", None), P(None, "region", "member"))
    return jax.shard_map(body, mesh=mesh, in_specs=in_specs, out_specs=out_specs, check_vma=False)
```

```python
import jax
import jax.numpy as jnp
from jax import lax
from jax.experimental import pallas as pl
from jax.experimental.pallas import tpu as pltpu
from jax.sharding import PartitionSpec as P

CYCLES = 2
STEPS = 2
LANES = 128
F32 = jnp.float32
BF16 = jnp.bfloat16
I32 = jnp.int32
PARAMS = pltpu.CompilerParams(vmem_limit_bytes=48 * 1024 * 1024)


def iota(shape, dim):
    return lax.broadcasted_iota(I32, shape, dim)


def whole_spec(shape):
    zeros = (0,) * len(shape)
    return pl.BlockSpec(shape, lambda i: zeros)


def call(kernel, outs, args, specs=None, scratch=(), name=None):
    specs = specs or [whole_spec(a.shape) for a in args]
    return pl.pallas_call(
        kernel,
        out_shape=[jax.ShapeDtypeStruct(s, d) for s, d in outs],
        grid=(1,),
        in_specs=specs,
        out_specs=[whole_spec(s) for s, _ in outs],
        scratch_shapes=[pltpu.VMEM(s, d) for s, d in scratch],
        compiler_params=PARAMS,
        name=name,
    )(*args)


def column_of(row):
    n = row.shape[1]
    square = jnp.broadcast_to(row, (n, n))
    return jnp.sum(jnp.where(iota((n, n), 0) == iota((n, n), 1), square, 0), axis=1, keepdims=True)


def here():
    return lax.axis_index("member")


EDGE_AT = 32
STRIDE = 8


def apart(i, half, pairs):
    if pairs < 4:
        return i
    if isinstance(i, int) and isinstance(half, int):
        return 3 - i if half == 1 and i in (1, 2) else i
    return jnp.where((half == 1) & ((i == 1) | (i == 2)), 3 - i, i)


def padded(pairs):
    return max(8, pairs)


def make_prepare(members, capacity, parts, tiles):
    width = 2 * STEPS
    pairs = members // 2
    rows = parts * tiles

    def kernel(st0, st1, df0, df1, pb0, pb1, am, slot, *outs):
        notes, trail, keys = outs[:pairs], outs[pairs], outs[pairs + 1]
        m = here()
        lane = iota((1, LANES), 1)
        last = tiles - 1
        trail[...] = jnp.zeros(trail.shape, F32)
        trail[0:1, :] = df1[last:last + 1, :]
        trail[1:2, :] = df0[0:1, :]
        edge = jnp.zeros((1, LANES), F32)
        for p in range(parts):
            for i, t in enumerate((last, 0)):
                source = am[0, p:p + 1, t:t + 1] ^ m
                half = source % 2
                index = apart(source // 2, (m % 2) ^ half, pairs)
                code = (slot[0, p:p + 1, t:t + 1] * 2 + half) * padded(pairs) + index
                row = 2 + i * parts + p
                trail[row:row + 1, :] = jnp.broadcast_to(code.astype(F32), (1, LANES))
            fields = (st1[p, last:last + 1, :], st0[p, 0:1, :], pb1[0, p, last:last + 1, :], pb0[0, p, 0:1, :])
            for i, x in enumerate(fields):
                to = EDGE_AT + STRIDE * (4 * p + i)
                start = 0 if i % 2 else LANES - width
                moved = pltpu.roll(x.astype(F32), (to - start) % LANES, 1)
                edge = jnp.where((lane >= to) & (lane < to + width), moved, edge)
        before = (iota((tiles, tiles), 0) < iota((tiles, tiles), 1)).astype(F32)
        asked = jnp.zeros((pairs, LANES), F32)
        for c in range(CYCLES):
            seen = jnp.zeros((members, 1), F32)
            for p in range(parts):
                source = am[c, p:p + 1, :] ^ m
                named = (iota((members, tiles), 0) == source).astype(F32)
                earlier = seen + jnp.dot(named, before, preferred_element_type=F32)
                rank = jnp.sum(named * earlier, axis=0, keepdims=True).astype(I32)
                seen = seen + jnp.sum(named, axis=1, keepdims=True)
                half = source % 2
                code = half * rows + slot[c, p:p + 1, :] * tiles + iota((1, tiles), 1)
                spot = (iota((LANES, tiles), 0) == (2 * c + half) * capacity + rank).astype(F32)
                index = apart(source // 2, m % 2, pairs)
                pair = jnp.where(iota((pairs, tiles), 0) == index, (code + 1).astype(F32), 0.0)
                asked = asked + lax.dot_general(pair, spot, (((1,), (1,)), ((), ())), preferred_element_type=F32)
                column = column_of((2 * index + half) * capacity + rank)
                keys[c, p * tiles:(p + 1) * tiles, :] = jnp.broadcast_to(column, (tiles, LANES))
        for k in range(pairs):
            notes[k][...] = jnp.where(lane < EDGE_AT, asked[k:k + 1, :] - 1.0, edge)

    return kernel


def halves(mine, theirs):
    half = theirs.shape[0] // 2
    theirs = jnp.concatenate([theirs[half:, :], theirs[:half, :]], axis=0)
    first = jnp.broadcast_to(here() % 2, mine.shape) == 0
    return jnp.where(first, mine, theirs), jnp.where(first, theirs, mine)


def edge_windows(own, below, above, size, parts):
    width = 2 * STEPS

    def field(note, p, i):
        at = EDGE_AT + STRIDE * (4 * p + i)
        start = 0 if i % 2 else LANES - width
        both = jnp.concatenate([note[:size, :], note[size + 8:2 * size + 8, :]], axis=0)
        return pltpu.roll(both, (start - at) % LANES, 1)

    low, high = [], []
    for out, before, after in ((low, below, own), (high, own, above)):
        d = jnp.concatenate([before[size:size + 1, :], after[size + 1:size + 2, :]], axis=1)
        for p in range(parts):
            x = jnp.concatenate([field(before, p, 0), field(after, p, 1)], axis=1)
            x = diffuse(x, d) + jnp.concatenate([field(before, p, 2), field(after, p, 3)], axis=1)
            out.append(x.astype(BF16).astype(F32))
    return jnp.concatenate(low, axis=0), jnp.concatenate(high, axis=0)


def patch(x, first, last):
    tiles = x.shape[0]
    row, lane = iota((tiles, LANES), 0), iota((tiles, LANES), 1)
    head = jnp.where((row == 0) & (lane < STEPS), first, x[:, :LANES])
    tail = jnp.where((row == tiles - 1) & (lane >= LANES - STEPS), last, x[:, -LANES:])
    return jnp.concatenate([head, x[:, LANES:-LANES], tail], axis=1)


def widen(x, left, right):
    tiles = x.shape[0]
    row = iota((tiles, LANES), 0)
    before = jnp.where(row == 0, left, pltpu.roll(x[:, -LANES:], 1, 0))
    after = jnp.where(row == tiles - 1, right, pltpu.roll(x[:, :LANES], tiles - 1, 0))
    return jnp.concatenate([before, x, after], axis=1)


def diffuse(x, d):
    n = x.shape[1]
    for _ in range(STEPS):
        x = x + d * (pltpu.roll(x, 1, 1) - 2.0 * x + pltpu.roll(x, n - 1, 1))
    return x


def pick_rows(wanted, rows):
    m = rows.shape[0]
    n = wanted.shape[0]
    choice = (wanted[:, :m] == iota((n, m), 1)).astype(F32).astype(BF16)
    return jnp.dot(choice, rows, preferred_element_type=F32)


def requested(notes, prior, cycle, rows):
    pairs = len(notes)
    total = pairs * rows
    asked = jnp.concatenate(notes, axis=0)
    spread = jnp.broadcast_to(asked[:, None, :], (pairs, rows, LANES)).reshape(total, LANES)
    mine = iota((total, LANES), 1) == cycle * rows + iota((total, LANES), 0) % rows
    wanted = jnp.sum(jnp.where(mine, spread, 0.0), axis=1, keepdims=True).astype(I32)
    return pick_rows(jnp.broadcast_to(wanted, (total, LANES)), prior)


def make_observe(blocks, per_block, tiles, near):
    count = blocks * per_block

    def kernel(tile, cell, prec, value, pattern, weight, where, terms, local):
        def line(x):
            wide = jnp.concatenate([x] * per_block, axis=1)
            own = iota((per_block, count), 1) // blocks == iota((per_block, count), 0)
            return jnp.sum(jnp.where(own, wide, 0), axis=0, keepdims=True)

        at = line(cell[...])
        row = (at // LANES) * tiles + jnp.concatenate([tile[...]] * per_block, axis=1)
        pick = iota((2, count), 0) == 0
        where[...] = jnp.where(pick, row, at % LANES)
        terms[0:1, :] = line(prec[...])
        for c in range(CYCLES):
            terms[c + 1:c + 2, :] = line(value[c])
        group = iota((tiles, count), 1) % blocks
        total = jnp.zeros((tiles, count), F32)
        for k in range(near):
            total = total + jnp.where(column_of(pattern[k:k + 1, :]) == group, column_of(weight[k:k + 1, :]), 0.0)
        local[...] = total

    return kernel


def assess(prior, where, prec, value, local, parts, tiles, cells):
    blocks = cells // LANES
    rows = tiles * blocks
    count = where.shape[1]
    stacked = jnp.concatenate(
        [jnp.concatenate([x[:, k * LANES:(k + 1) * LANES] for k in range(blocks)], axis=0) for x in prior],
        axis=1,
    )
    choice = (iota((rows, count), 0) == where[0:1, :]).astype(F32).astype(BF16)
    lines = lax.dot_general(stacked, choice, (((0,), (0,)), ((), ())), preferred_element_type=F32)
    lane = iota((LANES, count), 0) == where[1:2, :]
    score = []
    for p in range(parts):
        predicted = jnp.sum(jnp.where(lane, lines[p * LANES:(p + 1) * LANES, :], 0.0), axis=0, keepdims=True)
        miss = value - predicted
        term = 0.5 * (prec * miss * miss)
        score.append(jnp.sum(local * term, axis=1, keepdims=True))
    least = score[0]
    for s in score[1:]:
        least = jnp.minimum(least, s)
    scale = [jnp.exp(least - s) for s in score]
    total = scale[0]
    for s in scale[1:]:
        total = total + s
    weighted = scale[0] * prior[0].astype(F32)
    for s, x in zip(scale[1:], prior[1:]):
        weighted = weighted + s * x.astype(F32)
    return least, total, weighted


def pieces(x):
    high = x.astype(BF16).astype(F32)
    middle = (x - high).astype(BF16).astype(F32)
    low = (x - high - middle).astype(BF16).astype(F32)
    return high, middle, low


def share_of(ref, member, share):
    if share % LANES == 0:
        return ref[:, pl.ds(pl.multiple_of(member * share, LANES), share)]
    return pltpu.roll(ref[...], ref.shape[1] - member * share, 1)[:, :share]


def pack_mean(outs, at, least, total, sums, share):
    rows = outs[0].shape[0]
    tiles = sums.shape[0]
    groups = tiles // rows
    m = here()
    lane = iota((rows, LANES), 1)
    misc = jnp.zeros((rows, LANES), F32)
    spot = 0
    for x in (least, total):
        for piece in pieces(x):
            for g in range(groups):
                misc = jnp.where(lane == spot, piece[g * rows:(g + 1) * rows, :], misc)
                spot += 1
    end = at + groups * share
    for k, out in enumerate(outs):
        block = share_of(sums, m ^ (2 * apart(k, m % 2, len(outs))), share)
        for g in range(groups):
            out[:, at + g * share:at + (g + 1) * share] = block[g * rows:(g + 1) * rows, :].astype(BF16)
        out[:, end:end + LANES] = misc.astype(BF16)


def unpack_mean(got, at, tiles, share):
    rows = got[0].shape[0]
    groups = tiles // rows
    end = at + groups * share
    misc = [x[:, end:end + LANES].astype(F32) for x in got]
    means = []
    for g in range(groups):
        stats = []
        for x in misc:
            pair = []
            for kind in range(2):
                spot = [(kind * 3 + piece) * groups + g for piece in range(3)]
                high, middle, low = [x[:, i:i + 1] for i in spot]
                pair.append(high + middle + low)
            stats.append(pair)
        lowest = stats[0][0]
        for least, _ in stats[1:]:
            lowest = jnp.minimum(lowest, least)
        top, bottom = 0.0, 0.0
        for x, (least, total) in zip(got, stats):
            scale = jnp.exp(lowest - least)
            top = top + scale * x[:, at + g * share:at + (g + 1) * share].astype(F32)
            bottom = bottom + scale * total
        means.append(top / bottom)
    return means


def make_first(parts, tiles, cells):
    def kernel(state, diff, pert, after, prior):
        nothing = jnp.zeros((1, LANES), F32)
        d = widen(diff[...], nothing, nothing)
        for p in range(parts):
            x = diffuse(widen(state[p].astype(F32), nothing, nothing), d)
            now = x[:, LANES:LANES + cells] + pert[0, p].astype(F32)
            prior[p * tiles:(p + 1) * tiles, :] = now.astype(BF16)

    return kernel


def make_send(pairs, rows):
    def kernel(own, other, trail, *refs):
        notes, sends, half = refs[:pairs], refs[pairs:2 * pairs], refs[2 * pairs]
        prior = jnp.concatenate([own[...], other[...]], axis=0)
        sent = requested([x[...] for x in notes], prior, 0, rows)
        for k in range(pairs):
            sends[k][...] = sent[k * rows:(k + 1) * rows, :].astype(BF16)
        size = padded(pairs)
        half[...] = jnp.zeros(half.shape, F32)
        for k in range(pairs):
            half[k:k + 1, :] = notes[k][...]
        half[size:, :] = trail[...]

    return kernel


def make_assess(pairs, parts, tiles, cells, share):
    size = padded(pairs)

    def kernel(own, other, low, high, where, terms, local, *refs):
        outs, sums = refs[:pairs], refs[pairs]
        fixed = []
        for h, prior in enumerate((own, other)):
            for p in range(parts):
                row = (2 * p + h) * size
                x = prior[p * tiles:(p + 1) * tiles, :].astype(F32)
                x = patch(x, low[row:row + 1, LANES:], high[row:row + 1, :LANES])
                fixed.append(x.astype(BF16))
        least, total, weighted = assess(
            fixed, where[...], terms[0:1, :], terms[1:2, :], local[...], 2 * parts, tiles, cells
        )
        sums[...] = weighted
        pack_mean(outs, 0, least, total, sums, share)

    return kernel


def make_second(pairs, parts, tiles, cells):
    size = padded(pairs)

    def kernel(keys, diff, pert, message, mine, theirs, after, *refs):
        got, prior, low_out, high_out = refs[:pairs], refs[pairs], refs[pairs + 1], refs[pairs + 2]
        below, above = halves(mine[...], theirs[...])
        low, high = edge_windows(message[...], below, above, size, parts)
        low_out[...] = low
        high_out[...] = high
        below, above = below[size:size + 8, :], above[size:size + 8, :]
        arrived = jnp.concatenate([x[...] for x in got], axis=0)
        moved = pick_rows(keys[0], arrived)
        here_codes = message[size + 2:size + 2 + 2 * parts, :].astype(I32)
        codes = jnp.concatenate([here_codes[parts:], below[2:2 + parts, :].astype(I32)], axis=0)
        start = pick_rows(codes, low.astype(BF16))
        codes = jnp.concatenate([here_codes[:parts], above[2 + parts:2 + 2 * parts, :].astype(I32)], axis=0)
        end = pick_rows(codes, high.astype(BF16))
        d = widen(diff[...], below[0:1, :], above[1:2, :])
        for p in range(parts):
            x = patch(moved[p * tiles:(p + 1) * tiles, :], start[p:p + 1, LANES:], end[p:p + 1, :LANES])
            q = parts + p
            x = widen(x, start[q:q + 1, :LANES], end[q:q + 1, LANES:])
            x = diffuse(x, d)[:, LANES:LANES + cells]
            prior[p * tiles:(p + 1) * tiles, :] = (x + pert[0, p].astype(F32)).astype(BF16)

    return kernel


def make_send_second(pairs, rows, parts, tiles, cells, share):
    def kernel(own, other, where, terms, local, *refs):
        notes, kept, outs, sums = refs[:pairs], refs[pairs:2 * pairs], refs[2 * pairs:3 * pairs], refs[3 * pairs]
        prior = jnp.concatenate([own[...], other[...]], axis=0)
        sent = requested([x[...] for x in notes], prior, 1, rows)
        extra = kept[0].shape[1]
        for k in range(pairs):
            outs[k][:, :cells] = sent[k * rows:(k + 1) * rows, :].astype(BF16)
            outs[k][:, cells:cells + extra] = kept[k][...]
        least, total, weighted = assess(
            [x[p * tiles:(p + 1) * tiles, :] for x in (own, other) for p in range(parts)],
            where[...], terms[0:1, :], terms[2:3, :], local[...], 2 * parts, tiles, cells,
        )
        sums[...] = weighted
        pack_mean(outs, cells + extra, least, total, sums, share)

    return kernel


def make_last(pairs, rows, parts, tiles, cells):
    def kernel(keys, *refs):
        got, analysis, mean = refs[:pairs], refs[pairs], refs[pairs + 1]
        arrived = jnp.concatenate([x[:, :cells] for x in got], axis=0)
        picked = pick_rows(keys[1], arrived)
        for p in range(parts):
            analysis[p] = picked[p * tiles:(p + 1) * tiles, :].astype(BF16)
        share = mean.shape[2]
        extra = tiles // rows * share + LANES
        for c in range(CYCLES):
            for g, x in enumerate(unpack_mean(got, cells + c * extra, tiles, share)):
                mean[c, g * rows:(g + 1) * rows, :] = x

    return kernel


def body(
    state,
    diffusivity,
    model_perturbation,
    obs_values,
    obs_prec,
    obs_tile,
    obs_cell,
    pattern,
    loc_weight,
    anc_member,
    anc_slot,
):
    parts, tiles, cells = state.shape
    members = lax.axis_size("member")
    regions = lax.axis_size("region")
    capacity = max(2, 2 * parts * tiles // members)
    share = cells // members
    pairs = members // 2
    rows = 2 * capacity
    extra = tiles // rows * share + LANES
    blocks, per_block = obs_cell.shape
    count = blocks * per_block
    member_of = anc_member.reshape(CYCLES, parts, tiles)
    slot_of = anc_slot.reshape(CYCLES, parts, tiles)
    near = pattern.shape[1]
    ends = cells // LANES - 1

    def block(shape, at):
        lead = (0,) * (len(shape) - 1)
        return pl.BlockSpec(shape, lambda i: lead + (at,))

    edges = [state, state, diffusivity, diffusivity, model_perturbation, model_perturbation, member_of, slot_of]
    *notes, trail, keys = call(
        make_prepare(members, capacity, parts, tiles),
        [((1, LANES), F32)] * pairs + [((8, LANES), F32), ((CYCLES, parts * tiles, LANES), I32)],
        [pltpu.with_memory_space_constraint(x, pltpu.HBM) for x in edges],
        [
            block((parts, tiles, LANES), 0),
            block((parts, tiles, LANES), ends),
            block((tiles, LANES), 0),
            block((tiles, LANES), ends),
            block((1, parts, tiles, LANES), 0),
            block((1, parts, tiles, LANES), ends),
            whole_spec(member_of.shape),
            whole_spec(slot_of.shape),
        ],
        name="prepare",
    )

    def trade(x):
        return lax.ppermute(x, "member", [(i, i ^ 1) for i in range(members)])

    def exchange(sends):
        got = [sends[0]]
        for k in range(1, pairs):
            steps = [(i, i ^ (2 * apart(k, i % 2, pairs))) for i in range(members)]
            got.append(lax.ppermute(sends[k], "member", steps))
        return got

    notes = exchange(notes)

    where, terms, local = call(
        make_observe(blocks, per_block, tiles, near),
        [((2, count), I32), ((1 + CYCLES, count), F32), ((tiles, count), F32)],
        [obs_tile[None, :], obs_cell.T, obs_prec.T, jnp.swapaxes(obs_values, 1, 2), pattern.T, loc_weight.T],
        name="observe",
    )

    def noise_spec(c):
        return pl.BlockSpec((1, parts, tiles, cells), lambda i: (c, 0, 0, 0))

    args = [state, diffusivity, model_perturbation, trail]
    specs = [whole_spec(a.shape) for a in args]
    specs[2] = noise_spec(0)
    (prior,) = call(
        make_first(parts, tiles, cells), [((parts * tiles, cells), BF16)], args, specs, name="forecast_first"
    )
    other = trade(prior)
    size = padded(pairs)
    *sends, half = call(
        make_send(pairs, rows),
        [((rows, cells), BF16)] * pairs + [((size + trail.shape[0], LANES), F32)],
        [prior, other, trail, *notes],
        name="send_first",
    )
    got = exchange(sends)
    message = jnp.concatenate([half, trade(half)], axis=0)
    steps = []
    for i in range(members):
        first, last = (0, regions - 1) if i % 2 == 0 else (1, regions)
        steps += [(i * regions + r, i * regions + r + 1 - 2 * (i % 2)) for r in range(first, last)]
    mine = lax.ppermute(message, ("member", "region"), steps)
    theirs = trade(mine)
    window = ((parts * 2 * size, 2 * LANES), F32)
    sums = [((tiles, cells), F32)]
    args = [keys, diffusivity, model_perturbation, message, mine, theirs, where, *got]
    specs = [whole_spec(a.shape) for a in args]
    specs[2] = noise_spec(1)
    second, low, high = call(
        make_second(pairs, parts, tiles, cells),
        [((parts * tiles, cells), BF16), window, window],
        args,
        specs,
        name="forecast_second",
    )
    kept = call(
        make_assess(pairs, parts, tiles, cells, share),
        [((rows, extra), BF16)] * pairs,
        [prior, other, low, high, where, terms, local],
        scratch=sums,
        name="assess_first",
    )
    sends = call(
        make_send_second(pairs, rows, parts, tiles, cells, share),
        [((rows, cells + CYCLES * extra), BF16)] * pairs,
        [second, trade(second), where, terms, local, *notes, *kept],
        scratch=sums,
        name="send_second",
    )
    got = exchange(sends)
    return tuple(
        call(
            make_last(pairs, rows, parts, tiles, cells),
            [(state.shape, BF16), ((CYCLES, tiles, share), F32)],
            [keys, *got],
            name="finish",
        )
    )


def solution(mesh):
    in_specs = (
        P("member", "region", None),
        P("region", None),
        P(None, "member", "region", None),
        P(None, "region", None),
        P("region", None),
        P("region"),
        P("region", None),
        P("region", None),
        P("region", None),
        P(None, "region", "member", None, None),
        P(None, "region", "member", None),
    )
    out_specs = (P("member", "region", None), P(None, "region", "member"))
    return jax.shard_map(body, mesh=mesh, in_specs=in_specs, out_specs=out_specs, check_vma=False)
```

```python
import jax
import jax.numpy as jnp
from jax import lax
from jax.experimental import pallas as pl
from jax.experimental.pallas import tpu as pltpu
from jax.sharding import PartitionSpec as P

CYCLES = 2
STEPS = 2
LANES = 128
F32 = jnp.float32
BF16 = jnp.bfloat16
I32 = jnp.int32
PARAMS = pltpu.CompilerParams(vmem_limit_bytes=48 * 1024 * 1024)


def iota(shape, dim):
    return lax.broadcasted_iota(I32, shape, dim)


def whole_spec(shape):
    zeros = (0,) * len(shape)
    return pl.BlockSpec(shape, lambda i: zeros)


def call(kernel, outs, args, specs=None, scratch=(), name=None):
    specs = specs or [whole_spec(a.shape) for a in args]
    return pl.pallas_call(
        kernel,
        out_shape=[jax.ShapeDtypeStruct(s, d) for s, d in outs],
        grid=(1,),
        in_specs=specs,
        out_specs=[whole_spec(s) for s, _ in outs],
        scratch_shapes=[pltpu.VMEM(s, d) for s, d in scratch],
        compiler_params=PARAMS,
        name=name,
    )(*args)


def column_of(row):
    n = row.shape[1]
    square = jnp.broadcast_to(row, (n, n))
    return jnp.sum(jnp.where(iota((n, n), 0) == iota((n, n), 1), square, 0), axis=1, keepdims=True)


def here():
    return lax.axis_index("member")


EDGE_AT = 32
STRIDE = 8


def padded(pairs):
    return max(8, pairs)


def make_prepare(members, capacity, parts, tiles):
    width = 2 * STEPS
    pairs = members // 2
    rows = parts * tiles

    def kernel(st0, st1, df0, df1, pb0, pb1, am, slot, *outs):
        notes, trail, keys = outs[:pairs], outs[pairs], outs[pairs + 1]
        m = here()
        lane = iota((1, LANES), 1)
        last = tiles - 1
        trail[...] = jnp.zeros(trail.shape, F32)
        trail[0:1, :] = df1[last:last + 1, :]
        trail[1:2, :] = df0[0:1, :]
        edge = jnp.zeros((1, LANES), F32)
        for p in range(parts):
            for i, t in enumerate((last, 0)):
                source = am[0, p:p + 1, t:t + 1] ^ m
                code = (slot[0, p:p + 1, t:t + 1] * 2 + source % 2) * padded(pairs) + source // 2
                row = 2 + i * parts + p
                trail[row:row + 1, :] = jnp.broadcast_to(code.astype(F32), (1, LANES))
            fields = (st1[p, last:last + 1, :], st0[p, 0:1, :], pb1[0, p, last:last + 1, :], pb0[0, p, 0:1, :])
            for i, x in enumerate(fields):
                to = EDGE_AT + STRIDE * (4 * p + i)
                start = 0 if i % 2 else LANES - width
                moved = pltpu.roll(x.astype(F32), (to - start) % LANES, 1)
                edge = jnp.where((lane >= to) & (lane < to + width), moved, edge)
        before = (iota((tiles, tiles), 0) < iota((tiles, tiles), 1)).astype(F32)
        asked = jnp.zeros((pairs, LANES), F32)
        for c in range(CYCLES):
            seen = jnp.zeros((members, 1), F32)
            for p in range(parts):
                source = am[c, p:p + 1, :] ^ m
                named = (iota((members, tiles), 0) == source).astype(F32)
                earlier = seen + jnp.dot(named, before, preferred_element_type=F32)
                rank = jnp.sum(named * earlier, axis=0, keepdims=True).astype(I32)
                seen = seen + jnp.sum(named, axis=1, keepdims=True)
                half = source % 2
                code = half * rows + slot[c, p:p + 1, :] * tiles + iota((1, tiles), 1)
                spot = (iota((LANES, tiles), 0) == (2 * c + half) * capacity + rank).astype(F32)
                pair = jnp.where(iota((pairs, tiles), 0) == source // 2, (code + 1).astype(F32), 0.0)
                asked = asked + lax.dot_general(pair, spot, (((1,), (1,)), ((), ())), preferred_element_type=F32)
                column = column_of(source * capacity + rank)
                keys[c, p * tiles:(p + 1) * tiles, :] = jnp.broadcast_to(column, (tiles, LANES))
        for k in range(pairs):
            notes[k][...] = jnp.where(lane < EDGE_AT, asked[k:k + 1, :] - 1.0, edge)

    return kernel


def halves(mine, theirs):
    half = theirs.shape[0] // 2
    theirs = jnp.concatenate([theirs[half:, :], theirs[:half, :]], axis=0)
    first = jnp.broadcast_to(here() % 2, mine.shape) == 0
    return jnp.where(first, mine, theirs), jnp.where(first, theirs, mine)


def edge_windows(own, below, above, size, parts):
    width = 2 * STEPS

    def field(note, p, i):
        at = EDGE_AT + STRIDE * (4 * p + i)
        start = 0 if i % 2 else LANES - width
        both = jnp.concatenate([note[:size, :], note[size + 8:2 * size + 8, :]], axis=0)
        return pltpu.roll(both, (start - at) % LANES, 1)

    low, high = [], []
    for out, before, after in ((low, below, own), (high, own, above)):
        d = jnp.concatenate([before[size:size + 1, :], after[size + 1:size + 2, :]], axis=1)
        for p in range(parts):
            x = jnp.concatenate([field(before, p, 0), field(after, p, 1)], axis=1)
            x = diffuse(x, d) + jnp.concatenate([field(before, p, 2), field(after, p, 3)], axis=1)
            out.append(x.astype(BF16).astype(F32))
    return jnp.concatenate(low, axis=0), jnp.concatenate(high, axis=0)


def patch(x, first, last):
    tiles = x.shape[0]
    row, lane = iota((tiles, LANES), 0), iota((tiles, LANES), 1)
    head = jnp.where((row == 0) & (lane < STEPS), first, x[:, :LANES])
    tail = jnp.where((row == tiles - 1) & (lane >= LANES - STEPS), last, x[:, -LANES:])
    return jnp.concatenate([head, x[:, LANES:-LANES], tail], axis=1)


def widen(x, left, right):
    tiles = x.shape[0]
    row = iota((tiles, LANES), 0)
    before = jnp.where(row == 0, left, pltpu.roll(x[:, -LANES:], 1, 0))
    after = jnp.where(row == tiles - 1, right, pltpu.roll(x[:, :LANES], tiles - 1, 0))
    return jnp.concatenate([before, x, after], axis=1)


def diffuse(x, d):
    n = x.shape[1]
    for _ in range(STEPS):
        x = x + d * (pltpu.roll(x, 1, 1) - 2.0 * x + pltpu.roll(x, n - 1, 1))
    return x


def pick_rows(wanted, rows):
    m = rows.shape[0]
    n = wanted.shape[0]
    choice = (wanted[:, :m] == iota((n, m), 1)).astype(F32).astype(BF16)
    return jnp.dot(choice, rows, preferred_element_type=F32)


def requested(notes, prior, cycle, rows):
    pairs = len(notes)
    total = pairs * rows
    asked = jnp.concatenate(notes, axis=0)
    spread = jnp.broadcast_to(asked[:, None, :], (pairs, rows, LANES)).reshape(total, LANES)
    mine = iota((total, LANES), 1) == cycle * rows + iota((total, LANES), 0) % rows
    wanted = jnp.sum(jnp.where(mine, spread, 0.0), axis=1, keepdims=True).astype(I32)
    return pick_rows(jnp.broadcast_to(wanted, (total, LANES)), prior)


def make_observe(blocks, per_block, tiles, near):
    count = blocks * per_block

    def kernel(tile, cell, prec, value, pattern, weight, where, terms, local):
        def line(x):
            wide = jnp.concatenate([x] * per_block, axis=1)
            own = iota((per_block, count), 1) // blocks == iota((per_block, count), 0)
            return jnp.sum(jnp.where(own, wide, 0), axis=0, keepdims=True)

        at = line(cell[...])
        row = (at // LANES) * tiles + jnp.concatenate([tile[...]] * per_block, axis=1)
        pick = iota((2, count), 0) == 0
        where[...] = jnp.where(pick, row, at % LANES)
        terms[0:1, :] = line(prec[...])
        for c in range(CYCLES):
            terms[c + 1:c + 2, :] = line(value[c])
        group = iota((tiles, count), 1) % blocks
        total = jnp.zeros((tiles, count), F32)
        for k in range(near):
            total = total + jnp.where(column_of(pattern[k:k + 1, :]) == group, column_of(weight[k:k + 1, :]), 0.0)
        local[...] = total

    return kernel


def assess(prior, where, prec, value, local, parts, tiles, cells):
    blocks = cells // LANES
    rows = tiles * blocks
    count = where.shape[1]
    stacked = jnp.concatenate(
        [jnp.concatenate([x[:, k * LANES:(k + 1) * LANES] for k in range(blocks)], axis=0) for x in prior],
        axis=1,
    )
    choice = (iota((rows, count), 0) == where[0:1, :]).astype(F32).astype(BF16)
    lines = lax.dot_general(stacked, choice, (((0,), (0,)), ((), ())), preferred_element_type=F32)
    lane = iota((LANES, count), 0) == where[1:2, :]
    score = []
    for p in range(parts):
        predicted = jnp.sum(jnp.where(lane, lines[p * LANES:(p + 1) * LANES, :], 0.0), axis=0, keepdims=True)
        miss = value - predicted
        term = 0.5 * (prec * miss * miss)
        score.append(jnp.sum(local * term, axis=1, keepdims=True))
    least = score[0]
    for s in score[1:]:
        least = jnp.minimum(least, s)
    scale = [jnp.exp(least - s) for s in score]
    total = scale[0]
    for s in scale[1:]:
        total = total + s
    weighted = scale[0] * prior[0].astype(F32)
    for s, x in zip(scale[1:], prior[1:]):
        weighted = weighted + s * x.astype(F32)
    return least, total, weighted


def pieces(x):
    high = x.astype(BF16).astype(F32)
    middle = (x - high).astype(BF16).astype(F32)
    low = (x - high - middle).astype(BF16).astype(F32)
    return high, middle, low


def share_of(ref, member, share):
    if share % LANES == 0:
        return ref[:, pl.ds(pl.multiple_of(member * share, LANES), share)]
    return pltpu.roll(ref[...], ref.shape[1] - member * share, 1)[:, :share]


def pack_mean(outs, at, least, total, sums, share):
    rows = outs[0].shape[0]
    tiles = sums.shape[0]
    groups = tiles // rows
    m = here()
    lane = iota((rows, LANES), 1)
    misc = jnp.zeros((rows, LANES), F32)
    spot = 0
    for x in (least, total):
        for piece in pieces(x):
            for g in range(groups):
                misc = jnp.where(lane == spot, piece[g * rows:(g + 1) * rows, :], misc)
                spot += 1
    end = at + groups * share
    for k, out in enumerate(outs):
        block = share_of(sums, m ^ (2 * k), share)
        for g in range(groups):
            out[:, at + g * share:at + (g + 1) * share] = block[g * rows:(g + 1) * rows, :].astype(BF16)
        out[:, end:end + LANES] = misc.astype(BF16)


def unpack_mean(got, at, tiles, share):
    rows = got[0].shape[0]
    groups = tiles // rows
    end = at + groups * share
    misc = [x[:, end:end + LANES].astype(F32) for x in got]
    means = []
    for g in range(groups):
        stats = []
        for x in misc:
            pair = []
            for kind in range(2):
                spot = [(kind * 3 + piece) * groups + g for piece in range(3)]
                high, middle, low = [x[:, i:i + 1] for i in spot]
                pair.append(high + middle + low)
            stats.append(pair)
        lowest = stats[0][0]
        for least, _ in stats[1:]:
            lowest = jnp.minimum(lowest, least)
        top, bottom = 0.0, 0.0
        for x, (least, total) in zip(got, stats):
            scale = jnp.exp(lowest - least)
            top = top + scale * x[:, at + g * share:at + (g + 1) * share].astype(F32)
            bottom = bottom + scale * total
        means.append(top / bottom)
    return means


def make_first(parts, tiles, cells):
    def kernel(state, diff, pert, after, prior):
        nothing = jnp.zeros((1, LANES), F32)
        d = widen(diff[...], nothing, nothing)
        for p in range(parts):
            x = diffuse(widen(state[p].astype(F32), nothing, nothing), d)
            now = x[:, LANES:LANES + cells] + pert[0, p].astype(F32)
            prior[p * tiles:(p + 1) * tiles, :] = now.astype(BF16)

    return kernel


def make_send(pairs, rows):
    def kernel(own, other, trail, *refs):
        notes, sends, half = refs[:pairs], refs[pairs:2 * pairs], refs[2 * pairs]
        prior = jnp.concatenate([own[...], other[...]], axis=0)
        sent = requested([x[...] for x in notes], prior, 0, rows)
        for k in range(pairs):
            sends[k][...] = sent[k * rows:(k + 1) * rows, :].astype(BF16)
        size = padded(pairs)
        half[...] = jnp.zeros(half.shape, F32)
        for k in range(pairs):
            half[k:k + 1, :] = notes[k][...]
        half[size:, :] = trail[...]

    return kernel


def make_assess(pairs, parts, tiles, cells, share):
    size = padded(pairs)

    def kernel(own, other, low, high, where, terms, local, *refs):
        outs, sums = refs[:pairs], refs[pairs]
        fixed = []
        for h, prior in enumerate((own, other)):
            for p in range(parts):
                row = (2 * p + h) * size
                x = prior[p * tiles:(p + 1) * tiles, :].astype(F32)
                x = patch(x, low[row:row + 1, LANES:], high[row:row + 1, :LANES])
                fixed.append(x.astype(BF16))
        least, total, weighted = assess(
            fixed, where[...], terms[0:1, :], terms[1:2, :], local[...], 2 * parts, tiles, cells
        )
        sums[...] = weighted
        pack_mean(outs, 0, least, total, sums, share)

    return kernel


def make_second(pairs, parts, tiles, cells):
    size = padded(pairs)

    def kernel(keys, diff, pert, message, mine, theirs, after, *refs):
        got, prior, low_out, high_out = refs[:pairs], refs[pairs], refs[pairs + 1], refs[pairs + 2]
        below, above = halves(mine[...], theirs[...])
        low, high = edge_windows(message[...], below, above, size, parts)
        low_out[...] = low
        high_out[...] = high
        below, above = below[size:size + 8, :], above[size:size + 8, :]
        arrived = jnp.concatenate([x[...] for x in got], axis=0)
        moved = pick_rows(keys[0], arrived)
        here_codes = message[size + 2:size + 2 + 2 * parts, :].astype(I32)
        codes = jnp.concatenate([here_codes[parts:], below[2:2 + parts, :].astype(I32)], axis=0)
        start = pick_rows(codes, low.astype(BF16))
        codes = jnp.concatenate([here_codes[:parts], above[2 + parts:2 + 2 * parts, :].astype(I32)], axis=0)
        end = pick_rows(codes, high.astype(BF16))
        d = widen(diff[...], below[0:1, :], above[1:2, :])
        for p in range(parts):
            x = patch(moved[p * tiles:(p + 1) * tiles, :], start[p:p + 1, LANES:], end[p:p + 1, :LANES])
            q = parts + p
            x = widen(x, start[q:q + 1, :LANES], end[q:q + 1, LANES:])
            x = diffuse(x, d)[:, LANES:LANES + cells]
            prior[p * tiles:(p + 1) * tiles, :] = (x + pert[0, p].astype(F32)).astype(BF16)

    return kernel


def make_send_second(pairs, rows, parts, tiles, cells, share):
    def kernel(own, other, where, terms, local, *refs):
        notes, kept, outs, sums = refs[:pairs], refs[pairs:2 * pairs], refs[2 * pairs:3 * pairs], refs[3 * pairs]
        prior = jnp.concatenate([own[...], other[...]], axis=0)
        sent = requested([x[...] for x in notes], prior, 1, rows)
        extra = kept[0].shape[1]
        for k in range(pairs):
            outs[k][:, :cells] = sent[k * rows:(k + 1) * rows, :].astype(BF16)
            outs[k][:, cells:cells + extra] = kept[k][...]
        least, total, weighted = assess(
            [x[p * tiles:(p + 1) * tiles, :] for x in (own, other) for p in range(parts)],
            where[...], terms[0:1, :], terms[2:3, :], local[...], 2 * parts, tiles, cells,
        )
        sums[...] = weighted
        pack_mean(outs, cells + extra, least, total, sums, share)

    return kernel


def make_last(pairs, rows, parts, tiles, cells):
    def kernel(keys, *refs):
        got, analysis, mean = refs[:pairs], refs[pairs], refs[pairs + 1]
        arrived = jnp.concatenate([x[:, :cells] for x in got], axis=0)
        picked = pick_rows(keys[1], arrived)
        for p in range(parts):
            analysis[p] = picked[p * tiles:(p + 1) * tiles, :].astype(BF16)
        share = mean.shape[2]
        extra = tiles // rows * share + LANES
        for c in range(CYCLES):
            for g, x in enumerate(unpack_mean(got, cells + c * extra, tiles, share)):
                mean[c, g * rows:(g + 1) * rows, :] = x

    return kernel


def body(
    state,
    diffusivity,
    model_perturbation,
    obs_values,
    obs_prec,
    obs_tile,
    obs_cell,
    pattern,
    loc_weight,
    anc_member,
    anc_slot,
):
    parts, tiles, cells = state.shape
    members = lax.axis_size("member")
    regions = lax.axis_size("region")
    capacity = max(2, 2 * parts * tiles // members)
    share = cells // members
    pairs = members // 2
    rows = 2 * capacity
    extra = tiles // rows * share + LANES
    blocks, per_block = obs_cell.shape
    count = blocks * per_block
    member_of = anc_member.reshape(CYCLES, parts, tiles)
    slot_of = anc_slot.reshape(CYCLES, parts, tiles)
    near = pattern.shape[1]
    ends = cells // LANES - 1

    def block(shape, at):
        lead = (0,) * (len(shape) - 1)
        return pl.BlockSpec(shape, lambda i: lead + (at,))

    edges = [state, state, diffusivity, diffusivity, model_perturbation, model_perturbation, member_of, slot_of]
    *notes, trail, keys = call(
        make_prepare(members, capacity, parts, tiles),
        [((1, LANES), F32)] * pairs + [((8, LANES), F32), ((CYCLES, parts * tiles, LANES), I32)],
        [pltpu.with_memory_space_constraint(x, pltpu.HBM) for x in edges],
        [
            block((parts, tiles, LANES), 0),
            block((parts, tiles, LANES), ends),
            block((tiles, LANES), 0),
            block((tiles, LANES), ends),
            block((1, parts, tiles, LANES), 0),
            block((1, parts, tiles, LANES), ends),
            whole_spec(member_of.shape),
            whole_spec(slot_of.shape),
        ],
        name="prepare",
    )

    def trade(x):
        return lax.ppermute(x, "member", [(i, i ^ 1) for i in range(members)])

    def exchange(sends):
        got = [sends[0]]
        for k in range(1, pairs):
            got.append(lax.ppermute(sends[k], "member", [(i, i ^ (2 * k)) for i in range(members)]))
        return got

    notes = exchange(notes)

    where, terms, local = call(
        make_observe(blocks, per_block, tiles, near),
        [((2, count), I32), ((1 + CYCLES, count), F32), ((tiles, count), F32)],
        [obs_tile[None, :], obs_cell.T, obs_prec.T, jnp.swapaxes(obs_values, 1, 2), pattern.T, loc_weight.T],
        name="observe",
    )

    def noise_spec(c):
        return pl.BlockSpec((1, parts, tiles, cells), lambda i: (c, 0, 0, 0))

    args = [state, diffusivity, model_perturbation, trail]
    specs = [whole_spec(a.shape) for a in args]
    specs[2] = noise_spec(0)
    (prior,) = call(
        make_first(parts, tiles, cells), [((parts * tiles, cells), BF16)], args, specs, name="forecast_first"
    )
    other = trade(prior)
    size = padded(pairs)
    *sends, half = call(
        make_send(pairs, rows),
        [((rows, cells), BF16)] * pairs + [((size + trail.shape[0], LANES), F32)],
        [prior, other, trail, *notes],
        name="send_first",
    )
    got = exchange(sends)
    message = jnp.concatenate([half, trade(half)], axis=0)
    steps = []
    for i in range(members):
        first, last = (0, regions - 1) if i % 2 == 0 else (1, regions)
        steps += [(i * regions + r, i * regions + r + 1 - 2 * (i % 2)) for r in range(first, last)]
    mine = lax.ppermute(message, ("member", "region"), steps)
    theirs = trade(mine)
    window = ((parts * 2 * size, 2 * LANES), F32)
    sums = [((tiles, cells), F32)]
    args = [keys, diffusivity, model_perturbation, message, mine, theirs, where, *got]
    specs = [whole_spec(a.shape) for a in args]
    specs[2] = noise_spec(1)
    second, low, high = call(
        make_second(pairs, parts, tiles, cells),
        [((parts * tiles, cells), BF16), window, window],
        args,
        specs,
        name="forecast_second",
    )
    kept = call(
        make_assess(pairs, parts, tiles, cells, share),
        [((rows, extra), BF16)] * pairs,
        [prior, other, low, high, where, terms, local],
        scratch=sums,
        name="assess_first",
    )
    sends = call(
        make_send_second(pairs, rows, parts, tiles, cells, share),
        [((rows, cells + CYCLES * extra), BF16)] * pairs,
        [second, trade(second), where, terms, local, *notes, *kept],
        scratch=sums,
        name="send_second",
    )
    got = exchange(sends)
    return tuple(
        call(
            make_last(pairs, rows, parts, tiles, cells),
            [(state.shape, BF16), ((CYCLES, tiles, share), F32)],
            [keys, *got],
            name="finish",
        )
    )


def solution(mesh):
    in_specs = (
        P("member", "region", None),
        P("region", None),
        P(None, "member", "region", None),
        P(None, "region", None),
        P("region", None),
        P("region"),
        P("region", None),
        P("region", None),
        P("region", None),
        P(None, "region", "member", None, None),
        P(None, "region", "member", None),
    )
    out_specs = (P("member", "region", None), P(None, "region", "member"))
    return jax.shard_map(body, mesh=mesh, in_specs=in_specs, out_specs=out_specs, check_vma=False)
```

```python
import jax
import jax.numpy as jnp
from jax import lax
from jax.experimental import pallas as pl
from jax.experimental.pallas import tpu as pltpu
from jax.sharding import PartitionSpec as P

CYCLES = 2
STEPS = 2
LANES = 128
F32 = jnp.float32
BF16 = jnp.bfloat16
I32 = jnp.int32
PARAMS = pltpu.CompilerParams(vmem_limit_bytes=48 * 1024 * 1024)


def iota(shape, dim):
    return lax.broadcasted_iota(I32, shape, dim)


def whole_spec(shape):
    zeros = (0,) * len(shape)
    return pl.BlockSpec(shape, lambda i: zeros)


def call(kernel, outs, args, specs=None, scratch=(), name=None):
    specs = specs or [whole_spec(a.shape) for a in args]
    return pl.pallas_call(
        kernel,
        out_shape=[jax.ShapeDtypeStruct(s, d) for s, d in outs],
        grid=(1,),
        in_specs=specs,
        out_specs=[whole_spec(s) for s, _ in outs],
        scratch_shapes=[pltpu.VMEM(s, d) for s, d in scratch],
        compiler_params=PARAMS,
        name=name,
    )(*args)


def column_of(row):
    n = row.shape[1]
    square = jnp.broadcast_to(row, (n, n))
    return jnp.sum(jnp.where(iota((n, n), 0) == iota((n, n), 1), square, 0), axis=1, keepdims=True)


def here():
    return lax.axis_index("member")


EDGE_AT = 32
STRIDE = 8


def padded(pairs):
    return max(8, pairs)


def make_prepare(members, capacity, parts, tiles):
    width = 2 * STEPS
    pairs = members // 2
    rows = parts * tiles

    def kernel(st0, st1, df0, df1, pb0, pb1, am, slot, *outs):
        notes, trail, keys = outs[:pairs], outs[pairs], outs[pairs + 1]
        m = here()
        lane = iota((1, LANES), 1)
        last = tiles - 1
        trail[...] = jnp.zeros(trail.shape, F32)
        trail[0:1, :] = df1[last:last + 1, :]
        trail[1:2, :] = df0[0:1, :]
        edge = jnp.zeros((1, LANES), F32)
        for p in range(parts):
            for i, t in enumerate((last, 0)):
                source = am[0, p:p + 1, t:t + 1] ^ m
                code = (slot[0, p:p + 1, t:t + 1] * 2 + source % 2) * padded(pairs) + source // 2
                row = 2 + i * parts + p
                trail[row:row + 1, :] = jnp.broadcast_to(code.astype(F32), (1, LANES))
            fields = (st1[p, last:last + 1, :], st0[p, 0:1, :], pb1[0, p, last:last + 1, :], pb0[0, p, 0:1, :])
            for i, x in enumerate(fields):
                to = EDGE_AT + STRIDE * (4 * p + i)
                start = 0 if i % 2 else LANES - width
                moved = pltpu.roll(x.astype(F32), (to - start) % LANES, 1)
                edge = jnp.where((lane >= to) & (lane < to + width), moved, edge)
        before = (iota((tiles, tiles), 0) < iota((tiles, tiles), 1)).astype(F32)
        asked = jnp.zeros((pairs, LANES), F32)
        for c in range(CYCLES):
            seen = jnp.zeros((members, 1), F32)
            for p in range(parts):
                source = am[c, p:p + 1, :] ^ m
                named = (iota((members, tiles), 0) == source).astype(F32)
                earlier = seen + jnp.dot(named, before, preferred_element_type=F32)
                rank = jnp.sum(named * earlier, axis=0, keepdims=True).astype(I32)
                seen = seen + jnp.sum(named, axis=1, keepdims=True)
                half = source % 2
                code = half * rows + slot[c, p:p + 1, :] * tiles + iota((1, tiles), 1)
                spot = (iota((LANES, tiles), 0) == (2 * c + half) * capacity + rank).astype(F32)
                pair = jnp.where(iota((pairs, tiles), 0) == source // 2, (code + 1).astype(F32), 0.0)
                asked = asked + lax.dot_general(pair, spot, (((1,), (1,)), ((), ())), preferred_element_type=F32)
                column = column_of((source ^ (m // 2 * 2)) * capacity + rank)
                keys[c, p * tiles:(p + 1) * tiles, :] = jnp.broadcast_to(column, (tiles, LANES))
        for k in range(pairs):
            notes[k][...] = jnp.where(lane < EDGE_AT, asked[k:k + 1, :] - 1.0, edge)

    return kernel


def halves(mine, theirs):
    half = theirs.shape[0] // 2
    theirs = jnp.concatenate([theirs[half:, :], theirs[:half, :]], axis=0)
    first = jnp.broadcast_to(here() % 2, mine.shape) == 0
    return jnp.where(first, mine, theirs), jnp.where(first, theirs, mine)


def edge_windows(own, below, above, size, parts):
    width = 2 * STEPS

    def field(note, p, i):
        at = EDGE_AT + STRIDE * (4 * p + i)
        start = 0 if i % 2 else LANES - width
        both = jnp.concatenate([note[:size, :], note[size + 8:2 * size + 8, :]], axis=0)
        return pltpu.roll(both, (start - at) % LANES, 1)

    low, high = [], []
    for out, before, after in ((low, below, own), (high, own, above)):
        d = jnp.concatenate([before[size:size + 1, :], after[size + 1:size + 2, :]], axis=1)
        for p in range(parts):
            x = jnp.concatenate([field(before, p, 0), field(after, p, 1)], axis=1)
            x = diffuse(x, d) + jnp.concatenate([field(before, p, 2), field(after, p, 3)], axis=1)
            out.append(x.astype(BF16).astype(F32))
    return jnp.concatenate(low, axis=0), jnp.concatenate(high, axis=0)


def patch(x, first, last):
    tiles = x.shape[0]
    row, lane = iota((tiles, LANES), 0), iota((tiles, LANES), 1)
    head = jnp.where((row == 0) & (lane < STEPS), first, x[:, :LANES])
    tail = jnp.where((row == tiles - 1) & (lane >= LANES - STEPS), last, x[:, -LANES:])
    return jnp.concatenate([head, x[:, LANES:-LANES], tail], axis=1)


def widen(x, left, right):
    tiles = x.shape[0]
    row = iota((tiles, LANES), 0)
    before = jnp.where(row == 0, left, pltpu.roll(x[:, -LANES:], 1, 0))
    after = jnp.where(row == tiles - 1, right, pltpu.roll(x[:, :LANES], tiles - 1, 0))
    return jnp.concatenate([before, x, after], axis=1)


def diffuse(x, d):
    n = x.shape[1]
    for _ in range(STEPS):
        x = x + d * (pltpu.roll(x, 1, 1) - 2.0 * x + pltpu.roll(x, n - 1, 1))
    return x


def pick_rows(wanted, rows):
    m = rows.shape[0]
    n = wanted.shape[0]
    choice = (wanted[:, :m] == iota((n, m), 1)).astype(F32).astype(BF16)
    return jnp.dot(choice, rows, preferred_element_type=F32)


def requested(notes, prior, cycle, rows):
    pairs = len(notes)
    total = pairs * rows
    asked = jnp.concatenate(notes, axis=0)
    spread = jnp.broadcast_to(asked[:, None, :], (pairs, rows, LANES)).reshape(total, LANES)
    mine = iota((total, LANES), 1) == cycle * rows + iota((total, LANES), 0) % rows
    wanted = jnp.sum(jnp.where(mine, spread, 0.0), axis=1, keepdims=True).astype(I32)
    return pick_rows(jnp.broadcast_to(wanted, (total, LANES)), prior)


def make_observe(blocks, per_block, tiles, near):
    count = blocks * per_block

    def kernel(tile, cell, prec, value, pattern, weight, where, terms, local):
        def line(x):
            wide = jnp.concatenate([x] * per_block, axis=1)
            own = iota((per_block, count), 1) // blocks == iota((per_block, count), 0)
            return jnp.sum(jnp.where(own, wide, 0), axis=0, keepdims=True)

        at = line(cell[...])
        row = (at // LANES) * tiles + jnp.concatenate([tile[...]] * per_block, axis=1)
        pick = iota((2, count), 0) == 0
        where[...] = jnp.where(pick, row, at % LANES)
        terms[0:1, :] = line(prec[...])
        for c in range(CYCLES):
            terms[c + 1:c + 2, :] = line(value[c])
        group = iota((tiles, count), 1) % blocks
        total = jnp.zeros((tiles, count), F32)
        for k in range(near):
            total = total + jnp.where(column_of(pattern[k:k + 1, :]) == group, column_of(weight[k:k + 1, :]), 0.0)
        local[...] = total

    return kernel


def assess(prior, where, prec, value, local, parts, tiles, cells):
    blocks = cells // LANES
    rows = tiles * blocks
    count = where.shape[1]
    stacked = jnp.concatenate(
        [jnp.concatenate([x[:, k * LANES:(k + 1) * LANES] for k in range(blocks)], axis=0) for x in prior],
        axis=1,
    )
    choice = (iota((rows, count), 0) == where[0:1, :]).astype(F32).astype(BF16)
    lines = lax.dot_general(stacked, choice, (((0,), (0,)), ((), ())), preferred_element_type=F32)
    lane = iota((LANES, count), 0) == where[1:2, :]
    score = []
    for p in range(parts):
        predicted = jnp.sum(jnp.where(lane, lines[p * LANES:(p + 1) * LANES, :], 0.0), axis=0, keepdims=True)
        miss = value - predicted
        term = 0.5 * (prec * miss * miss)
        score.append(jnp.sum(local * term, axis=1, keepdims=True))
    least = score[0]
    for s in score[1:]:
        least = jnp.minimum(least, s)
    scale = [jnp.exp(least - s) for s in score]
    total = scale[0]
    for s in scale[1:]:
        total = total + s
    weighted = scale[0] * prior[0].astype(F32)
    for s, x in zip(scale[1:], prior[1:]):
        weighted = weighted + s * x.astype(F32)
    return least, total, weighted


def pieces(x):
    high = x.astype(BF16).astype(F32)
    middle = (x - high).astype(BF16).astype(F32)
    low = (x - high - middle).astype(BF16).astype(F32)
    return high, middle, low


def share_of(ref, member, share):
    if share % LANES == 0:
        return ref[:, pl.ds(pl.multiple_of(member * share, LANES), share)]
    return pltpu.roll(ref[...], ref.shape[1] - member * share, 1)[:, :share]


def pack_mean(outs, at, least, total, sums, share):
    rows = outs[0].shape[0]
    tiles = sums.shape[0]
    groups = tiles // rows
    m = here()
    lane = iota((rows, LANES), 1)
    misc = jnp.zeros((rows, LANES), F32)
    spot = 0
    for x in (least, total):
        for piece in pieces(x):
            for g in range(groups):
                misc = jnp.where(lane == spot, piece[g * rows:(g + 1) * rows, :], misc)
                spot += 1
    end = at + groups * share
    for k, out in enumerate(outs):
        block = share_of(sums, m ^ (2 * k), share)
        for g in range(groups):
            out[:, at + g * share:at + (g + 1) * share] = block[g * rows:(g + 1) * rows, :].astype(BF16)
        out[:, end:end + LANES] = misc.astype(BF16)


def unpack_mean(got, at, tiles, share):
    rows = got[0].shape[0]
    groups = tiles // rows
    end = at + groups * share
    misc = [x[:, end:end + LANES].astype(F32) for x in got]
    means = []
    for g in range(groups):
        stats = []
        for x in misc:
            pair = []
            for kind in range(2):
                spot = [(kind * 3 + piece) * groups + g for piece in range(3)]
                high, middle, low = [x[:, i:i + 1] for i in spot]
                pair.append(high + middle + low)
            stats.append(pair)
        lowest = stats[0][0]
        for least, _ in stats[1:]:
            lowest = jnp.minimum(lowest, least)
        top, bottom = 0.0, 0.0
        for x, (least, total) in zip(got, stats):
            scale = jnp.exp(lowest - least)
            top = top + scale * x[:, at + g * share:at + (g + 1) * share].astype(F32)
            bottom = bottom + scale * total
        means.append(top / bottom)
    return means


def make_first(parts, tiles, cells):
    def kernel(state, diff, pert, after, prior):
        nothing = jnp.zeros((1, LANES), F32)
        d = widen(diff[...], nothing, nothing)
        for p in range(parts):
            x = diffuse(widen(state[p].astype(F32), nothing, nothing), d)
            now = x[:, LANES:LANES + cells] + pert[0, p].astype(F32)
            prior[p * tiles:(p + 1) * tiles, :] = now.astype(BF16)

    return kernel


def make_send(pairs, rows):
    def kernel(own, other, trail, *refs):
        notes, send, half = refs[:pairs], refs[pairs], refs[pairs + 1]
        prior = jnp.concatenate([own[...], other[...]], axis=0)
        sent = requested([x[...] for x in notes], prior, 0, rows)
        g = here() // 2
        for k in range(pairs):
            send[g ^ k] = sent[k * rows:(k + 1) * rows, :].astype(BF16)
        size = padded(pairs)
        half[...] = jnp.zeros(half.shape, F32)
        for k in range(pairs):
            half[k:k + 1, :] = notes[k][...]
        half[size:, :] = trail[...]

    return kernel


def make_assess(pairs, parts, tiles, cells, share):
    size = padded(pairs)

    def kernel(own, other, low, high, where, terms, local, *refs):
        outs, sums = refs[:pairs], refs[pairs]
        fixed = []
        for h, prior in enumerate((own, other)):
            for p in range(parts):
                row = (2 * p + h) * size
                x = prior[p * tiles:(p + 1) * tiles, :].astype(F32)
                x = patch(x, low[row:row + 1, LANES:], high[row:row + 1, :LANES])
                fixed.append(x.astype(BF16))
        least, total, weighted = assess(
            fixed, where[...], terms[0:1, :], terms[1:2, :], local[...], 2 * parts, tiles, cells
        )
        sums[...] = weighted
        pack_mean(outs, 0, least, total, sums, share)

    return kernel


def make_second(pairs, parts, tiles, cells):
    size = padded(pairs)

    def kernel(keys, diff, pert, message, mine, theirs, after, *refs):
        got, prior, low_out, high_out = refs
        below, above = halves(mine[...], theirs[...])
        low, high = edge_windows(message[...], below, above, size, parts)
        low_out[...] = low
        high_out[...] = high
        below, above = below[size:size + 8, :], above[size:size + 8, :]
        moved = pick_rows(keys[0], got[...].reshape(-1, cells))
        here_codes = message[size + 2:size + 2 + 2 * parts, :].astype(I32)
        codes = jnp.concatenate([here_codes[parts:], below[2:2 + parts, :].astype(I32)], axis=0)
        start = pick_rows(codes, low.astype(BF16))
        codes = jnp.concatenate([here_codes[:parts], above[2 + parts:2 + 2 * parts, :].astype(I32)], axis=0)
        end = pick_rows(codes, high.astype(BF16))
        d = widen(diff[...], below[0:1, :], above[1:2, :])
        for p in range(parts):
            x = patch(moved[p * tiles:(p + 1) * tiles, :], start[p:p + 1, LANES:], end[p:p + 1, :LANES])
            q = parts + p
            x = widen(x, start[q:q + 1, :LANES], end[q:q + 1, LANES:])
            x = diffuse(x, d)[:, LANES:LANES + cells]
            prior[p * tiles:(p + 1) * tiles, :] = (x + pert[0, p].astype(F32)).astype(BF16)

    return kernel


def make_send_second(pairs, rows, parts, tiles, cells, share):
    def kernel(own, other, where, terms, local, *refs):
        notes, kept, send, sums = refs[:pairs], refs[pairs:2 * pairs], refs[2 * pairs], refs[2 * pairs + 1]
        g = here() // 2
        outs = [send.at[g ^ k] for k in range(pairs)]
        prior = jnp.concatenate([own[...], other[...]], axis=0)
        sent = requested([x[...] for x in notes], prior, 1, rows)
        extra = kept[0].shape[1]
        for k in range(pairs):
            outs[k][:, :cells] = sent[k * rows:(k + 1) * rows, :].astype(BF16)
            outs[k][:, cells:cells + extra] = kept[k][...]
        least, total, weighted = assess(
            [x[p * tiles:(p + 1) * tiles, :] for x in (own, other) for p in range(parts)],
            where[...], terms[0:1, :], terms[2:3, :], local[...], 2 * parts, tiles, cells,
        )
        sums[...] = weighted
        pack_mean(outs, cells + extra, least, total, sums, share)

    return kernel


def make_last(pairs, rows, parts, tiles, cells):
    def kernel(keys, arrived, analysis, mean):
        got = [arrived.at[k] for k in range(pairs)]
        picked = pick_rows(keys[1], arrived[:, :, :cells].reshape(pairs * rows, cells))
        for p in range(parts):
            analysis[p] = picked[p * tiles:(p + 1) * tiles, :].astype(BF16)
        share = mean.shape[2]
        extra = tiles // rows * share + LANES
        for c in range(CYCLES):
            for g, x in enumerate(unpack_mean(got, cells + c * extra, tiles, share)):
                mean[c, g * rows:(g + 1) * rows, :] = x

    return kernel


def body(
    state,
    diffusivity,
    model_perturbation,
    obs_values,
    obs_prec,
    obs_tile,
    obs_cell,
    pattern,
    loc_weight,
    anc_member,
    anc_slot,
):
    parts, tiles, cells = state.shape
    members = lax.axis_size("member")
    regions = lax.axis_size("region")
    capacity = max(2, 2 * parts * tiles // members)
    share = cells // members
    pairs = members // 2
    rows = 2 * capacity
    extra = tiles // rows * share + LANES
    blocks, per_block = obs_cell.shape
    count = blocks * per_block
    member_of = anc_member.reshape(CYCLES, parts, tiles)
    slot_of = anc_slot.reshape(CYCLES, parts, tiles)
    near = pattern.shape[1]
    ends = cells // LANES - 1

    def block(shape, at):
        lead = (0,) * (len(shape) - 1)
        return pl.BlockSpec(shape, lambda i: lead + (at,))

    edges = [state, state, diffusivity, diffusivity, model_perturbation, model_perturbation, member_of, slot_of]
    *notes, trail, keys = call(
        make_prepare(members, capacity, parts, tiles),
        [((1, LANES), F32)] * pairs + [((8, LANES), F32), ((CYCLES, parts * tiles, LANES), I32)],
        [pltpu.with_memory_space_constraint(x, pltpu.HBM) for x in edges],
        [
            block((parts, tiles, LANES), 0),
            block((parts, tiles, LANES), ends),
            block((tiles, LANES), 0),
            block((tiles, LANES), ends),
            block((1, parts, tiles, LANES), 0),
            block((1, parts, tiles, LANES), ends),
            whole_spec(member_of.shape),
            whole_spec(slot_of.shape),
        ],
        name="prepare",
    )

    def trade(x):
        return lax.ppermute(x, "member", [(i, i ^ 1) for i in range(members)])

    def exchange(send):
        groups = [[2 * k + h for k in range(pairs)] for h in range(2)]
        return lax.all_to_all(send, "member", 0, 0, axis_index_groups=groups, tiled=True)

    for k in range(1, pairs):
        notes[k] = lax.ppermute(notes[k], "member", [(i, i ^ (2 * k)) for i in range(members)])

    where, terms, local = call(
        make_observe(blocks, per_block, tiles, near),
        [((2, count), I32), ((1 + CYCLES, count), F32), ((tiles, count), F32)],
        [obs_tile[None, :], obs_cell.T, obs_prec.T, jnp.swapaxes(obs_values, 1, 2), pattern.T, loc_weight.T],
        name="observe",
    )

    def noise_spec(c):
        return pl.BlockSpec((1, parts, tiles, cells), lambda i: (c, 0, 0, 0))

    args = [state, diffusivity, model_perturbation, trail]
    specs = [whole_spec(a.shape) for a in args]
    specs[2] = noise_spec(0)
    (prior,) = call(
        make_first(parts, tiles, cells), [((parts * tiles, cells), BF16)], args, specs, name="forecast_first"
    )
    other = trade(prior)
    size = padded(pairs)
    send, half = call(
        make_send(pairs, rows),
        [((pairs, rows, cells), BF16), ((size + trail.shape[0], LANES), F32)],
        [prior, other, trail, *notes],
        name="send_first",
    )
    got = exchange(send)
    message = jnp.concatenate([half, trade(half)], axis=0)
    steps = []
    for i in range(members):
        first, last = (0, regions - 1) if i % 2 == 0 else (1, regions)
        steps += [(i * regions + r, i * regions + r + 1 - 2 * (i % 2)) for r in range(first, last)]
    mine = lax.ppermute(message, ("member", "region"), steps)
    theirs = trade(mine)
    window = ((parts * 2 * size, 2 * LANES), F32)
    sums = [((tiles, cells), F32)]
    args = [keys, diffusivity, model_perturbation, message, mine, theirs, where, got]
    specs = [whole_spec(a.shape) for a in args]
    specs[2] = noise_spec(1)
    second, low, high = call(
        make_second(pairs, parts, tiles, cells),
        [((parts * tiles, cells), BF16), window, window],
        args,
        specs,
        name="forecast_second",
    )
    kept = call(
        make_assess(pairs, parts, tiles, cells, share),
        [((rows, extra), BF16)] * pairs,
        [prior, other, low, high, where, terms, local],
        scratch=sums,
        name="assess_first",
    )
    (send,) = call(
        make_send_second(pairs, rows, parts, tiles, cells, share),
        [((pairs, rows, cells + CYCLES * extra), BF16)],
        [second, trade(second), where, terms, local, *notes, *kept],
        scratch=sums,
        name="send_second",
    )
    got = exchange(send)
    return tuple(
        call(
            make_last(pairs, rows, parts, tiles, cells),
            [(state.shape, BF16), ((CYCLES, tiles, share), F32)],
            [keys, got],
            name="finish",
        )
    )


def solution(mesh):
    in_specs = (
        P("member", "region", None),
        P("region", None),
        P(None, "member", "region", None),
        P(None, "region", None),
        P("region", None),
        P("region"),
        P("region", None),
        P("region", None),
        P("region", None),
        P(None, "region", "member", None, None),
        P(None, "region", "member", None),
    )
    out_specs = (P("member", "region", None), P(None, "region", "member"))
    return jax.shard_map(body, mesh=mesh, in_specs=in_specs, out_specs=out_specs, check_vma=False)
```

```python
import jax
import jax.numpy as jnp
from jax import lax
from jax.experimental import pallas as pl
from jax.experimental.pallas import tpu as pltpu
from jax.sharding import PartitionSpec as P

CYCLES = 2
STEPS = 2
LANES = 128
F32 = jnp.float32
BF16 = jnp.bfloat16
I32 = jnp.int32
PARAMS = pltpu.CompilerParams(vmem_limit_bytes=48 * 1024 * 1024)


def iota(shape, dim):
    return lax.broadcasted_iota(I32, shape, dim)


def whole_spec(shape):
    zeros = (0,) * len(shape)
    return pl.BlockSpec(shape, lambda i: zeros)


def call(kernel, outs, args, specs=None, scratch=(), name=None):
    specs = specs or [whole_spec(a.shape) for a in args]
    return pl.pallas_call(
        kernel,
        out_shape=[jax.ShapeDtypeStruct(s, d) for s, d in outs],
        grid=(1,),
        in_specs=specs,
        out_specs=[whole_spec(s) for s, _ in outs],
        scratch_shapes=[pltpu.VMEM(s, d) for s, d in scratch],
        compiler_params=PARAMS,
        name=name,
    )(*args)


def column_of(row):
    n = row.shape[1]
    square = jnp.broadcast_to(row, (n, n))
    return jnp.sum(jnp.where(iota((n, n), 0) == iota((n, n), 1), square, 0), axis=1, keepdims=True)


def here():
    return lax.axis_index("member")


EDGE_AT = 32
STRIDE = 8


def padded(pairs):
    return max(8, pairs)


def make_prepare(members, capacity, parts, tiles):
    width = 2 * STEPS
    pairs = members // 2
    rows = parts * tiles

    def kernel(st0, st1, df0, df1, pb0, pb1, am, slot, *outs):
        *notes, trail, keys = outs
        m = here()
        lane = iota((1, LANES), 1)
        last = tiles - 1
        trail[...] = jnp.zeros(trail.shape, F32)
        trail[0:1, :] = df1[last:last + 1, :]
        trail[1:2, :] = df0[0:1, :]
        edge = jnp.zeros((1, LANES), F32)
        for p in range(parts):
            for i, t in enumerate((last, 0)):
                source = am[0, p:p + 1, t:t + 1] ^ m
                code = (slot[0, p:p + 1, t:t + 1] * 2 + source % 2) * padded(pairs) + source // 2
                row = 2 + i * parts + p
                trail[row:row + 1, :] = jnp.broadcast_to(code.astype(F32), (1, LANES))
            fields = (st1[p, last:last + 1, :], st0[p, 0:1, :], pb1[0, p, last:last + 1, :], pb0[0, p, 0:1, :])
            for i, x in enumerate(fields):
                to = EDGE_AT + STRIDE * (4 * p + i)
                start = 0 if i % 2 else LANES - width
                moved = pltpu.roll(x.astype(F32), (to - start) % LANES, 1)
                edge = jnp.where((lane >= to) & (lane < to + width), moved, edge)
        before = (iota((tiles, tiles), 0) < iota((tiles, tiles), 1)).astype(F32)
        asked = jnp.zeros((pairs, LANES), F32)
        for c in range(CYCLES):
            seen = jnp.zeros((members, 1), F32)
            for p in range(parts):
                source = am[c, p:p + 1, :] ^ m
                named = (iota((members, tiles), 0) == source).astype(F32)
                earlier = seen + jnp.dot(named, before, preferred_element_type=F32)
                rank = jnp.sum(named * earlier, axis=0, keepdims=True).astype(I32)
                seen = seen + jnp.sum(named, axis=1, keepdims=True)
                half = source % 2
                code = half * rows + slot[c, p:p + 1, :] * tiles + iota((1, tiles), 1)
                spot = (iota((LANES, tiles), 0) == (2 * c + half) * capacity + rank).astype(F32)
                pair = jnp.where(iota((pairs, tiles), 0) == source // 2, (code + 1).astype(F32), 0.0)
                asked = asked + lax.dot_general(pair, spot, (((1,), (1,)), ((), ())), preferred_element_type=F32)
                column = column_of(source * capacity + rank)
                keys[c, p * tiles:(p + 1) * tiles, :] = jnp.broadcast_to(column, (tiles, LANES))
        evens = [[k] for k in range(0, pairs, 2)]
        for ref, rows_of in zip(notes, evens + [list(range(1, pairs, 2))]):
            for i, k in enumerate(rows_of):
                ref[i:i + 1, :] = jnp.where(lane < EDGE_AT, asked[k:k + 1, :] - 1.0, edge)

    return kernel


def halves(mine, theirs):
    half = theirs.shape[0] // 2
    theirs = jnp.concatenate([theirs[half:, :], theirs[:half, :]], axis=0)
    first = jnp.broadcast_to(here() % 2, mine.shape) == 0
    return jnp.where(first, mine, theirs), jnp.where(first, theirs, mine)


def edge_windows(own, below, above, size, parts):
    width = 2 * STEPS

    def field(note, p, i):
        at = EDGE_AT + STRIDE * (4 * p + i)
        start = 0 if i % 2 else LANES - width
        both = jnp.concatenate([note[:size, :], note[size + 8:2 * size + 8, :]], axis=0)
        return pltpu.roll(both, (start - at) % LANES, 1)

    low, high = [], []
    for out, before, after in ((low, below, own), (high, own, above)):
        d = jnp.concatenate([before[size:size + 1, :], after[size + 1:size + 2, :]], axis=1)
        for p in range(parts):
            x = jnp.concatenate([field(before, p, 0), field(after, p, 1)], axis=1)
            x = diffuse(x, d) + jnp.concatenate([field(before, p, 2), field(after, p, 3)], axis=1)
            out.append(x.astype(BF16).astype(F32))
    return jnp.concatenate(low, axis=0), jnp.concatenate(high, axis=0)


def patch(x, first, last):
    tiles = x.shape[0]
    row, lane = iota((tiles, LANES), 0), iota((tiles, LANES), 1)
    head = jnp.where((row == 0) & (lane < STEPS), first, x[:, :LANES])
    tail = jnp.where((row == tiles - 1) & (lane >= LANES - STEPS), last, x[:, -LANES:])
    return jnp.concatenate([head, x[:, LANES:-LANES], tail], axis=1)


def widen(x, left, right):
    tiles = x.shape[0]
    row = iota((tiles, LANES), 0)
    before = jnp.where(row == 0, left, pltpu.roll(x[:, -LANES:], 1, 0))
    after = jnp.where(row == tiles - 1, right, pltpu.roll(x[:, :LANES], tiles - 1, 0))
    return jnp.concatenate([before, x, after], axis=1)


def diffuse(x, d):
    n = x.shape[1]
    for _ in range(STEPS):
        x = x + d * (pltpu.roll(x, 1, 1) - 2.0 * x + pltpu.roll(x, n - 1, 1))
    return x


def pick_rows(wanted, rows):
    m = rows.shape[0]
    n = wanted.shape[0]
    choice = (wanted[:, :m] == iota((n, m), 1)).astype(F32).astype(BF16)
    return jnp.dot(choice, rows, preferred_element_type=F32)


def requested(notes, prior, cycle, rows):
    pairs = len(notes)
    total = pairs * rows
    asked = jnp.concatenate(notes, axis=0)
    spread = jnp.broadcast_to(asked[:, None, :], (pairs, rows, LANES)).reshape(total, LANES)
    mine = iota((total, LANES), 1) == cycle * rows + iota((total, LANES), 0) % rows
    wanted = jnp.sum(jnp.where(mine, spread, 0.0), axis=1, keepdims=True).astype(I32)
    return pick_rows(jnp.broadcast_to(wanted, (total, LANES)), prior)


def make_observe(blocks, per_block, tiles, near):
    count = blocks * per_block

    def kernel(tile, cell, prec, value, pattern, weight, where, terms, local):
        def line(x):
            wide = jnp.concatenate([x] * per_block, axis=1)
            own = iota((per_block, count), 1) // blocks == iota((per_block, count), 0)
            return jnp.sum(jnp.where(own, wide, 0), axis=0, keepdims=True)

        at = line(cell[...])
        row = (at // LANES) * tiles + jnp.concatenate([tile[...]] * per_block, axis=1)
        pick = iota((2, count), 0) == 0
        where[...] = jnp.where(pick, row, at % LANES)
        terms[0:1, :] = line(prec[...])
        for c in range(CYCLES):
            terms[c + 1:c + 2, :] = line(value[c])
        group = iota((tiles, count), 1) % blocks
        total = jnp.zeros((tiles, count), F32)
        for k in range(near):
            total = total + jnp.where(column_of(pattern[k:k + 1, :]) == group, column_of(weight[k:k + 1, :]), 0.0)
        local[...] = total

    return kernel


def assess(prior, where, prec, value, local, parts, tiles, cells):
    blocks = cells // LANES
    rows = tiles * blocks
    count = where.shape[1]
    stacked = jnp.concatenate(
        [jnp.concatenate([x[:, k * LANES:(k + 1) * LANES] for k in range(blocks)], axis=0) for x in prior],
        axis=1,
    )
    choice = (iota((rows, count), 0) == where[0:1, :]).astype(F32).astype(BF16)
    lines = lax.dot_general(stacked, choice, (((0,), (0,)), ((), ())), preferred_element_type=F32)
    lane = iota((LANES, count), 0) == where[1:2, :]
    score = []
    for p in range(parts):
        predicted = jnp.sum(jnp.where(lane, lines[p * LANES:(p + 1) * LANES, :], 0.0), axis=0, keepdims=True)
        miss = value - predicted
        term = 0.5 * (prec * miss * miss)
        score.append(jnp.sum(local * term, axis=1, keepdims=True))
    least = score[0]
    for s in score[1:]:
        least = jnp.minimum(least, s)
    scale = [jnp.exp(least - s) for s in score]
    total = scale[0]
    for s in scale[1:]:
        total = total + s
    weighted = scale[0] * prior[0].astype(F32)
    for s, x in zip(scale[1:], prior[1:]):
        weighted = weighted + s * x.astype(F32)
    return least, total, weighted


def pieces(x):
    high = x.astype(BF16).astype(F32)
    middle = (x - high).astype(BF16).astype(F32)
    low = (x - high - middle).astype(BF16).astype(F32)
    return high, middle, low


def share_of(ref, member, share):
    if share % LANES == 0:
        return ref[:, pl.ds(pl.multiple_of(member * share, LANES), share)]
    return pltpu.roll(ref[...], ref.shape[1] - member * share, 1)[:, :share]


def pack_mean(outs, at, least, total, sums, share):
    rows = outs[0].shape[0]
    tiles = sums.shape[0]
    groups = tiles // rows
    m = here()
    lane = iota((rows, LANES), 1)
    misc = jnp.zeros((rows, LANES), F32)
    spot = 0
    for x in (least, total):
        for piece in pieces(x):
            for g in range(groups):
                misc = jnp.where(lane == spot, piece[g * rows:(g + 1) * rows, :], misc)
                spot += 1
    end = at + groups * share
    for k, out in enumerate(outs):
        block = share_of(sums, m ^ (2 * k), share)
        for g in range(groups):
            out[:, at + g * share:at + (g + 1) * share] = block[g * rows:(g + 1) * rows, :].astype(BF16)
        out[:, end:end + LANES] = misc.astype(BF16)


def unpack_mean(got, at, tiles, share):
    rows = got[0].shape[0]
    groups = tiles // rows
    end = at + groups * share
    misc = [x[:, end:end + LANES].astype(F32) for x in got]
    means = []
    for g in range(groups):
        stats = []
        for x in misc:
            pair = []
            for kind in range(2):
                spot = [(kind * 3 + piece) * groups + g for piece in range(3)]
                high, middle, low = [x[:, i:i + 1] for i in spot]
                pair.append(high + middle + low)
            stats.append(pair)
        lowest = stats[0][0]
        for least, _ in stats[1:]:
            lowest = jnp.minimum(lowest, least)
        top, bottom = 0.0, 0.0
        for x, (least, total) in zip(got, stats):
            scale = jnp.exp(lowest - least)
            top = top + scale * x[:, at + g * share:at + (g + 1) * share].astype(F32)
            bottom = bottom + scale * total
        means.append(top / bottom)
    return means


def make_first(parts, tiles, cells):
    def kernel(state, diff, pert, after, prior):
        nothing = jnp.zeros((1, LANES), F32)
        d = widen(diff[...], nothing, nothing)
        for p in range(parts):
            x = diffuse(widen(state[p].astype(F32), nothing, nothing), d)
            now = x[:, LANES:LANES + cells] + pert[0, p].astype(F32)
            prior[p * tiles:(p + 1) * tiles, :] = now.astype(BF16)

    return kernel


def read_notes(refs, spots):
    return [refs[i][row:row + 1, :] for i, row in spots]


def make_send(pairs, rows, spots):
    count = 1 + max(i for i, _ in spots)

    def kernel(own, other, trail, *refs):
        notes = read_notes(refs, spots)
        sends, half = refs[count:count + pairs], refs[count + pairs]
        prior = jnp.concatenate([own[...], other[...]], axis=0)
        sent = requested(notes, prior, 0, rows)
        for k in range(pairs):
            sends[k][...] = sent[k * rows:(k + 1) * rows, :].astype(BF16)
        size = padded(pairs)
        half[...] = jnp.zeros(half.shape, F32)
        for k in range(pairs):
            half[k:k + 1, :] = notes[k]
        half[size:, :] = trail[...]

    return kernel


def make_assess(pairs, parts, tiles, cells, share):
    size = padded(pairs)

    def kernel(own, other, low, high, where, terms, local, *refs):
        outs, sums = refs[:pairs], refs[pairs]
        fixed = []
        for h, prior in enumerate((own, other)):
            for p in range(parts):
                row = (2 * p + h) * size
                x = prior[p * tiles:(p + 1) * tiles, :].astype(F32)
                x = patch(x, low[row:row + 1, LANES:], high[row:row + 1, :LANES])
                fixed.append(x.astype(BF16))
        least, total, weighted = assess(
            fixed, where[...], terms[0:1, :], terms[1:2, :], local[...], 2 * parts, tiles, cells
        )
        sums[...] = weighted
        pack_mean(outs, 0, least, total, sums, share)

    return kernel


def make_second(pairs, parts, tiles, cells):
    size = padded(pairs)

    def kernel(keys, diff, pert, message, mine, theirs, after, *refs):
        got, prior, low_out, high_out = refs[:pairs], refs[pairs], refs[pairs + 1], refs[pairs + 2]
        below, above = halves(mine[...], theirs[...])
        low, high = edge_windows(message[...], below, above, size, parts)
        low_out[...] = low
        high_out[...] = high
        below, above = below[size:size + 8, :], above[size:size + 8, :]
        arrived = jnp.concatenate([x[...] for x in got], axis=0)
        moved = pick_rows(keys[0], arrived)
        here_codes = message[size + 2:size + 2 + 2 * parts, :].astype(I32)
        codes = jnp.concatenate([here_codes[parts:], below[2:2 + parts, :].astype(I32)], axis=0)
        start = pick_rows(codes, low.astype(BF16))
        codes = jnp.concatenate([here_codes[:parts], above[2 + parts:2 + 2 * parts, :].astype(I32)], axis=0)
        end = pick_rows(codes, high.astype(BF16))
        d = widen(diff[...], below[0:1, :], above[1:2, :])
        for p in range(parts):
            x = patch(moved[p * tiles:(p + 1) * tiles, :], start[p:p + 1, LANES:], end[p:p + 1, :LANES])
            q = parts + p
            x = widen(x, start[q:q + 1, :LANES], end[q:q + 1, LANES:])
            x = diffuse(x, d)[:, LANES:LANES + cells]
            prior[p * tiles:(p + 1) * tiles, :] = (x + pert[0, p].astype(F32)).astype(BF16)

    return kernel


def make_send_second(pairs, rows, parts, tiles, cells, share, spots):
    count = 1 + max(i for i, _ in spots)

    def kernel(own, other, where, terms, local, *refs):
        notes, refs = read_notes(refs, spots), refs[count:]
        kept, outs, sums = refs[:pairs], refs[pairs:2 * pairs], refs[2 * pairs]
        prior = jnp.concatenate([own[...], other[...]], axis=0)
        sent = requested(notes, prior, 1, rows)
        extra = kept[0].shape[1]
        for k in range(pairs):
            outs[k][:, :cells] = sent[k * rows:(k + 1) * rows, :].astype(BF16)
            outs[k][:, cells:cells + extra] = kept[k][...]
        least, total, weighted = assess(
            [x[p * tiles:(p + 1) * tiles, :] for x in (own, other) for p in range(parts)],
            where[...], terms[0:1, :], terms[2:3, :], local[...], 2 * parts, tiles, cells,
        )
        sums[...] = weighted
        pack_mean(outs, cells + extra, least, total, sums, share)

    return kernel


def make_last(pairs, rows, parts, tiles, cells):
    def kernel(keys, *refs):
        got, analysis, mean = refs[:pairs], refs[pairs], refs[pairs + 1]
        arrived = jnp.concatenate([x[:, :cells] for x in got], axis=0)
        picked = pick_rows(keys[1], arrived)
        for p in range(parts):
            analysis[p] = picked[p * tiles:(p + 1) * tiles, :].astype(BF16)
        share = mean.shape[2]
        extra = tiles // rows * share + LANES
        for c in range(CYCLES):
            for g, x in enumerate(unpack_mean(got, cells + c * extra, tiles, share)):
                mean[c, g * rows:(g + 1) * rows, :] = x

    return kernel


def body(
    state,
    diffusivity,
    model_perturbation,
    obs_values,
    obs_prec,
    obs_tile,
    obs_cell,
    pattern,
    loc_weight,
    anc_member,
    anc_slot,
):
    parts, tiles, cells = state.shape
    members = lax.axis_size("member")
    regions = lax.axis_size("region")
    capacity = max(2, 2 * parts * tiles // members)
    share = cells // members
    pairs = members // 2
    rows = 2 * capacity
    extra = tiles // rows * share + LANES
    blocks, per_block = obs_cell.shape
    count = blocks * per_block
    member_of = anc_member.reshape(CYCLES, parts, tiles)
    slot_of = anc_slot.reshape(CYCLES, parts, tiles)
    near = pattern.shape[1]
    ends = cells // LANES - 1

    def block(shape, at):
        lead = (0,) * (len(shape) - 1)
        return pl.BlockSpec(shape, lambda i: lead + (at,))

    edges = [state, state, diffusivity, diffusivity, model_perturbation, model_perturbation, member_of, slot_of]
    *notes, trail, keys = call(
        make_prepare(members, capacity, parts, tiles),
        [((1, LANES), F32)] * (pairs // 2) + [((pairs // 2, LANES), F32), ((8, LANES), F32), ((CYCLES, parts * tiles, LANES), I32)],
        [pltpu.with_memory_space_constraint(x, pltpu.HBM) for x in edges],
        [
            block((parts, tiles, LANES), 0),
            block((parts, tiles, LANES), ends),
            block((tiles, LANES), 0),
            block((tiles, LANES), ends),
            block((1, parts, tiles, LANES), 0),
            block((1, parts, tiles, LANES), ends),
            whole_spec(member_of.shape),
            whole_spec(slot_of.shape),
        ],
        name="prepare",
    )

    def trade(x):
        return lax.ppermute(x, "member", [(i, i ^ 1) for i in range(members)])

    def exchange(sends):
        got = [sends[0]]
        for k in range(1, pairs):
            got.append(lax.ppermute(sends[k], "member", [(i, i ^ (2 * k)) for i in range(members)]))
        return got

    held = {k: (notes[k // 2], 0) for k in range(0, pairs, 2)}
    held.update({k: (notes[-1], k // 2) for k in range(1, pairs, 2)})
    bit = 1
    while bit < pairs:
        moving = [k for k in range(pairs) if k & bit]
        message = notes[-1]
        if bit > 1:
            message = jnp.concatenate([held[k][0][held[k][1]:held[k][1] + 1] for k in moving], axis=0)
        arrived = lax.ppermute(message, "member", [(i, i ^ (2 * bit)) for i in range(members)])
        held.update({k: (arrived, i) for i, k in enumerate(moving)})
        bit *= 2
    notes = []
    for x, _ in held.values():
        if not any(x is y for y in notes):
            notes.append(x)
    spots = [([x is held[k][0] for x in notes].index(True), held[k][1]) for k in range(pairs)]

    where, terms, local = call(
        make_observe(blocks, per_block, tiles, near),
        [((2, count), I32), ((1 + CYCLES, count), F32), ((tiles, count), F32)],
        [obs_tile[None, :], obs_cell.T, obs_prec.T, jnp.swapaxes(obs_values, 1, 2), pattern.T, loc_weight.T],
        name="observe",
    )

    def noise_spec(c):
        return pl.BlockSpec((1, parts, tiles, cells), lambda i: (c, 0, 0, 0))

    args = [state, diffusivity, model_perturbation, trail]
    specs = [whole_spec(a.shape) for a in args]
    specs[2] = noise_spec(0)
    (prior,) = call(
        make_first(parts, tiles, cells), [((parts * tiles, cells), BF16)], args, specs, name="forecast_first"
    )
    other = trade(prior)
    size = padded(pairs)
    *sends, half = call(
        make_send(pairs, rows, spots),
        [((rows, cells), BF16)] * pairs + [((size + trail.shape[0], LANES), F32)],
        [prior, other, trail, *notes],
        name="send_first",
    )
    got = exchange(sends)
    message = jnp.concatenate([half, trade(half)], axis=0)
    steps = []
    for i in range(members):
        first, last = (0, regions - 1) if i % 2 == 0 else (1, regions)
        steps += [(i * regions + r, i * regions + r + 1 - 2 * (i % 2)) for r in range(first, last)]
    mine = lax.ppermute(message, ("member", "region"), steps)
    theirs = trade(mine)
    window = ((parts * 2 * size, 2 * LANES), F32)
    sums = [((tiles, cells), F32)]
    args = [keys, diffusivity, model_perturbation, message, mine, theirs, where, *got]
    specs = [whole_spec(a.shape) for a in args]
    specs[2] = noise_spec(1)
    second, low, high = call(
        make_second(pairs, parts, tiles, cells),
        [((parts * tiles, cells), BF16), window, window],
        args,
        specs,
        name="forecast_second",
    )
    kept = call(
        make_assess(pairs, parts, tiles, cells, share),
        [((rows, extra), BF16)] * pairs,
        [prior, other, low, high, where, terms, local],
        scratch=sums,
        name="assess_first",
    )
    sends = call(
        make_send_second(pairs, rows, parts, tiles, cells, share, spots),
        [((rows, cells + CYCLES * extra), BF16)] * pairs,
        [second, trade(second), where, terms, local, *notes, *kept],
        scratch=sums,
        name="send_second",
    )
    got = exchange(sends)
    return tuple(
        call(
            make_last(pairs, rows, parts, tiles, cells),
            [(state.shape, BF16), ((CYCLES, tiles, share), F32)],
            [keys, *got],
            name="finish",
        )
    )


def solution(mesh):
    in_specs = (
        P("member", "region", None),
        P("region", None),
        P(None, "member", "region", None),
        P(None, "region", None),
        P("region", None),
        P("region"),
        P("region", None),
        P("region", None),
        P("region", None),
        P(None, "region", "member", None, None),
        P(None, "region", "member", None),
    )
    out_specs = (P("member", "region", None), P(None, "region", "member"))
    return jax.shard_map(body, mesh=mesh, in_specs=in_specs, out_specs=out_specs, check_vma=False)
```

```python
import jax
import jax.numpy as jnp
from jax import lax
from jax.experimental import pallas as pl
from jax.experimental.pallas import tpu as pltpu
from jax.sharding import PartitionSpec as P

CYCLES = 2
STEPS = 2
LANES = 128
F32 = jnp.float32
BF16 = jnp.bfloat16
I32 = jnp.int32
PARAMS = pltpu.CompilerParams(vmem_limit_bytes=48 * 1024 * 1024)


def iota(shape, dim):
    return lax.broadcasted_iota(I32, shape, dim)


def whole_spec(shape):
    zeros = (0,) * len(shape)
    return pl.BlockSpec(shape, lambda i: zeros)


def call(kernel, outs, args, specs=None, scratch=(), name=None):
    specs = specs or [whole_spec(a.shape) for a in args]
    return pl.pallas_call(
        kernel,
        out_shape=[jax.ShapeDtypeStruct(s, d) for s, d in outs],
        grid=(1,),
        in_specs=specs,
        out_specs=[whole_spec(s) for s, _ in outs],
        scratch_shapes=[pltpu.VMEM(s, d) for s, d in scratch],
        compiler_params=PARAMS,
        name=name,
    )(*args)


def column_of(row):
    n = row.shape[1]
    square = jnp.broadcast_to(row, (n, n))
    return jnp.sum(jnp.where(iota((n, n), 0) == iota((n, n), 1), square, 0), axis=1, keepdims=True)


def here():
    return lax.axis_index("member")


EDGE_AT = 32
STRIDE = 8


def falling(pairs):
    return [0, *range(pairs - 1, 0, -1)]


def padded(pairs):
    return max(8, pairs)


def make_prepare(members, capacity, parts, tiles):
    width = 2 * STEPS
    pairs = members // 2
    rows = parts * tiles

    def kernel(st0, st1, df0, df1, pb0, pb1, am, slot, *outs):
        notes, trail, keys = outs[:pairs], outs[pairs], outs[pairs + 1]
        m = here()
        lane = iota((1, LANES), 1)
        last = tiles - 1
        trail[...] = jnp.zeros(trail.shape, F32)
        trail[0:1, :] = df1[last:last + 1, :]
        trail[1:2, :] = df0[0:1, :]
        edge = jnp.zeros((1, LANES), F32)
        for p in range(parts):
            for i, t in enumerate((last, 0)):
                source = am[0, p:p + 1, t:t + 1] ^ m
                code = (slot[0, p:p + 1, t:t + 1] * 2 + source % 2) * padded(pairs) + source // 2
                row = 2 + i * parts + p
                trail[row:row + 1, :] = jnp.broadcast_to(code.astype(F32), (1, LANES))
            fields = (st1[p, last:last + 1, :], st0[p, 0:1, :], pb1[0, p, last:last + 1, :], pb0[0, p, 0:1, :])
            for i, x in enumerate(fields):
                to = EDGE_AT + STRIDE * (4 * p + i)
                start = 0 if i % 2 else LANES - width
                moved = pltpu.roll(x.astype(F32), (to - start) % LANES, 1)
                edge = jnp.where((lane >= to) & (lane < to + width), moved, edge)
        before = (iota((tiles, tiles), 0) < iota((tiles, tiles), 1)).astype(F32)
        asked = jnp.zeros((pairs, LANES), F32)
        for c in range(CYCLES):
            seen = jnp.zeros((members, 1), F32)
            for p in range(parts):
                source = am[c, p:p + 1, :] ^ m
                named = (iota((members, tiles), 0) == source).astype(F32)
                earlier = seen + jnp.dot(named, before, preferred_element_type=F32)
                rank = jnp.sum(named * earlier, axis=0, keepdims=True).astype(I32)
                seen = seen + jnp.sum(named, axis=1, keepdims=True)
                half = source % 2
                code = half * rows + slot[c, p:p + 1, :] * tiles + iota((1, tiles), 1)
                spot = (iota((LANES, tiles), 0) == (2 * c + half) * capacity + rank).astype(F32)
                pair = jnp.where(iota((pairs, tiles), 0) == source // 2, (code + 1).astype(F32), 0.0)
                asked = asked + lax.dot_general(pair, spot, (((1,), (1,)), ((), ())), preferred_element_type=F32)
                column = column_of(source * capacity + rank)
                keys[c, p * tiles:(p + 1) * tiles, :] = jnp.broadcast_to(column, (tiles, LANES))
        for k in range(pairs):
            notes[k][...] = jnp.where(lane < EDGE_AT, asked[k:k + 1, :] - 1.0, edge)

    return kernel


def halves(mine, theirs):
    half = theirs.shape[0] // 2
    theirs = jnp.concatenate([theirs[half:, :], theirs[:half, :]], axis=0)
    first = jnp.broadcast_to(here() % 2, mine.shape) == 0
    return jnp.where(first, mine, theirs), jnp.where(first, theirs, mine)


def edge_windows(own, below, above, size, parts):
    width = 2 * STEPS

    def field(note, p, i):
        at = EDGE_AT + STRIDE * (4 * p + i)
        start = 0 if i % 2 else LANES - width
        both = jnp.concatenate([note[:size, :], note[size + 8:2 * size + 8, :]], axis=0)
        return pltpu.roll(both, (start - at) % LANES, 1)

    low, high = [], []
    for out, before, after in ((low, below, own), (high, own, above)):
        d = jnp.concatenate([before[size:size + 1, :], after[size + 1:size + 2, :]], axis=1)
        for p in range(parts):
            x = jnp.concatenate([field(before, p, 0), field(after, p, 1)], axis=1)
            x = diffuse(x, d) + jnp.concatenate([field(before, p, 2), field(after, p, 3)], axis=1)
            out.append(x.astype(BF16).astype(F32))
    return jnp.concatenate(low, axis=0), jnp.concatenate(high, axis=0)


def patch(x, first, last):
    tiles = x.shape[0]
    row, lane = iota((tiles, LANES), 0), iota((tiles, LANES), 1)
    head = jnp.where((row == 0) & (lane < STEPS), first, x[:, :LANES])
    tail = jnp.where((row == tiles - 1) & (lane >= LANES - STEPS), last, x[:, -LANES:])
    return jnp.concatenate([head, x[:, LANES:-LANES], tail], axis=1)


def widen(x, left, right):
    tiles = x.shape[0]
    row = iota((tiles, LANES), 0)
    before = jnp.where(row == 0, left, pltpu.roll(x[:, -LANES:], 1, 0))
    after = jnp.where(row == tiles - 1, right, pltpu.roll(x[:, :LANES], tiles - 1, 0))
    return jnp.concatenate([before, x, after], axis=1)


def diffuse(x, d):
    n = x.shape[1]
    for _ in range(STEPS):
        x = x + d * (pltpu.roll(x, 1, 1) - 2.0 * x + pltpu.roll(x, n - 1, 1))
    return x


def pick_rows(wanted, rows):
    m = rows.shape[0]
    n = wanted.shape[0]
    choice = (wanted[:, :m] == iota((n, m), 1)).astype(F32).astype(BF16)
    return jnp.dot(choice, rows, preferred_element_type=F32)


def requested(notes, prior, cycle, rows):
    pairs = len(notes)
    total = pairs * rows
    asked = jnp.concatenate(notes, axis=0)
    spread = jnp.broadcast_to(asked[:, None, :], (pairs, rows, LANES)).reshape(total, LANES)
    mine = iota((total, LANES), 1) == cycle * rows + iota((total, LANES), 0) % rows
    wanted = jnp.sum(jnp.where(mine, spread, 0.0), axis=1, keepdims=True).astype(I32)
    return pick_rows(jnp.broadcast_to(wanted, (total, LANES)), prior)


def make_observe(blocks, per_block, tiles, near):
    count = blocks * per_block

    def kernel(tile, cell, prec, value, pattern, weight, where, terms, local):
        def line(x):
            wide = jnp.concatenate([x] * per_block, axis=1)
            own = iota((per_block, count), 1) // blocks == iota((per_block, count), 0)
            return jnp.sum(jnp.where(own, wide, 0), axis=0, keepdims=True)

        at = line(cell[...])
        row = (at // LANES) * tiles + jnp.concatenate([tile[...]] * per_block, axis=1)
        pick = iota((2, count), 0) == 0
        where[...] = jnp.where(pick, row, at % LANES)
        terms[0:1, :] = line(prec[...])
        for c in range(CYCLES):
            terms[c + 1:c + 2, :] = line(value[c])
        group = iota((tiles, count), 1) % blocks
        total = jnp.zeros((tiles, count), F32)
        for k in range(near):
            total = total + jnp.where(column_of(pattern[k:k + 1, :]) == group, column_of(weight[k:k + 1, :]), 0.0)
        local[...] = total

    return kernel


def assess(prior, where, prec, value, local, parts, tiles, cells):
    blocks = cells // LANES
    rows = tiles * blocks
    count = where.shape[1]
    stacked = jnp.concatenate(
        [jnp.concatenate([x[:, k * LANES:(k + 1) * LANES] for k in range(blocks)], axis=0) for x in prior],
        axis=1,
    )
    choice = (iota((rows, count), 0) == where[0:1, :]).astype(F32).astype(BF16)
    lines = lax.dot_general(stacked, choice, (((0,), (0,)), ((), ())), preferred_element_type=F32)
    lane = iota((LANES, count), 0) == where[1:2, :]
    score = []
    for p in range(parts):
        predicted = jnp.sum(jnp.where(lane, lines[p * LANES:(p + 1) * LANES, :], 0.0), axis=0, keepdims=True)
        miss = value - predicted
        term = 0.5 * (prec * miss * miss)
        score.append(jnp.sum(local * term, axis=1, keepdims=True))
    least = score[0]
    for s in score[1:]:
        least = jnp.minimum(least, s)
    scale = [jnp.exp(least - s) for s in score]
    total = scale[0]
    for s in scale[1:]:
        total = total + s
    weighted = scale[0] * prior[0].astype(F32)
    for s, x in zip(scale[1:], prior[1:]):
        weighted = weighted + s * x.astype(F32)
    return least, total, weighted


def pieces(x):
    high = x.astype(BF16).astype(F32)
    middle = (x - high).astype(BF16).astype(F32)
    low = (x - high - middle).astype(BF16).astype(F32)
    return high, middle, low


def share_of(ref, member, share):
    if share % LANES == 0:
        return ref[:, pl.ds(pl.multiple_of(member * share, LANES), share)]
    return pltpu.roll(ref[...], ref.shape[1] - member * share, 1)[:, :share]


def pack_mean(outs, at, least, total, sums, share):
    rows = outs[0].shape[0]
    tiles = sums.shape[0]
    groups = tiles // rows
    m = here()
    lane = iota((rows, LANES), 1)
    misc = jnp.zeros((rows, LANES), F32)
    spot = 0
    for x in (least, total):
        for piece in pieces(x):
            for g in range(groups):
                misc = jnp.where(lane == spot, piece[g * rows:(g + 1) * rows, :], misc)
                spot += 1
    end = at + groups * share
    for k, out in enumerate(outs):
        block = share_of(sums, m ^ (2 * k), share)
        for g in range(groups):
            out[:, at + g * share:at + (g + 1) * share] = block[g * rows:(g + 1) * rows, :].astype(BF16)
        out[:, end:end + LANES] = misc.astype(BF16)


def unpack_mean(got, at, tiles, share):
    rows = got[0].shape[0]
    groups = tiles // rows
    end = at + groups * share
    misc = [x[:, end:end + LANES].astype(F32) for x in got]
    means = []
    for g in range(groups):
        stats = []
        for x in misc:
            pair = []
            for kind in range(2):
                spot = [(kind * 3 + piece) * groups + g for piece in range(3)]
                high, middle, low = [x[:, i:i + 1] for i in spot]
                pair.append(high + middle + low)
            stats.append(pair)
        lowest = stats[0][0]
        for least, _ in stats[1:]:
            lowest = jnp.minimum(lowest, least)
        top, bottom = 0.0, 0.0
        for x, (least, total) in zip(got, stats):
            scale = jnp.exp(lowest - least)
            top = top + scale * x[:, at + g * share:at + (g + 1) * share].astype(F32)
            bottom = bottom + scale * total
        means.append(top / bottom)
    return means


def make_first(parts, tiles, cells):
    def kernel(state, diff, pert, after, prior):
        nothing = jnp.zeros((1, LANES), F32)
        d = widen(diff[...], nothing, nothing)
        for p in range(parts):
            x = diffuse(widen(state[p].astype(F32), nothing, nothing), d)
            now = x[:, LANES:LANES + cells] + pert[0, p].astype(F32)
            prior[p * tiles:(p + 1) * tiles, :] = now.astype(BF16)

    return kernel


def make_send(pairs, rows):
    def kernel(own, other, trail, *refs):
        notes, sends, half = refs[:pairs], refs[pairs:2 * pairs], refs[2 * pairs]
        prior = jnp.concatenate([own[...], other[...]], axis=0)
        sent = requested([x[...] for x in notes], prior, 0, rows)
        for k in range(pairs):
            sends[k][...] = sent[k * rows:(k + 1) * rows, :].astype(BF16)
        size = padded(pairs)
        half[...] = jnp.zeros(half.shape, F32)
        for k in range(pairs):
            half[k:k + 1, :] = notes[k][...]
        half[size:, :] = trail[...]

    return kernel


def make_assess(pairs, parts, tiles, cells, share):
    size = padded(pairs)

    def kernel(own, other, low, high, where, terms, local, second, *refs):
        outs, stats, weighted_out, sums = refs[:pairs], refs[pairs], refs[pairs + 1], refs[pairs + 2]
        fixed = []
        for h, prior in enumerate((own, other)):
            for p in range(parts):
                row = (2 * p + h) * size
                x = prior[p * tiles:(p + 1) * tiles, :].astype(F32)
                x = patch(x, low[row:row + 1, LANES:], high[row:row + 1, :LANES])
                fixed.append(x.astype(BF16))
        least, total, weighted = assess(
            fixed, where[...], terms[0:1, :], terms[1:2, :], local[...], 2 * parts, tiles, cells
        )
        sums[...] = weighted
        pack_mean(outs, 0, least, total, sums, share)
        least, total, weighted = assess(
            [second[p * tiles:(p + 1) * tiles, :] for p in range(parts)],
            where[...], terms[0:1, :], terms[2:3, :], local[...], parts, tiles, cells,
        )
        stats[...] = jnp.where(iota((tiles, LANES), 1) == 0, least, total)
        weighted_out[...] = weighted

    return kernel


def make_second(pairs, parts, tiles, cells):
    size = padded(pairs)

    def kernel(keys, diff, pert, message, mine, theirs, after, *refs):
        got, prior, low_out, high_out = refs[:pairs], refs[pairs], refs[pairs + 1], refs[pairs + 2]
        below, above = halves(mine[...], theirs[...])
        low, high = edge_windows(message[...], below, above, size, parts)
        low_out[...] = low
        high_out[...] = high
        below, above = below[size:size + 8, :], above[size:size + 8, :]
        arrived = jnp.concatenate([x[...] for x in got], axis=0)
        moved = pick_rows(keys[0], arrived)
        here_codes = message[size + 2:size + 2 + 2 * parts, :].astype(I32)
        codes = jnp.concatenate([here_codes[parts:], below[2:2 + parts, :].astype(I32)], axis=0)
        start = pick_rows(codes, low.astype(BF16))
        codes = jnp.concatenate([here_codes[:parts], above[2 + parts:2 + 2 * parts, :].astype(I32)], axis=0)
        end = pick_rows(codes, high.astype(BF16))
        d = widen(diff[...], below[0:1, :], above[1:2, :])
        for p in range(parts):
            x = patch(moved[p * tiles:(p + 1) * tiles, :], start[p:p + 1, LANES:], end[p:p + 1, :LANES])
            q = parts + p
            x = widen(x, start[q:q + 1, :LANES], end[q:q + 1, LANES:])
            x = diffuse(x, d)[:, LANES:LANES + cells]
            prior[p * tiles:(p + 1) * tiles, :] = (x + pert[0, p].astype(F32)).astype(BF16)

    return kernel


def make_send_second(pairs, rows, parts, tiles, cells, share):
    def kernel(own, other, where, terms, local, stats, own_sums, *refs):
        notes, kept, outs, sums = refs[:pairs], refs[pairs:2 * pairs], refs[2 * pairs:3 * pairs], refs[3 * pairs]
        outs = [outs[falling(pairs).index(k)] for k in range(pairs)]
        prior = jnp.concatenate([own[...], other[...]], axis=0)
        sent = requested([x[...] for x in notes], prior, 1, rows)
        extra = kept[0].shape[1]
        for k in range(pairs):
            outs[k][:, :cells] = sent[k * rows:(k + 1) * rows, :].astype(BF16)
            outs[k][:, cells:cells + extra] = kept[k][...]
        least, total, weighted = assess(
            [other[p * tiles:(p + 1) * tiles, :] for p in range(parts)],
            where[...], terms[0:1, :], terms[2:3, :], local[...], parts, tiles, cells,
        )
        mine = stats[:, 0:1]
        lower = jnp.minimum(least, mine)
        scale, own_scale = jnp.exp(lower - least), jnp.exp(lower - mine)
        total = scale * total + own_scale * stats[:, 1:2]
        sums[...] = scale * weighted + own_scale * own_sums[...]
        least = lower
        pack_mean(outs, cells + extra, least, total, sums, share)

    return kernel


def make_last(pairs, rows, parts, tiles, cells):
    def kernel(keys, *refs):
        got, analysis, mean = refs[:pairs], refs[pairs], refs[pairs + 1]
        got = [got[falling(pairs).index(k)] for k in range(pairs)]
        arrived = jnp.concatenate([x[:, :cells] for x in got], axis=0)
        picked = pick_rows(keys[1], arrived)
        for p in range(parts):
            analysis[p] = picked[p * tiles:(p + 1) * tiles, :].astype(BF16)
        share = mean.shape[2]
        extra = tiles // rows * share + LANES
        for c in range(CYCLES):
            for g, x in enumerate(unpack_mean(got, cells + c * extra, tiles, share)):
                mean[c, g * rows:(g + 1) * rows, :] = x

    return kernel


def body(
    state,
    diffusivity,
    model_perturbation,
    obs_values,
    obs_prec,
    obs_tile,
    obs_cell,
    pattern,
    loc_weight,
    anc_member,
    anc_slot,
):
    parts, tiles, cells = state.shape
    members = lax.axis_size("member")
    regions = lax.axis_size("region")
    capacity = max(2, 2 * parts * tiles // members)
    share = cells // members
    pairs = members // 2
    rows = 2 * capacity
    extra = tiles // rows * share + LANES
    blocks, per_block = obs_cell.shape
    count = blocks * per_block
    member_of = anc_member.reshape(CYCLES, parts, tiles)
    slot_of = anc_slot.reshape(CYCLES, parts, tiles)
    near = pattern.shape[1]
    ends = cells // LANES - 1

    def block(shape, at):
        lead = (0,) * (len(shape) - 1)
        return pl.BlockSpec(shape, lambda i: lead + (at,))

    edges = [state, state, diffusivity, diffusivity, model_perturbation, model_perturbation, member_of, slot_of]
    *notes, trail, keys = call(
        make_prepare(members, capacity, parts, tiles),
        [((1, LANES), F32)] * pairs + [((8, LANES), F32), ((CYCLES, parts * tiles, LANES), I32)],
        [pltpu.with_memory_space_constraint(x, pltpu.HBM) for x in edges],
        [
            block((parts, tiles, LANES), 0),
            block((parts, tiles, LANES), ends),
            block((tiles, LANES), 0),
            block((tiles, LANES), ends),
            block((1, parts, tiles, LANES), 0),
            block((1, parts, tiles, LANES), ends),
            whole_spec(member_of.shape),
            whole_spec(slot_of.shape),
        ],
        name="prepare",
    )

    def trade(x):
        return lax.ppermute(x, "member", [(i, i ^ 1) for i in range(members)])

    def exchange(sends, order):
        got = [sends[0]]
        for x, k in list(zip(sends, order))[1:]:
            got.append(lax.ppermute(x, "member", [(i, i ^ (2 * k)) for i in range(members)]))
        return got

    notes = exchange(notes, range(pairs))

    where, terms, local = call(
        make_observe(blocks, per_block, tiles, near),
        [((2, count), I32), ((1 + CYCLES, count), F32), ((tiles, count), F32)],
        [obs_tile[None, :], obs_cell.T, obs_prec.T, jnp.swapaxes(obs_values, 1, 2), pattern.T, loc_weight.T],
        name="observe",
    )

    def noise_spec(c):
        return pl.BlockSpec((1, parts, tiles, cells), lambda i: (c, 0, 0, 0))

    args = [state, diffusivity, model_perturbation, trail]
    specs = [whole_spec(a.shape) for a in args]
    specs[2] = noise_spec(0)
    (prior,) = call(
        make_first(parts, tiles, cells), [((parts * tiles, cells), BF16)], args, specs, name="forecast_first"
    )
    other = trade(prior)
    size = padded(pairs)
    *sends, half = call(
        make_send(pairs, rows),
        [((rows, cells), BF16)] * pairs + [((size + trail.shape[0], LANES), F32)],
        [prior, other, trail, *notes],
        name="send_first",
    )
    got = exchange(sends, range(pairs))
    message = jnp.concatenate([half, trade(half)], axis=0)
    steps = []
    for i in range(members):
        first, last = (0, regions - 1) if i % 2 == 0 else (1, regions)
        steps += [(i * regions + r, i * regions + r + 1 - 2 * (i % 2)) for r in range(first, last)]
    mine = lax.ppermute(message, ("member", "region"), steps)
    theirs = trade(mine)
    window = ((parts * 2 * size, 2 * LANES), F32)
    sums = [((tiles, cells), F32)]
    args = [keys, diffusivity, model_perturbation, message, mine, theirs, where, *got]
    specs = [whole_spec(a.shape) for a in args]
    specs[2] = noise_spec(1)
    second, low, high = call(
        make_second(pairs, parts, tiles, cells),
        [((parts * tiles, cells), BF16), window, window],
        args,
        specs,
        name="forecast_second",
    )
    *kept, stats, own_sums = call(
        make_assess(pairs, parts, tiles, cells, share),
        [((rows, extra), BF16)] * pairs + [((tiles, LANES), F32), ((tiles, cells), F32)],
        [prior, other, low, high, where, terms, local, second],
        scratch=sums,
        name="assess_first",
    )
    sends = call(
        make_send_second(pairs, rows, parts, tiles, cells, share),
        [((rows, cells + CYCLES * extra), BF16)] * pairs,
        [second, trade(second), where, terms, local, stats, own_sums, *notes, *kept],
        scratch=sums,
        name="send_second",
    )
    got = exchange(sends, falling(pairs))
    return tuple(
        call(
            make_last(pairs, rows, parts, tiles, cells),
            [(state.shape, BF16), ((CYCLES, tiles, share), F32)],
            [keys, *got],
            name="finish",
        )
    )


def solution(mesh):
    in_specs = (
        P("member", "region", None),
        P("region", None),
        P(None, "member", "region", None),
        P(None, "region", None),
        P("region", None),
        P("region"),
        P("region", None),
        P("region", None),
        P("region", None),
        P(None, "region", "member", None, None),
        P(None, "region", "member", None),
    )
    out_specs = (P("member", "region", None), P(None, "region", "member"))
    return jax.shard_map(body, mesh=mesh, in_specs=in_specs, out_specs=out_specs, check_vma=False)
```

```python
import jax
import jax.numpy as jnp
from jax import lax
from jax.experimental import pallas as pl
from jax.experimental.pallas import tpu as pltpu
from jax.sharding import PartitionSpec as P

CYCLES = 2
STEPS = 2
LANES = 128
F32 = jnp.float32
BF16 = jnp.bfloat16
I32 = jnp.int32
PARAMS = pltpu.CompilerParams(vmem_limit_bytes=48 * 1024 * 1024)


def iota(shape, dim):
    return lax.broadcasted_iota(I32, shape, dim)


def whole_spec(shape):
    zeros = (0,) * len(shape)
    return pl.BlockSpec(shape, lambda i: zeros)


def call(kernel, outs, args, specs=None, scratch=(), name=None):
    specs = specs or [whole_spec(a.shape) for a in args]
    return pl.pallas_call(
        kernel,
        out_shape=[jax.ShapeDtypeStruct(s, d) for s, d in outs],
        grid=(1,),
        in_specs=specs,
        out_specs=[whole_spec(s) for s, _ in outs],
        scratch_shapes=[pltpu.VMEM(s, d) for s, d in scratch],
        compiler_params=PARAMS,
        name=name,
    )(*args)


def column_of(row):
    n = row.shape[1]
    square = jnp.broadcast_to(row, (n, n))
    return jnp.sum(jnp.where(iota((n, n), 0) == iota((n, n), 1), square, 0), axis=1, keepdims=True)


def here():
    return lax.axis_index("member")


EDGE_AT = 32
STRIDE = 8


def falling(pairs):
    return [0, 1, *range(pairs - 1, 1, -1)]


def padded(pairs):
    return max(8, pairs)


def make_prepare(members, capacity, parts, tiles):
    width = 2 * STEPS
    pairs = members // 2
    rows = parts * tiles

    def kernel(st0, st1, df0, df1, pb0, pb1, am, slot, *outs):
        notes, trail, keys = outs[:pairs], outs[pairs], outs[pairs + 1]
        m = here()
        lane = iota((1, LANES), 1)
        last = tiles - 1
        trail[...] = jnp.zeros(trail.shape, F32)
        trail[0:1, :] = df1[last:last + 1, :]
        trail[1:2, :] = df0[0:1, :]
        edge = jnp.zeros((1, LANES), F32)
        for p in range(parts):
            for i, t in enumerate((last, 0)):
                source = am[0, p:p + 1, t:t + 1] ^ m
                code = (slot[0, p:p + 1, t:t + 1] * 2 + source % 2) * padded(pairs) + source // 2
                row = 2 + i * parts + p
                trail[row:row + 1, :] = jnp.broadcast_to(code.astype(F32), (1, LANES))
            fields = (st1[p, last:last + 1, :], st0[p, 0:1, :], pb1[0, p, last:last + 1, :], pb0[0, p, 0:1, :])
            for i, x in enumerate(fields):
                to = EDGE_AT + STRIDE * (4 * p + i)
                start = 0 if i % 2 else LANES - width
                moved = pltpu.roll(x.astype(F32), (to - start) % LANES, 1)
                edge = jnp.where((lane >= to) & (lane < to + width), moved, edge)
        before = (iota((tiles, tiles), 0) < iota((tiles, tiles), 1)).astype(F32)
        asked = jnp.zeros((pairs, LANES), F32)
        for c in range(CYCLES):
            seen = jnp.zeros((members, 1), F32)
            for p in range(parts):
                source = am[c, p:p + 1, :] ^ m
                named = (iota((members, tiles), 0) == source).astype(F32)
                earlier = seen + jnp.dot(named, before, preferred_element_type=F32)
                rank = jnp.sum(named * earlier, axis=0, keepdims=True).astype(I32)
                seen = seen + jnp.sum(named, axis=1, keepdims=True)
                half = source % 2
                code = half * rows + slot[c, p:p + 1, :] * tiles + iota((1, tiles), 1)
                spot = (iota((LANES, tiles), 0) == (2 * c + half) * capacity + rank).astype(F32)
                pair = jnp.where(iota((pairs, tiles), 0) == source // 2, (code + 1).astype(F32), 0.0)
                asked = asked + lax.dot_general(pair, spot, (((1,), (1,)), ((), ())), preferred_element_type=F32)
                column = column_of(source * capacity + rank)
                keys[c, p * tiles:(p + 1) * tiles, :] = jnp.broadcast_to(column, (tiles, LANES))
        for k in range(pairs):
            notes[k][...] = jnp.where(lane < EDGE_AT, asked[k:k + 1, :] - 1.0, edge)

    return kernel


def halves(mine, theirs):
    half = theirs.shape[0] // 2
    theirs = jnp.concatenate([theirs[half:, :], theirs[:half, :]], axis=0)
    first = jnp.broadcast_to(here() % 2, mine.shape) == 0
    return jnp.where(first, mine, theirs), jnp.where(first, theirs, mine)


def edge_windows(own, below, above, size, parts):
    width = 2 * STEPS

    def field(note, p, i):
        at = EDGE_AT + STRIDE * (4 * p + i)
        start = 0 if i % 2 else LANES - width
        both = jnp.concatenate([note[:size, :], note[size + 8:2 * size + 8, :]], axis=0)
        return pltpu.roll(both, (start - at) % LANES, 1)

    low, high = [], []
    for out, before, after in ((low, below, own), (high, own, above)):
        d = jnp.concatenate([before[size:size + 1, :], after[size + 1:size + 2, :]], axis=1)
        for p in range(parts):
            x = jnp.concatenate([field(before, p, 0), field(after, p, 1)], axis=1)
            x = diffuse(x, d) + jnp.concatenate([field(before, p, 2), field(after, p, 3)], axis=1)
            out.append(x.astype(BF16).astype(F32))
    return jnp.concatenate(low, axis=0), jnp.concatenate(high, axis=0)


def patch(x, first, last):
    tiles = x.shape[0]
    row, lane = iota((tiles, LANES), 0), iota((tiles, LANES), 1)
    head = jnp.where((row == 0) & (lane < STEPS), first, x[:, :LANES])
    tail = jnp.where((row == tiles - 1) & (lane >= LANES - STEPS), last, x[:, -LANES:])
    return jnp.concatenate([head, x[:, LANES:-LANES], tail], axis=1)


def widen(x, left, right):
    tiles = x.shape[0]
    row = iota((tiles, LANES), 0)
    before = jnp.where(row == 0, left, pltpu.roll(x[:, -LANES:], 1, 0))
    after = jnp.where(row == tiles - 1, right, pltpu.roll(x[:, :LANES], tiles - 1, 0))
    return jnp.concatenate([before, x, after], axis=1)


def diffuse(x, d):
    n = x.shape[1]
    for _ in range(STEPS):
        x = x + d * (pltpu.roll(x, 1, 1) - 2.0 * x + pltpu.roll(x, n - 1, 1))
    return x


def pick_rows(wanted, rows):
    m = rows.shape[0]
    n = wanted.shape[0]
    choice = (wanted[:, :m] == iota((n, m), 1)).astype(F32).astype(BF16)
    return jnp.dot(choice, rows, preferred_element_type=F32)


def requested(notes, prior, cycle, rows):
    pairs = len(notes)
    total = pairs * rows
    asked = jnp.concatenate(notes, axis=0)
    spread = jnp.broadcast_to(asked[:, None, :], (pairs, rows, LANES)).reshape(total, LANES)
    mine = iota((total, LANES), 1) == cycle * rows + iota((total, LANES), 0) % rows
    wanted = jnp.sum(jnp.where(mine, spread, 0.0), axis=1, keepdims=True).astype(I32)
    return pick_rows(jnp.broadcast_to(wanted, (total, LANES)), prior)


def make_observe(blocks, per_block, tiles, near):
    count = blocks * per_block

    def kernel(tile, cell, prec, value, pattern, weight, where, terms, local):
        def line(x):
            wide = jnp.concatenate([x] * per_block, axis=1)
            own = iota((per_block, count), 1) // blocks == iota((per_block, count), 0)
            return jnp.sum(jnp.where(own, wide, 0), axis=0, keepdims=True)

        at = line(cell[...])
        row = (at // LANES) * tiles + jnp.concatenate([tile[...]] * per_block, axis=1)
        pick = iota((2, count), 0) == 0
        where[...] = jnp.where(pick, row, at % LANES)
        terms[0:1, :] = line(prec[...])
        for c in range(CYCLES):
            terms[c + 1:c + 2, :] = line(value[c])
        group = iota((tiles, count), 1) % blocks
        total = jnp.zeros((tiles, count), F32)
        for k in range(near):
            total = total + jnp.where(column_of(pattern[k:k + 1, :]) == group, column_of(weight[k:k + 1, :]), 0.0)
        local[...] = total

    return kernel


def assess(prior, where, prec, value, local, parts, tiles, cells):
    blocks = cells // LANES
    rows = tiles * blocks
    count = where.shape[1]
    stacked = jnp.concatenate(
        [jnp.concatenate([x[:, k * LANES:(k + 1) * LANES] for k in range(blocks)], axis=0) for x in prior],
        axis=1,
    )
    choice = (iota((rows, count), 0) == where[0:1, :]).astype(F32).astype(BF16)
    lines = lax.dot_general(stacked, choice, (((0,), (0,)), ((), ())), preferred_element_type=F32)
    lane = iota((LANES, count), 0) == where[1:2, :]
    score = []
    for p in range(parts):
        predicted = jnp.sum(jnp.where(lane, lines[p * LANES:(p + 1) * LANES, :], 0.0), axis=0, keepdims=True)
        miss = value - predicted
        term = 0.5 * (prec * miss * miss)
        score.append(jnp.sum(local * term, axis=1, keepdims=True))
    least = score[0]
    for s in score[1:]:
        least = jnp.minimum(least, s)
    scale = [jnp.exp(least - s) for s in score]
    total = scale[0]
    for s in scale[1:]:
        total = total + s
    weighted = scale[0] * prior[0].astype(F32)
    for s, x in zip(scale[1:], prior[1:]):
        weighted = weighted + s * x.astype(F32)
    return least, total, weighted


def pieces(x):
    high = x.astype(BF16).astype(F32)
    middle = (x - high).astype(BF16).astype(F32)
    low = (x - high - middle).astype(BF16).astype(F32)
    return high, middle, low


def share_of(ref, member, share):
    if share % LANES == 0:
        return ref[:, pl.ds(pl.multiple_of(member * share, LANES), share)]
    return pltpu.roll(ref[...], ref.shape[1] - member * share, 1)[:, :share]


def pack_mean(outs, at, least, total, sums, share):
    rows = outs[0].shape[0]
    tiles = sums.shape[0]
    groups = tiles // rows
    m = here()
    lane = iota((rows, LANES), 1)
    misc = jnp.zeros((rows, LANES), F32)
    spot = 0
    for x in (least, total):
        for piece in pieces(x):
            for g in range(groups):
                misc = jnp.where(lane == spot, piece[g * rows:(g + 1) * rows, :], misc)
                spot += 1
    end = at + groups * share
    for k, out in enumerate(outs):
        block = share_of(sums, m ^ (2 * k), share)
        for g in range(groups):
            out[:, at + g * share:at + (g + 1) * share] = block[g * rows:(g + 1) * rows, :].astype(BF16)
        out[:, end:end + LANES] = misc.astype(BF16)


def unpack_mean(got, at, tiles, share):
    rows = got[0].shape[0]
    groups = tiles // rows
    end = at + groups * share
    misc = [x[:, end:end + LANES].astype(F32) for x in got]
    means = []
    for g in range(groups):
        stats = []
        for x in misc:
            pair = []
            for kind in range(2):
                spot = [(kind * 3 + piece) * groups + g for piece in range(3)]
                high, middle, low = [x[:, i:i + 1] for i in spot]
                pair.append(high + middle + low)
            stats.append(pair)
        lowest = stats[0][0]
        for least, _ in stats[1:]:
            lowest = jnp.minimum(lowest, least)
        top, bottom = 0.0, 0.0
        for x, (least, total) in zip(got, stats):
            scale = jnp.exp(lowest - least)
            top = top + scale * x[:, at + g * share:at + (g + 1) * share].astype(F32)
            bottom = bottom + scale * total
        means.append(top / bottom)
    return means


def make_first(parts, tiles, cells):
    def kernel(state, diff, pert, after, prior):
        nothing = jnp.zeros((1, LANES), F32)
        d = widen(diff[...], nothing, nothing)
        for p in range(parts):
            x = diffuse(widen(state[p].astype(F32), nothing, nothing), d)
            now = x[:, LANES:LANES + cells] + pert[0, p].astype(F32)
            prior[p * tiles:(p + 1) * tiles, :] = now.astype(BF16)

    return kernel


def make_send(pairs, rows):
    def kernel(own, other, trail, *refs):
        notes, sends, half = refs[:pairs], refs[pairs:2 * pairs], refs[2 * pairs]
        prior = jnp.concatenate([own[...], other[...]], axis=0)
        sent = requested([x[...] for x in notes], prior, 0, rows)
        for k in range(pairs):
            sends[k][...] = sent[k * rows:(k + 1) * rows, :].astype(BF16)
        size = padded(pairs)
        half[...] = jnp.zeros(half.shape, F32)
        for k in range(pairs):
            half[k:k + 1, :] = notes[k][...]
        half[size:, :] = trail[...]

    return kernel


def make_assess(pairs, parts, tiles, cells, share):
    size = padded(pairs)

    def kernel(own, other, low, high, where, terms, local, second, *refs):
        outs, stats, weighted_out, sums = refs[:pairs], refs[pairs], refs[pairs + 1], refs[pairs + 2]
        fixed = []
        for h, prior in enumerate((own, other)):
            for p in range(parts):
                row = (2 * p + h) * size
                x = prior[p * tiles:(p + 1) * tiles, :].astype(F32)
                x = patch(x, low[row:row + 1, LANES:], high[row:row + 1, :LANES])
                fixed.append(x.astype(BF16))
        least, total, weighted = assess(
            fixed, where[...], terms[0:1, :], terms[1:2, :], local[...], 2 * parts, tiles, cells
        )
        sums[...] = weighted
        pack_mean(outs, 0, least, total, sums, share)
        least, total, weighted = assess(
            [second[p * tiles:(p + 1) * tiles, :] for p in range(parts)],
            where[...], terms[0:1, :], terms[2:3, :], local[...], parts, tiles, cells,
        )
        stats[...] = jnp.where(iota((tiles, LANES), 1) == 0, least, total)
        weighted_out[...] = weighted

    return kernel


def make_second(pairs, parts, tiles, cells):
    size = padded(pairs)

    def kernel(keys, diff, pert, message, mine, theirs, after, *refs):
        got, prior, low_out, high_out = refs[:pairs], refs[pairs], refs[pairs + 1], refs[pairs + 2]
        below, above = halves(mine[...], theirs[...])
        low, high = edge_windows(message[...], below, above, size, parts)
        low_out[...] = low
        high_out[...] = high
        below, above = below[size:size + 8, :], above[size:size + 8, :]
        arrived = jnp.concatenate([x[...] for x in got], axis=0)
        moved = pick_rows(keys[0], arrived)
        here_codes = message[size + 2:size + 2 + 2 * parts, :].astype(I32)
        codes = jnp.concatenate([here_codes[parts:], below[2:2 + parts, :].astype(I32)], axis=0)
        start = pick_rows(codes, low.astype(BF16))
        codes = jnp.concatenate([here_codes[:parts], above[2 + parts:2 + 2 * parts, :].astype(I32)], axis=0)
        end = pick_rows(codes, high.astype(BF16))
        d = widen(diff[...], below[0:1, :], above[1:2, :])
        for p in range(parts):
            x = patch(moved[p * tiles:(p + 1) * tiles, :], start[p:p + 1, LANES:], end[p:p + 1, :LANES])
            q = parts + p
            x = widen(x, start[q:q + 1, :LANES], end[q:q + 1, LANES:])
            x = diffuse(x, d)[:, LANES:LANES + cells]
            prior[p * tiles:(p + 1) * tiles, :] = (x + pert[0, p].astype(F32)).astype(BF16)

    return kernel


def make_send_second(pairs, rows, parts, tiles, cells, share):
    def kernel(own, other, where, terms, local, stats, own_sums, *refs):
        notes, kept, outs, sums = refs[:pairs], refs[pairs:2 * pairs], refs[2 * pairs:3 * pairs], refs[3 * pairs]
        outs = [outs[falling(pairs).index(k)] for k in range(pairs)]
        prior = jnp.concatenate([own[...], other[...]], axis=0)
        sent = requested([x[...] for x in notes], prior, 1, rows)
        extra = kept[0].shape[1]
        for k in range(pairs):
            outs[k][:, :cells] = sent[k * rows:(k + 1) * rows, :].astype(BF16)
            outs[k][:, cells:cells + extra] = kept[k][...]
        least, total, weighted = assess(
            [other[p * tiles:(p + 1) * tiles, :] for p in range(parts)],
            where[...], terms[0:1, :], terms[2:3, :], local[...], parts, tiles, cells,
        )
        mine = stats[:, 0:1]
        lower = jnp.minimum(least, mine)
        scale, own_scale = jnp.exp(lower - least), jnp.exp(lower - mine)
        total = scale * total + own_scale * stats[:, 1:2]
        sums[...] = scale * weighted + own_scale * own_sums[...]
        least = lower
        pack_mean(outs, cells + extra, least, total, sums, share)

    return kernel


def make_last(pairs, rows, parts, tiles, cells):
    pieces_of = 4
    piece = cells // pieces_of

    def kernel(keys, *refs):
        got, (analysis, mean, buffer, sems) = refs[:pairs], refs[pairs:]
        got = [got[falling(pairs).index(k)] for k in range(pairs)]
        copies = []
        for i in range(pieces_of):
            cut = slice(i * piece, (i + 1) * piece)
            picked = pick_rows(keys[1], jnp.concatenate([x[:, cut] for x in got], axis=0))
            for p in range(parts):
                buffer[p, :, cut] = picked[p * tiles:(p + 1) * tiles, :].astype(BF16)
            copies.append(pltpu.make_async_copy(buffer.at[:, :, cut], analysis.at[:, :, cut], sems.at[i]))
            copies[-1].start()
        share = mean.shape[2]
        extra = tiles // rows * share + LANES
        for c in range(CYCLES):
            for g, x in enumerate(unpack_mean(got, cells + c * extra, tiles, share)):
                mean[c, g * rows:(g + 1) * rows, :] = x
        for copy in copies:
            copy.wait()

    return kernel


def body(
    state,
    diffusivity,
    model_perturbation,
    obs_values,
    obs_prec,
    obs_tile,
    obs_cell,
    pattern,
    loc_weight,
    anc_member,
    anc_slot,
):
    parts, tiles, cells = state.shape
    members = lax.axis_size("member")
    regions = lax.axis_size("region")
    capacity = max(2, 2 * parts * tiles // members)
    share = cells // members
    pairs = members // 2
    rows = 2 * capacity
    extra = tiles // rows * share + LANES
    blocks, per_block = obs_cell.shape
    count = blocks * per_block
    member_of = anc_member.reshape(CYCLES, parts, tiles)
    slot_of = anc_slot.reshape(CYCLES, parts, tiles)
    near = pattern.shape[1]
    ends = cells // LANES - 1

    def block(shape, at):
        lead = (0,) * (len(shape) - 1)
        return pl.BlockSpec(shape, lambda i: lead + (at,))

    edges = [state, state, diffusivity, diffusivity, model_perturbation, model_perturbation, member_of, slot_of]
    *notes, trail, keys = call(
        make_prepare(members, capacity, parts, tiles),
        [((1, LANES), F32)] * pairs + [((8, LANES), F32), ((CYCLES, parts * tiles, LANES), I32)],
        [pltpu.with_memory_space_constraint(x, pltpu.HBM) for x in edges],
        [
            block((parts, tiles, LANES), 0),
            block((parts, tiles, LANES), ends),
            block((tiles, LANES), 0),
            block((tiles, LANES), ends),
            block((1, parts, tiles, LANES), 0),
            block((1, parts, tiles, LANES), ends),
            whole_spec(member_of.shape),
            whole_spec(slot_of.shape),
        ],
        name="prepare",
    )

    def trade(x):
        return lax.ppermute(x, "member", [(i, i ^ 1) for i in range(members)])

    def exchange(sends, order):
        got = [sends[0]]
        for x, k in list(zip(sends, order))[1:]:
            got.append(lax.ppermute(x, "member", [(i, i ^ (2 * k)) for i in range(members)]))
        return got

    notes = exchange(notes, range(pairs))

    where, terms, local = call(
        make_observe(blocks, per_block, tiles, near),
        [((2, count), I32), ((1 + CYCLES, count), F32), ((tiles, count), F32)],
        [obs_tile[None, :], obs_cell.T, obs_prec.T, jnp.swapaxes(obs_values, 1, 2), pattern.T, loc_weight.T],
        name="observe",
    )

    def noise_spec(c):
        return pl.BlockSpec((1, parts, tiles, cells), lambda i: (c, 0, 0, 0))

    args = [state, diffusivity, model_perturbation, trail]
    specs = [whole_spec(a.shape) for a in args]
    specs[2] = noise_spec(0)
    (prior,) = call(
        make_first(parts, tiles, cells), [((parts * tiles, cells), BF16)], args, specs, name="forecast_first"
    )
    other = trade(prior)
    size = padded(pairs)
    *sends, half = call(
        make_send(pairs, rows),
        [((rows, cells), BF16)] * pairs + [((size + trail.shape[0], LANES), F32)],
        [prior, other, trail, *notes],
        name="send_first",
    )
    got = exchange(sends, range(pairs))
    message = jnp.concatenate([half, trade(half)], axis=0)
    steps = []
    for i in range(members):
        first, last = (0, regions - 1) if i % 2 == 0 else (1, regions)
        steps += [(i * regions + r, i * regions + r + 1 - 2 * (i % 2)) for r in range(first, last)]
    mine = lax.ppermute(message, ("member", "region"), steps)
    theirs = trade(mine)
    window = ((parts * 2 * size, 2 * LANES), F32)
    sums = [((tiles, cells), F32)]
    args = [keys, diffusivity, model_perturbation, message, mine, theirs, where, *got]
    specs = [whole_spec(a.shape) for a in args]
    specs[2] = noise_spec(1)
    second, low, high = call(
        make_second(pairs, parts, tiles, cells),
        [((parts * tiles, cells), BF16), window, window],
        args,
        specs,
        name="forecast_second",
    )
    *kept, stats, own_sums = call(
        make_assess(pairs, parts, tiles, cells, share),
        [((rows, extra), BF16)] * pairs + [((tiles, LANES), F32), ((tiles, cells), F32)],
        [prior, other, low, high, where, terms, local, second],
        scratch=sums,
        name="assess_first",
    )
    sends = call(
        make_send_second(pairs, rows, parts, tiles, cells, share),
        [((rows, cells + CYCLES * extra), BF16)] * pairs,
        [second, trade(second), where, terms, local, stats, own_sums, *notes, *kept],
        scratch=sums,
        name="send_second",
    )
    got = exchange(sends, falling(pairs))
    mean_shape = (CYCLES, tiles, share)
    args = [keys, *got]
    return tuple(
        pl.pallas_call(
            make_last(pairs, rows, parts, tiles, cells),
            out_shape=[jax.ShapeDtypeStruct(state.shape, BF16), jax.ShapeDtypeStruct(mean_shape, F32)],
            grid=(1,),
            in_specs=[whole_spec(a.shape) for a in args],
            out_specs=[pl.BlockSpec(memory_space=pl.ANY), whole_spec(mean_shape)],
            scratch_shapes=[pltpu.VMEM(state.shape, BF16), pltpu.SemaphoreType.DMA((4,))],
            compiler_params=PARAMS,
            name="finish",
        )(*args)
    )


def solution(mesh):
    in_specs = (
        P("member", "region", None),
        P("region", None),
        P(None, "member", "region", None),
        P(None, "region", None),
        P("region", None),
        P("region"),
        P("region", None),
        P("region", None),
        P("region", None),
        P(None, "region", "member", None, None),
        P(None, "region", "member", None),
    )
    out_specs = (P("member", "region", None), P(None, "region", "member"))
    return jax.shard_map(body, mesh=mesh, in_specs=in_specs, out_specs=out_specs, check_vma=False)
```

```python
import jax
import jax.numpy as jnp
from jax import lax
from jax.experimental import pallas as pl
from jax.experimental.pallas import tpu as pltpu
from jax.sharding import PartitionSpec as P

CYCLES = 2
STEPS = 2
LANES = 128
F32 = jnp.float32
BF16 = jnp.bfloat16
I32 = jnp.int32
PARAMS = pltpu.CompilerParams(vmem_limit_bytes=48 * 1024 * 1024)


def iota(shape, dim):
    return lax.broadcasted_iota(I32, shape, dim)


def whole_spec(shape):
    zeros = (0,) * len(shape)
    return pl.BlockSpec(shape, lambda i: zeros)


def call(kernel, outs, args, specs=None, scratch=(), name=None):
    specs = specs or [whole_spec(a.shape) for a in args]
    return pl.pallas_call(
        kernel,
        out_shape=[jax.ShapeDtypeStruct(s, d) for s, d in outs],
        grid=(1,),
        in_specs=specs,
        out_specs=[whole_spec(s) for s, _ in outs],
        scratch_shapes=[pltpu.VMEM(s, d) for s, d in scratch],
        compiler_params=PARAMS,
        name=name,
    )(*args)


def column_of(row):
    n = row.shape[1]
    square = jnp.broadcast_to(row, (n, n))
    return jnp.sum(jnp.where(iota((n, n), 0) == iota((n, n), 1), square, 0), axis=1, keepdims=True)


def here():
    return lax.axis_index("member")


EDGE_AT = 32
STRIDE = 8


def falling(pairs):
    return [0, *range(pairs - 1, 0, -1)]


def padded(pairs):
    return max(8, pairs)


def make_prepare(members, capacity, parts, tiles):
    width = 2 * STEPS
    pairs = members // 2
    rows = parts * tiles

    def kernel(st0, st1, df0, df1, pb0, pb1, am, slot, *outs):
        notes, trail, keys = outs[:pairs], outs[pairs], outs[pairs + 1]
        m = here()
        lane = iota((1, LANES), 1)
        last = tiles - 1
        trail[...] = jnp.zeros(trail.shape, F32)
        trail[0:1, :] = df1[last:last + 1, :]
        trail[1:2, :] = df0[0:1, :]
        edge = jnp.zeros((1, LANES), F32)
        for p in range(parts):
            for i, t in enumerate((last, 0)):
                source = am[0, p:p + 1, t:t + 1] ^ m
                code = (slot[0, p:p + 1, t:t + 1] * 2 + source % 2) * padded(pairs) + source // 2
                row = 2 + i * parts + p
                trail[row:row + 1, :] = jnp.broadcast_to(code.astype(F32), (1, LANES))
            fields = (st1[p, last:last + 1, :], st0[p, 0:1, :], pb1[0, p, last:last + 1, :], pb0[0, p, 0:1, :])
            for i, x in enumerate(fields):
                to = EDGE_AT + STRIDE * (4 * p + i)
                start = 0 if i % 2 else LANES - width
                moved = pltpu.roll(x.astype(F32), (to - start) % LANES, 1)
                edge = jnp.where((lane >= to) & (lane < to + width), moved, edge)
        before = (iota((tiles, tiles), 0) < iota((tiles, tiles), 1)).astype(F32)
        asked = jnp.zeros((pairs, LANES), F32)
        sources = [[am[c, p:p + 1, :] ^ m for p in range(parts)] for c in range(CYCLES)]
        every = [(iota((members, tiles), 0) == x).astype(F32) for some in sources for x in some]
        earlier_all = jnp.dot(jnp.concatenate(every, axis=0), before, preferred_element_type=F32)
        for c in range(CYCLES):
            seen = jnp.zeros((members, 1), F32)
            for p in range(parts):
                source = sources[c][p]
                at = c * parts + p
                named = every[at]
                earlier = seen + earlier_all[at * members:(at + 1) * members, :]
                rank = jnp.sum(named * earlier, axis=0, keepdims=True).astype(I32)
                seen = seen + jnp.sum(named, axis=1, keepdims=True)
                half = source % 2
                code = half * rows + slot[c, p:p + 1, :] * tiles + iota((1, tiles), 1)
                spot = (iota((LANES, tiles), 0) == (2 * c + half) * capacity + rank).astype(F32)
                pair = jnp.where(iota((pairs, tiles), 0) == source // 2, (code + 1).astype(F32), 0.0)
                asked = asked + lax.dot_general(pair, spot, (((1,), (1,)), ((), ())), preferred_element_type=F32)
                column = column_of(source * capacity + rank)
                keys[c, p * tiles:(p + 1) * tiles, :] = jnp.broadcast_to(column, (tiles, LANES))
        for k in range(pairs):
            notes[k][...] = jnp.where(lane < EDGE_AT, asked[k:k + 1, :] - 1.0, edge)

    return kernel


def halves(mine, theirs):
    half = theirs.shape[0] // 2
    theirs = jnp.concatenate([theirs[half:, :], theirs[:half, :]], axis=0)
    first = jnp.broadcast_to(here() % 2, mine.shape) == 0
    return jnp.where(first, mine, theirs), jnp.where(first, theirs, mine)


def edge_windows(own, below, above, size, parts):
    width = 2 * STEPS

    def field(note, p, i):
        at = EDGE_AT + STRIDE * (4 * p + i)
        start = 0 if i % 2 else LANES - width
        both = jnp.concatenate([note[:size, :], note[size + 8:2 * size + 8, :]], axis=0)
        return pltpu.roll(both, (start - at) % LANES, 1)

    low, high = [], []
    for out, before, after in ((low, below, own), (high, own, above)):
        d = jnp.concatenate([before[size:size + 1, :], after[size + 1:size + 2, :]], axis=1)
        for p in range(parts):
            x = jnp.concatenate([field(before, p, 0), field(after, p, 1)], axis=1)
            x = diffuse(x, d) + jnp.concatenate([field(before, p, 2), field(after, p, 3)], axis=1)
            out.append(x.astype(BF16).astype(F32))
    return jnp.concatenate(low, axis=0), jnp.concatenate(high, axis=0)


def patch(x, first, last):
    tiles = x.shape[0]
    row, lane = iota((tiles, LANES), 0), iota((tiles, LANES), 1)
    head = jnp.where((row == 0) & (lane < STEPS), first, x[:, :LANES])
    tail = jnp.where((row == tiles - 1) & (lane >= LANES - STEPS), last, x[:, -LANES:])
    return jnp.concatenate([head, x[:, LANES:-LANES], tail], axis=1)


def widen(x, left, right):
    tiles = x.shape[0]
    row = iota((tiles, LANES), 0)
    before = jnp.where(row == 0, left, pltpu.roll(x[:, -LANES:], 1, 0))
    after = jnp.where(row == tiles - 1, right, pltpu.roll(x[:, :LANES], tiles - 1, 0))
    return jnp.concatenate([before, x, after], axis=1)


def diffuse(x, d):
    n = x.shape[1]
    for _ in range(STEPS):
        x = x + d * (pltpu.roll(x, 1, 1) - 2.0 * x + pltpu.roll(x, n - 1, 1))
    return x


def pick_rows(wanted, rows):
    m = rows.shape[0]
    n = wanted.shape[0]
    choice = (wanted[:, :m] == iota((n, m), 1)).astype(F32).astype(BF16)
    return jnp.dot(choice, rows, preferred_element_type=F32)


def requested(notes, prior, cycle, rows):
    pairs = len(notes)
    total = pairs * rows
    asked = jnp.concatenate(notes, axis=0)
    spread = jnp.broadcast_to(asked[:, None, :], (pairs, rows, LANES)).reshape(total, LANES)
    mine = iota((total, LANES), 1) == cycle * rows + iota((total, LANES), 0) % rows
    wanted = jnp.sum(jnp.where(mine, spread, 0.0), axis=1, keepdims=True).astype(I32)
    return pick_rows(jnp.broadcast_to(wanted, (total, LANES)), prior)


def make_observe(blocks, per_block, tiles, near):
    count = blocks * per_block

    def kernel(tile, cell, prec, value, pattern, weight, where, terms, local):
        def line(x):
            wide = jnp.concatenate([x] * per_block, axis=1)
            own = iota((per_block, count), 1) // blocks == iota((per_block, count), 0)
            return jnp.sum(jnp.where(own, wide, 0), axis=0, keepdims=True)

        at = line(cell[...])
        row = (at // LANES) * tiles + jnp.concatenate([tile[...]] * per_block, axis=1)
        pick = iota((2, count), 0) == 0
        where[...] = jnp.where(pick, row, at % LANES)
        terms[0:1, :] = line(prec[...])
        for c in range(CYCLES):
            terms[c + 1:c + 2, :] = line(value[c])
        group = iota((tiles, count), 1) % blocks
        total = jnp.zeros((tiles, count), F32)
        for k in range(near):
            total = total + jnp.where(column_of(pattern[k:k + 1, :]) == group, column_of(weight[k:k + 1, :]), 0.0)
        local[...] = total

    return kernel


def assess(prior, where, prec, value, local, parts, tiles, cells):
    blocks = cells // LANES
    rows = tiles * blocks
    count = where.shape[1]
    stacked = jnp.concatenate(
        [jnp.concatenate([x[:, k * LANES:(k + 1) * LANES] for k in range(blocks)], axis=0) for x in prior],
        axis=1,
    )
    choice = (iota((rows, count), 0) == where[0:1, :]).astype(F32).astype(BF16)
    lines = lax.dot_general(stacked, choice, (((0,), (0,)), ((), ())), preferred_element_type=F32)
    lane = iota((LANES, count), 0) == where[1:2, :]
    score = []
    for p in range(parts):
        predicted = jnp.sum(jnp.where(lane, lines[p * LANES:(p + 1) * LANES, :], 0.0), axis=0, keepdims=True)
        miss = value - predicted
        term = 0.5 * (prec * miss * miss)
        score.append(jnp.sum(local * term, axis=1, keepdims=True))
    least = score[0]
    for s in score[1:]:
        least = jnp.minimum(least, s)
    scale = [jnp.exp(least - s) for s in score]
    total = scale[0]
    for s in scale[1:]:
        total = total + s
    weighted = scale[0] * prior[0].astype(F32)
    for s, x in zip(scale[1:], prior[1:]):
        weighted = weighted + s * x.astype(F32)
    return least, total, weighted


def pieces(x):
    high = x.astype(BF16).astype(F32)
    middle = (x - high).astype(BF16).astype(F32)
    low = (x - high - middle).astype(BF16).astype(F32)
    return high, middle, low


def share_of(ref, member, share):
    if share % LANES == 0:
        return ref[:, pl.ds(pl.multiple_of(member * share, LANES), share)]
    return pltpu.roll(ref[...], ref.shape[1] - member * share, 1)[:, :share]


def pack_mean(outs, at, least, total, sums, share):
    rows = outs[0].shape[0]
    tiles = sums.shape[0]
    groups = tiles // rows
    m = here()
    lane = iota((rows, LANES), 1)
    misc = jnp.zeros((rows, LANES), F32)
    spot = 0
    for x in (least, total):
        for piece in pieces(x):
            for g in range(groups):
                misc = jnp.where(lane == spot, piece[g * rows:(g + 1) * rows, :], misc)
                spot += 1
    end = at + groups * share
    for k, out in enumerate(outs):
        block = share_of(sums, m ^ (2 * k), share)
        for g in range(groups):
            out[:, at + g * share:at + (g + 1) * share] = block[g * rows:(g + 1) * rows, :].astype(BF16)
        out[:, end:end + LANES] = misc.astype(BF16)


def unpack_mean(got, at, tiles, share):
    rows = got[0].shape[0]
    groups = tiles // rows
    end = at + groups * share
    misc = [x[:, end:end + LANES].astype(F32) for x in got]
    means = []
    for g in range(groups):
        stats = []
        for x in misc:
            pair = []
            for kind in range(2):
                spot = [(kind * 3 + piece) * groups + g for piece in range(3)]
                high, middle, low = [x[:, i:i + 1] for i in spot]
                pair.append(high + middle + low)
            stats.append(pair)
        lowest = stats[0][0]
        for least, _ in stats[1:]:
            lowest = jnp.minimum(lowest, least)
        top, bottom = 0.0, 0.0
        for x, (least, total) in zip(got, stats):
            scale = jnp.exp(lowest - least)
            top = top + scale * x[:, at + g * share:at + (g + 1) * share].astype(F32)
            bottom = bottom + scale * total
        means.append(top / bottom)
    return means


def make_first(parts, tiles, cells):
    def kernel(state, diff, pert, after, prior):
        nothing = jnp.zeros((1, LANES), F32)
        d = widen(diff[...], nothing, nothing)
        for p in range(parts):
            x = diffuse(widen(state[p].astype(F32), nothing, nothing), d)
            now = x[:, LANES:LANES + cells] + pert[0, p].astype(F32)
            prior[p * tiles:(p + 1) * tiles, :] = now.astype(BF16)

    return kernel


def make_send(pairs, rows):
    def kernel(own, other, trail, *refs):
        notes, sends, half = refs[:pairs], refs[pairs:2 * pairs], refs[2 * pairs]
        sends = [sends[falling(pairs).index(k)] for k in range(pairs)]
        prior = jnp.concatenate([own[...], other[...]], axis=0)
        sent = requested([x[...] for x in notes], prior, 0, rows)
        for k in range(pairs):
            sends[k][...] = sent[k * rows:(k + 1) * rows, :].astype(BF16)
        size = padded(pairs)
        half[...] = jnp.zeros(half.shape, F32)
        for k in range(pairs):
            half[k:k + 1, :] = notes[k][...]
        half[size:, :] = trail[...]

    return kernel


def make_assess(pairs, parts, tiles, cells, share):
    size = padded(pairs)

    def kernel(own, other, low, high, where, terms, local, second, *refs):
        outs, stats, weighted_out, sums = refs[:pairs], refs[pairs], refs[pairs + 1], refs[pairs + 2]
        fixed = []
        for h, prior in enumerate((own, other)):
            for p in range(parts):
                row = (2 * p + h) * size
                x = prior[p * tiles:(p + 1) * tiles, :].astype(F32)
                x = patch(x, low[row:row + 1, LANES:], high[row:row + 1, :LANES])
                fixed.append(x.astype(BF16))
        least, total, weighted = assess(
            fixed, where[...], terms[0:1, :], terms[1:2, :], local[...], 2 * parts, tiles, cells
        )
        sums[...] = weighted
        pack_mean(outs, 0, least, total, sums, share)
        least, total, weighted = assess(
            [second[p * tiles:(p + 1) * tiles, :] for p in range(parts)],
            where[...], terms[0:1, :], terms[2:3, :], local[...], parts, tiles, cells,
        )
        stats[...] = jnp.where(iota((tiles, LANES), 1) == 0, least, total)
        weighted_out[...] = weighted

    return kernel


def make_second(pairs, parts, tiles, cells):
    size = padded(pairs)

    def kernel(keys, diff, pert, message, mine, theirs, after, *refs):
        got, prior, low_out, high_out = refs[:pairs], refs[pairs], refs[pairs + 1], refs[pairs + 2]
        got = [got[falling(pairs).index(k)] for k in range(pairs)]
        below, above = halves(mine[...], theirs[...])
        low, high = edge_windows(message[...], below, above, size, parts)
        low_out[...] = low
        high_out[...] = high
        below, above = below[size:size + 8, :], above[size:size + 8, :]
        arrived = jnp.concatenate([x[...] for x in got], axis=0)
        moved = pick_rows(keys[0], arrived)
        here_codes = message[size + 2:size + 2 + 2 * parts, :].astype(I32)
        codes = jnp.concatenate([here_codes[parts:], below[2:2 + parts, :].astype(I32)], axis=0)
        start = pick_rows(codes, low.astype(BF16))
        codes = jnp.concatenate([here_codes[:parts], above[2 + parts:2 + 2 * parts, :].astype(I32)], axis=0)
        end = pick_rows(codes, high.astype(BF16))
        d = widen(diff[...], below[0:1, :], above[1:2, :])
        for p in range(parts):
            x = patch(moved[p * tiles:(p + 1) * tiles, :], start[p:p + 1, LANES:], end[p:p + 1, :LANES])
            q = parts + p
            x = widen(x, start[q:q + 1, :LANES], end[q:q + 1, LANES:])
            x = diffuse(x, d)[:, LANES:LANES + cells]
            prior[p * tiles:(p + 1) * tiles, :] = (x + pert[0, p].astype(F32)).astype(BF16)

    return kernel


def make_send_second(pairs, rows, parts, tiles, cells, share):
    def kernel(own, other, where, terms, local, stats, own_sums, *refs):
        notes, kept, outs, sums = refs[:pairs], refs[pairs:2 * pairs], refs[2 * pairs:3 * pairs], refs[3 * pairs]
        outs = [outs[falling(pairs).index(k)] for k in range(pairs)]
        prior = jnp.concatenate([own[...], other[...]], axis=0)
        sent = requested([x[...] for x in notes], prior, 1, rows)
        extra = kept[0].shape[1]
        for k in range(pairs):
            outs[k][:, :cells] = sent[k * rows:(k + 1) * rows, :].astype(BF16)
            outs[k][:, cells:cells + extra] = kept[k][...]
        least, total, weighted = assess(
            [other[p * tiles:(p + 1) * tiles, :] for p in range(parts)],
            where[...], terms[0:1, :], terms[2:3, :], local[...], parts, tiles, cells,
        )
        mine = stats[:, 0:1]
        lower = jnp.minimum(least, mine)
        scale, own_scale = jnp.exp(lower - least), jnp.exp(lower - mine)
        total = scale * total + own_scale * stats[:, 1:2]
        sums[...] = scale * weighted + own_scale * own_sums[...]
        least = lower
        pack_mean(outs, cells + extra, least, total, sums, share)

    return kernel


def make_last(pairs, rows, parts, tiles, cells):
    def kernel(keys, *refs):
        got, analysis, mean = refs[:pairs], refs[pairs], refs[pairs + 1]
        got = [got[falling(pairs).index(k)] for k in range(pairs)]
        arrived = jnp.concatenate([x[:, :cells] for x in got], axis=0)
        picked = pick_rows(keys[1], arrived)
        for p in range(parts):
            analysis[p] = picked[p * tiles:(p + 1) * tiles, :].astype(BF16)
        share = mean.shape[2]
        extra = tiles // rows * share + LANES
        for c in range(CYCLES):
            for g, x in enumerate(unpack_mean(got, cells + c * extra, tiles, share)):
                mean[c, g * rows:(g + 1) * rows, :] = x

    return kernel


def body(
    state,
    diffusivity,
    model_perturbation,
    obs_values,
    obs_prec,
    obs_tile,
    obs_cell,
    pattern,
    loc_weight,
    anc_member,
    anc_slot,
):
    parts, tiles, cells = state.shape
    members = lax.axis_size("member")
    regions = lax.axis_size("region")
    capacity = max(2, 2 * parts * tiles // members)
    share = cells // members
    pairs = members // 2
    rows = 2 * capacity
    extra = tiles // rows * share + LANES
    blocks, per_block = obs_cell.shape
    count = blocks * per_block
    member_of = anc_member.reshape(CYCLES, parts, tiles)
    slot_of = anc_slot.reshape(CYCLES, parts, tiles)
    near = pattern.shape[1]
    ends = cells // LANES - 1

    def block(shape, at):
        lead = (0,) * (len(shape) - 1)
        return pl.BlockSpec(shape, lambda i: lead + (at,))

    edges = [state, state, diffusivity, diffusivity, model_perturbation, model_perturbation, member_of, slot_of]
    *notes, trail, keys = call(
        make_prepare(members, capacity, parts, tiles),
        [((1, LANES), F32)] * pairs + [((8, LANES), F32), ((CYCLES, parts * tiles, LANES), I32)],
        [pltpu.with_memory_space_constraint(x, pltpu.HBM) for x in edges],
        [
            block((parts, tiles, LANES), 0),
            block((parts, tiles, LANES), ends),
            block((tiles, LANES), 0),
            block((tiles, LANES), ends),
            block((1, parts, tiles, LANES), 0),
            block((1, parts, tiles, LANES), ends),
            whole_spec(member_of.shape),
            whole_spec(slot_of.shape),
        ],
        name="prepare",
    )

    def trade(x):
        return lax.ppermute(x, "member", [(i, i ^ 1) for i in range(members)])

    def exchange(sends, order):
        got = [sends[0]]
        for x, k in list(zip(sends, order))[1:]:
            got.append(lax.ppermute(x, "member", [(i, i ^ (2 * k)) for i in range(members)]))
        return got

    notes = exchange(notes, range(pairs))

    where, terms, local = call(
        make_observe(blocks, per_block, tiles, near),
        [((2, count), I32), ((1 + CYCLES, count), F32), ((tiles, count), F32)],
        [obs_tile[None, :], obs_cell.T, obs_prec.T, jnp.swapaxes(obs_values, 1, 2), pattern.T, loc_weight.T],
        name="observe",
    )

    def noise_spec(c):
        return pl.BlockSpec((1, parts, tiles, cells), lambda i: (c, 0, 0, 0))

    args = [state, diffusivity, model_perturbation, trail]
    specs = [whole_spec(a.shape) for a in args]
    specs[2] = noise_spec(0)
    (prior,) = call(
        make_first(parts, tiles, cells), [((parts * tiles, cells), BF16)], args, specs, name="forecast_first"
    )
    other = trade(prior)
    size = padded(pairs)
    *sends, half = call(
        make_send(pairs, rows),
        [((rows, cells), BF16)] * pairs + [((size + trail.shape[0], LANES), F32)],
        [prior, other, trail, *notes],
        name="send_first",
    )
    got = exchange(sends, falling(pairs))
    message = jnp.concatenate([half, trade(half)], axis=0)
    steps = []
    for i in range(members):
        first, last = (0, regions - 1) if i % 2 == 0 else (1, regions)
        steps += [(i * regions + r, i * regions + r + 1 - 2 * (i % 2)) for r in range(first, last)]
    mine = lax.ppermute(message, ("member", "region"), steps)
    theirs = trade(mine)
    window = ((parts * 2 * size, 2 * LANES), F32)
    sums = [((tiles, cells), F32)]
    args = [keys, diffusivity, model_perturbation, message, mine, theirs, where, *got]
    specs = [whole_spec(a.shape) for a in args]
    specs[2] = noise_spec(1)
    second, low, high = call(
        make_second(pairs, parts, tiles, cells),
        [((parts * tiles, cells), BF16), window, window],
        args,
        specs,
        name="forecast_second",
    )
    *kept, stats, own_sums = call(
        make_assess(pairs, parts, tiles, cells, share),
        [((rows, extra), BF16)] * pairs + [((tiles, LANES), F32), ((tiles, cells), F32)],
        [prior, other, low, high, where, terms, local, second],
        scratch=sums,
        name="assess_first",
    )
    sends = call(
        make_send_second(pairs, rows, parts, tiles, cells, share),
        [((rows, cells + CYCLES * extra), BF16)] * pairs,
        [second, trade(second), where, terms, local, stats, own_sums, *notes, *kept],
        scratch=sums,
        name="send_second",
    )
    got = exchange(sends, falling(pairs))
    return tuple(
        call(
            make_last(pairs, rows, parts, tiles, cells),
            [(state.shape, BF16), ((CYCLES, tiles, share), F32)],
            [keys, *got],
            name="finish",
        )
    )


def solution(mesh):
    in_specs = (
        P("member", "region", None),
        P("region", None),
        P(None, "member", "region", None),
        P(None, "region", None),
        P("region", None),
        P("region"),
        P("region", None),
        P("region", None),
        P("region", None),
        P(None, "region", "member", None, None),
        P(None, "region", "member", None),
    )
    out_specs = (P("member", "region", None), P(None, "region", "member"))
    return jax.shard_map(body, mesh=mesh, in_specs=in_specs, out_specs=out_specs, check_vma=False)
```

```python
import jax
import jax.numpy as jnp
from jax import lax
from jax.experimental import pallas as pl
from jax.experimental.pallas import tpu as pltpu
from jax.sharding import PartitionSpec as P

CYCLES = 2
STEPS = 2
LANES = 128
F32 = jnp.float32
BF16 = jnp.bfloat16
I32 = jnp.int32
PARAMS = pltpu.CompilerParams(vmem_limit_bytes=48 * 1024 * 1024)


def iota(shape, dim):
    return lax.broadcasted_iota(I32, shape, dim)


def whole_spec(shape):
    zeros = (0,) * len(shape)
    return pl.BlockSpec(shape, lambda i: zeros)


def call(kernel, outs, args, specs=None, scratch=(), name=None):
    specs = specs or [whole_spec(a.shape) for a in args]
    return pl.pallas_call(
        kernel,
        out_shape=[jax.ShapeDtypeStruct(s, d) for s, d in outs],
        grid=(1,),
        in_specs=specs,
        out_specs=[whole_spec(s) for s, _ in outs],
        scratch_shapes=[pltpu.VMEM(s, d) for s, d in scratch],
        compiler_params=PARAMS,
        name=name,
    )(*args)


def column_of(row):
    n = row.shape[1]
    square = jnp.broadcast_to(row, (n, n))
    return jnp.sum(jnp.where(iota((n, n), 0) == iota((n, n), 1), square, 0), axis=1, keepdims=True)


def here():
    return lax.axis_index("member")


EDGE_AT = 32
STRIDE = 8


def falling(pairs):
    return [0, *range(pairs - 1, 0, -1)]


def padded(pairs):
    return max(8, pairs)


def make_prepare(members, capacity, parts, tiles):
    width = 2 * STEPS
    pairs = members // 2
    rows = parts * tiles

    def kernel(st0, st1, df0, df1, pb0, pb1, am, slot, *outs):
        notes, trail, keys = outs[:pairs], outs[pairs], outs[pairs + 1]
        m = here()
        lane = iota((1, LANES), 1)
        last = tiles - 1
        trail[...] = jnp.zeros(trail.shape, F32)
        trail[0:1, :] = df1[last:last + 1, :]
        trail[1:2, :] = df0[0:1, :]
        edge = jnp.zeros((1, LANES), F32)
        for p in range(parts):
            for i, t in enumerate((last, 0)):
                source = am[0, p:p + 1, t:t + 1] ^ m
                code = (slot[0, p:p + 1, t:t + 1] * 2 + source % 2) * padded(pairs) + source // 2
                row = 2 + i * parts + p
                trail[row:row + 1, :] = jnp.broadcast_to(code.astype(F32), (1, LANES))
            fields = (st1[p, last:last + 1, :], st0[p, 0:1, :], pb1[0, p, last:last + 1, :], pb0[0, p, 0:1, :])
            for i, x in enumerate(fields):
                to = EDGE_AT + STRIDE * (4 * p + i)
                start = 0 if i % 2 else LANES - width
                moved = pltpu.roll(x.astype(F32), (to - start) % LANES, 1)
                edge = jnp.where((lane >= to) & (lane < to + width), moved, edge)
        before = (iota((tiles, tiles), 0) < iota((tiles, tiles), 1)).astype(F32)
        asked = jnp.zeros((pairs, LANES), F32)
        sources = [[am[c, p:p + 1, :] ^ m for p in range(parts)] for c in range(CYCLES)]
        every = [(iota((members, tiles), 0) == x).astype(F32) for some in sources for x in some]
        earlier_all = jnp.dot(jnp.concatenate(every, axis=0), before, preferred_element_type=F32)
        for c in range(CYCLES):
            seen = jnp.zeros((members, 1), F32)
            for p in range(parts):
                source = sources[c][p]
                at = c * parts + p
                named = every[at]
                earlier = seen + earlier_all[at * members:(at + 1) * members, :]
                rank = jnp.sum(named * earlier, axis=0, keepdims=True).astype(I32)
                seen = seen + jnp.sum(named, axis=1, keepdims=True)
                half = source % 2
                code = half * rows + slot[c, p:p + 1, :] * tiles + iota((1, tiles), 1)
                spot = (iota((LANES, tiles), 0) == (2 * c + half) * capacity + rank).astype(F32)
                pair = jnp.where(iota((pairs, tiles), 0) == source // 2, (code + 1).astype(F32), 0.0)
                asked = asked + lax.dot_general(pair, spot, (((1,), (1,)), ((), ())), preferred_element_type=F32)
                column = column_of(source * capacity + rank)
                keys[c, p * tiles:(p + 1) * tiles, :] = jnp.broadcast_to(column, (tiles, LANES))
        for k in range(pairs):
            notes[falling(pairs).index(k)][...] = jnp.where(lane < EDGE_AT, asked[k:k + 1, :] - 1.0, edge)

    return kernel


def halves(mine, theirs):
    half = theirs.shape[0] // 2
    theirs = jnp.concatenate([theirs[half:, :], theirs[:half, :]], axis=0)
    first = jnp.broadcast_to(here() % 2, mine.shape) == 0
    return jnp.where(first, mine, theirs), jnp.where(first, theirs, mine)


def edge_windows(own, below, above, size, parts):
    width = 2 * STEPS

    def field(note, p, i):
        at = EDGE_AT + STRIDE * (4 * p + i)
        start = 0 if i % 2 else LANES - width
        both = jnp.concatenate([note[:size, :], note[size + 8:2 * size + 8, :]], axis=0)
        return pltpu.roll(both, (start - at) % LANES, 1)

    low, high = [], []
    for out, before, after in ((low, below, own), (high, own, above)):
        d = jnp.concatenate([before[size:size + 1, :], after[size + 1:size + 2, :]], axis=1)
        for p in range(parts):
            x = jnp.concatenate([field(before, p, 0), field(after, p, 1)], axis=1)
            x = diffuse(x, d) + jnp.concatenate([field(before, p, 2), field(after, p, 3)], axis=1)
            out.append(x.astype(BF16).astype(F32))
    return jnp.concatenate(low, axis=0), jnp.concatenate(high, axis=0)


def patch(x, first, last):
    tiles = x.shape[0]
    row, lane = iota((tiles, LANES), 0), iota((tiles, LANES), 1)
    head = jnp.where((row == 0) & (lane < STEPS), first, x[:, :LANES])
    tail = jnp.where((row == tiles - 1) & (lane >= LANES - STEPS), last, x[:, -LANES:])
    return jnp.concatenate([head, x[:, LANES:-LANES], tail], axis=1)


def widen(x, left, right):
    tiles = x.shape[0]
    row = iota((tiles, LANES), 0)
    before = jnp.where(row == 0, left, pltpu.roll(x[:, -LANES:], 1, 0))
    after = jnp.where(row == tiles - 1, right, pltpu.roll(x[:, :LANES], tiles - 1, 0))
    return jnp.concatenate([before, x, after], axis=1)


def diffuse(x, d):
    n = x.shape[1]
    for _ in range(STEPS):
        x = x + d * (pltpu.roll(x, 1, 1) - 2.0 * x + pltpu.roll(x, n - 1, 1))
    return x


def pick_rows(wanted, rows):
    m = rows.shape[0]
    n = wanted.shape[0]
    choice = (wanted[:, :m] == iota((n, m), 1)).astype(F32).astype(BF16)
    return jnp.dot(choice, rows, preferred_element_type=F32)


def requested(notes, prior, cycle, rows):
    pairs = len(notes)
    total = pairs * rows
    asked = jnp.concatenate(notes, axis=0)
    spread = jnp.broadcast_to(asked[:, None, :], (pairs, rows, LANES)).reshape(total, LANES)
    mine = iota((total, LANES), 1) == cycle * rows + iota((total, LANES), 0) % rows
    wanted = jnp.sum(jnp.where(mine, spread, 0.0), axis=1, keepdims=True).astype(I32)
    return pick_rows(jnp.broadcast_to(wanted, (total, LANES)), prior)


def make_observe(blocks, per_block, tiles, near):
    count = blocks * per_block

    def kernel(tile, cell, prec, value, pattern, weight, where, terms, local):
        def line(x):
            wide = jnp.concatenate([x] * per_block, axis=1)
            own = iota((per_block, count), 1) // blocks == iota((per_block, count), 0)
            return jnp.sum(jnp.where(own, wide, 0), axis=0, keepdims=True)

        at = line(cell[...])
        row = (at // LANES) * tiles + jnp.concatenate([tile[...]] * per_block, axis=1)
        pick = iota((2, count), 0) == 0
        where[...] = jnp.where(pick, row, at % LANES)
        terms[0:1, :] = line(prec[...])
        for c in range(CYCLES):
            terms[c + 1:c + 2, :] = line(value[c])
        group = iota((tiles, count), 1) % blocks
        total = jnp.zeros((tiles, count), F32)
        for k in range(near):
            total = total + jnp.where(column_of(pattern[k:k + 1, :]) == group, column_of(weight[k:k + 1, :]), 0.0)
        local[...] = total

    return kernel


def assess(prior, where, prec, value, local, parts, tiles, cells):
    blocks = cells // LANES
    rows = tiles * blocks
    count = where.shape[1]
    stacked = jnp.concatenate(
        [jnp.concatenate([x[:, k * LANES:(k + 1) * LANES] for k in range(blocks)], axis=0) for x in prior],
        axis=1,
    )
    choice = (iota((rows, count), 0) == where[0:1, :]).astype(F32).astype(BF16)
    lines = lax.dot_general(stacked, choice, (((0,), (0,)), ((), ())), preferred_element_type=F32)
    lane = iota((LANES, count), 0) == where[1:2, :]
    score = []
    for p in range(parts):
        predicted = jnp.sum(jnp.where(lane, lines[p * LANES:(p + 1) * LANES, :], 0.0), axis=0, keepdims=True)
        miss = value - predicted
        term = 0.5 * (prec * miss * miss)
        score.append(jnp.sum(local * term, axis=1, keepdims=True))
    least = score[0]
    for s in score[1:]:
        least = jnp.minimum(least, s)
    scale = [jnp.exp(least - s) for s in score]
    total = scale[0]
    for s in scale[1:]:
        total = total + s
    weighted = scale[0] * prior[0].astype(F32)
    for s, x in zip(scale[1:], prior[1:]):
        weighted = weighted + s * x.astype(F32)
    return least, total, weighted


def pieces(x):
    high = x.astype(BF16).astype(F32)
    middle = (x - high).astype(BF16).astype(F32)
    low = (x - high - middle).astype(BF16).astype(F32)
    return high, middle, low


def share_of(ref, member, share):
    if share % LANES == 0:
        return ref[:, pl.ds(pl.multiple_of(member * share, LANES), share)]
    return pltpu.roll(ref[...], ref.shape[1] - member * share, 1)[:, :share]


def pack_mean(outs, at, least, total, sums, share):
    rows = outs[0].shape[0]
    tiles = sums.shape[0]
    groups = tiles // rows
    m = here()
    lane = iota((rows, LANES), 1)
    misc = jnp.zeros((rows, LANES), F32)
    spot = 0
    for x in (least, total):
        for piece in pieces(x):
            for g in range(groups):
                misc = jnp.where(lane == spot, piece[g * rows:(g + 1) * rows, :], misc)
                spot += 1
    end = at + groups * share
    for k, out in enumerate(outs):
        block = share_of(sums, m ^ (2 * k), share)
        for g in range(groups):
            out[:, at + g * share:at + (g + 1) * share] = block[g * rows:(g + 1) * rows, :].astype(BF16)
        out[:, end:end + LANES] = misc.astype(BF16)


def unpack_mean(got, at, tiles, share):
    rows = got[0].shape[0]
    groups = tiles // rows
    end = at + groups * share
    misc = [x[:, end:end + LANES].astype(F32) for x in got]
    means = []
    for g in range(groups):
        stats = []
        for x in misc:
            pair = []
            for kind in range(2):
                spot = [(kind * 3 + piece) * groups + g for piece in range(3)]
                high, middle, low = [x[:, i:i + 1] for i in spot]
                pair.append(high + middle + low)
            stats.append(pair)
        lowest = stats[0][0]
        for least, _ in stats[1:]:
            lowest = jnp.minimum(lowest, least)
        top, bottom = 0.0, 0.0
        for x, (least, total) in zip(got, stats):
            scale = jnp.exp(lowest - least)
            top = top + scale * x[:, at + g * share:at + (g + 1) * share].astype(F32)
            bottom = bottom + scale * total
        means.append(top / bottom)
    return means


def make_first(parts, tiles, cells):
    def kernel(state, diff, pert, after, prior):
        nothing = jnp.zeros((1, LANES), F32)
        d = widen(diff[...], nothing, nothing)
        for p in range(parts):
            x = diffuse(widen(state[p].astype(F32), nothing, nothing), d)
            now = x[:, LANES:LANES + cells] + pert[0, p].astype(F32)
            prior[p * tiles:(p + 1) * tiles, :] = now.astype(BF16)

    return kernel


def make_send(pairs, rows):
    def kernel(own, other, trail, *refs):
        notes, sends, half = refs[:pairs], refs[pairs:2 * pairs], refs[2 * pairs]
        notes, sends = [[x[falling(pairs).index(k)] for k in range(pairs)] for x in (notes, sends)]
        prior = jnp.concatenate([own[...], other[...]], axis=0)
        sent = requested([x[...] for x in notes], prior, 0, rows)
        for k in range(pairs):
            sends[k][...] = sent[k * rows:(k + 1) * rows, :].astype(BF16)
        size = padded(pairs)
        half[...] = jnp.zeros(half.shape, F32)
        for k in range(pairs):
            half[k:k + 1, :] = notes[k][...]
        half[size:, :] = trail[...]

    return kernel


def make_assess(pairs, parts, tiles, cells, share):
    size = padded(pairs)

    def kernel(own, other, low, high, where, terms, local, second, *refs):
        outs, stats, weighted_out, sums = refs[:pairs], refs[pairs], refs[pairs + 1], refs[pairs + 2]
        fixed = []
        for h, prior in enumerate((own, other)):
            for p in range(parts):
                row = (2 * p + h) * size
                x = prior[p * tiles:(p + 1) * tiles, :].astype(F32)
                x = patch(x, low[row:row + 1, LANES:], high[row:row + 1, :LANES])
                fixed.append(x.astype(BF16))
        least, total, weighted = assess(
            fixed, where[...], terms[0:1, :], terms[1:2, :], local[...], 2 * parts, tiles, cells
        )
        sums[...] = weighted
        pack_mean(outs, 0, least, total, sums, share)
        least, total, weighted = assess(
            [second[p * tiles:(p + 1) * tiles, :] for p in range(parts)],
            where[...], terms[0:1, :], terms[2:3, :], local[...], parts, tiles, cells,
        )
        stats[...] = jnp.where(iota((tiles, LANES), 1) == 0, least, total)
        weighted_out[...] = weighted

    return kernel


def make_second(pairs, parts, tiles, cells):
    size = padded(pairs)

    def kernel(keys, diff, pert, message, mine, theirs, after, *refs):
        got, prior, low_out, high_out = refs[:pairs], refs[pairs], refs[pairs + 1], refs[pairs + 2]
        got = [got[falling(pairs).index(k)] for k in range(pairs)]
        below, above = halves(mine[...], theirs[...])
        low, high = edge_windows(message[...], below, above, size, parts)
        low_out[...] = low
        high_out[...] = high
        below, above = below[size:size + 8, :], above[size:size + 8, :]
        arrived = jnp.concatenate([x[...] for x in got], axis=0)
        moved = pick_rows(keys[0], arrived)
        here_codes = message[size + 2:size + 2 + 2 * parts, :].astype(I32)
        codes = jnp.concatenate([here_codes[parts:], below[2:2 + parts, :].astype(I32)], axis=0)
        start = pick_rows(codes, low.astype(BF16))
        codes = jnp.concatenate([here_codes[:parts], above[2 + parts:2 + 2 * parts, :].astype(I32)], axis=0)
        end = pick_rows(codes, high.astype(BF16))
        d = widen(diff[...], below[0:1, :], above[1:2, :])
        for p in range(parts):
            x = patch(moved[p * tiles:(p + 1) * tiles, :], start[p:p + 1, LANES:], end[p:p + 1, :LANES])
            q = parts + p
            x = widen(x, start[q:q + 1, :LANES], end[q:q + 1, LANES:])
            x = diffuse(x, d)[:, LANES:LANES + cells]
            prior[p * tiles:(p + 1) * tiles, :] = (x + pert[0, p].astype(F32)).astype(BF16)

    return kernel


def make_send_second(pairs, rows, parts, tiles, cells, share):
    def kernel(own, other, where, terms, local, stats, own_sums, *refs):
        notes, kept, outs, sums = refs[:pairs], refs[pairs:2 * pairs], refs[2 * pairs:3 * pairs], refs[3 * pairs]
        notes, outs = [[x[falling(pairs).index(k)] for k in range(pairs)] for x in (notes, outs)]
        prior = jnp.concatenate([own[...], other[...]], axis=0)
        sent = requested([x[...] for x in notes], prior, 1, rows)
        extra = kept[0].shape[1]
        for k in range(pairs):
            outs[k][:, :cells] = sent[k * rows:(k + 1) * rows, :].astype(BF16)
            outs[k][:, cells:cells + extra] = kept[k][...]
        least, total, weighted = assess(
            [other[p * tiles:(p + 1) * tiles, :] for p in range(parts)],
            where[...], terms[0:1, :], terms[2:3, :], local[...], parts, tiles, cells,
        )
        mine = stats[:, 0:1]
        lower = jnp.minimum(least, mine)
        scale, own_scale = jnp.exp(lower - least), jnp.exp(lower - mine)
        total = scale * total + own_scale * stats[:, 1:2]
        sums[...] = scale * weighted + own_scale * own_sums[...]
        least = lower
        pack_mean(outs, cells + extra, least, total, sums, share)

    return kernel


def make_last(pairs, rows, parts, tiles, cells):
    def kernel(keys, *refs):
        got, analysis, mean = refs[:pairs], refs[pairs], refs[pairs + 1]
        got = [got[falling(pairs).index(k)] for k in range(pairs)]
        arrived = jnp.concatenate([x[:, :cells] for x in got], axis=0)
        picked = pick_rows(keys[1], arrived)
        for p in range(parts):
            analysis[p] = picked[p * tiles:(p + 1) * tiles, :].astype(BF16)
        share = mean.shape[2]
        extra = tiles // rows * share + LANES
        for c in range(CYCLES):
            for g, x in enumerate(unpack_mean(got, cells + c * extra, tiles, share)):
                mean[c, g * rows:(g + 1) * rows, :] = x

    return kernel


def body(
    state,
    diffusivity,
    model_perturbation,
    obs_values,
    obs_prec,
    obs_tile,
    obs_cell,
    pattern,
    loc_weight,
    anc_member,
    anc_slot,
):
    parts, tiles, cells = state.shape
    members = lax.axis_size("member")
    regions = lax.axis_size("region")
    capacity = max(2, 2 * parts * tiles // members)
    share = cells // members
    pairs = members // 2
    rows = 2 * capacity
    extra = tiles // rows * share + LANES
    blocks, per_block = obs_cell.shape
    count = blocks * per_block
    member_of = anc_member.reshape(CYCLES, parts, tiles)
    slot_of = anc_slot.reshape(CYCLES, parts, tiles)
    near = pattern.shape[1]
    ends = cells // LANES - 1

    def block(shape, at):
        lead = (0,) * (len(shape) - 1)
        return pl.BlockSpec(shape, lambda i: lead + (at,))

    edges = [state, state, diffusivity, diffusivity, model_perturbation, model_perturbation, member_of, slot_of]
    *notes, trail, keys = call(
        make_prepare(members, capacity, parts, tiles),
        [((1, LANES), F32)] * pairs + [((8, LANES), F32), ((CYCLES, parts * tiles, LANES), I32)],
        [pltpu.with_memory_space_constraint(x, pltpu.HBM) for x in edges],
        [
            block((parts, tiles, LANES), 0),
            block((parts, tiles, LANES), ends),
            block((tiles, LANES), 0),
            block((tiles, LANES), ends),
            block((1, parts, tiles, LANES), 0),
            block((1, parts, tiles, LANES), ends),
            whole_spec(member_of.shape),
            whole_spec(slot_of.shape),
        ],
        name="prepare",
    )

    def trade(x):
        return lax.ppermute(x, "member", [(i, i ^ 1) for i in range(members)])

    def exchange(sends, order):
        got = [sends[0]]
        for x, k in list(zip(sends, order))[1:]:
            got.append(lax.ppermute(x, "member", [(i, i ^ (2 * k)) for i in range(members)]))
        return got

    notes = exchange(notes, falling(pairs))

    where, terms, local = call(
        make_observe(blocks, per_block, tiles, near),
        [((2, count), I32), ((1 + CYCLES, count), F32), ((tiles, count), F32)],
        [obs_tile[None, :], obs_cell.T, obs_prec.T, jnp.swapaxes(obs_values, 1, 2), pattern.T, loc_weight.T],
        name="observe",
    )

    def noise_spec(c):
        return pl.BlockSpec((1, parts, tiles, cells), lambda i: (c, 0, 0, 0))

    args = [state, diffusivity, model_perturbation, trail]
    specs = [whole_spec(a.shape) for a in args]
    specs[2] = noise_spec(0)
    (prior,) = call(
        make_first(parts, tiles, cells), [((parts * tiles, cells), BF16)], args, specs, name="forecast_first"
    )
    other = trade(prior)
    size = padded(pairs)
    *sends, half = call(
        make_send(pairs, rows),
        [((rows, cells), BF16)] * pairs + [((size + trail.shape[0], LANES), F32)],
        [prior, other, trail, *notes],
        name="send_first",
    )
    got = exchange(sends, falling(pairs))
    message = jnp.concatenate([half, trade(half)], axis=0)
    steps = []
    for i in range(members):
        first, last = (0, regions - 1) if i % 2 == 0 else (1, regions)
        steps += [(i * regions + r, i * regions + r + 1 - 2 * (i % 2)) for r in range(first, last)]
    mine = lax.ppermute(message, ("member", "region"), steps)
    theirs = trade(mine)
    window = ((parts * 2 * size, 2 * LANES), F32)
    sums = [((tiles, cells), F32)]
    args = [keys, diffusivity, model_perturbation, message, mine, theirs, where, *got]
    specs = [whole_spec(a.shape) for a in args]
    specs[2] = noise_spec(1)
    second, low, high = call(
        make_second(pairs, parts, tiles, cells),
        [((parts * tiles, cells), BF16), window, window],
        args,
        specs,
        name="forecast_second",
    )
    *kept, stats, own_sums = call(
        make_assess(pairs, parts, tiles, cells, share),
        [((rows, extra), BF16)] * pairs + [((tiles, LANES), F32), ((tiles, cells), F32)],
        [prior, other, low, high, where, terms, local, second],
        scratch=sums,
        name="assess_first",
    )
    sends = call(
        make_send_second(pairs, rows, parts, tiles, cells, share),
        [((rows, cells + CYCLES * extra), BF16)] * pairs,
        [second, trade(second), where, terms, local, stats, own_sums, *notes, *kept],
        scratch=sums,
        name="send_second",
    )
    got = exchange(sends, falling(pairs))
    return tuple(
        call(
            make_last(pairs, rows, parts, tiles, cells),
            [(state.shape, BF16), ((CYCLES, tiles, share), F32)],
            [keys, *got],
            name="finish",
        )
    )


def solution(mesh):
    in_specs = (
        P("member", "region", None),
        P("region", None),
        P(None, "member", "region", None),
        P(None, "region", None),
        P("region", None),
        P("region"),
        P("region", None),
        P("region", None),
        P("region", None),
        P(None, "region", "member", None, None),
        P(None, "region", "member", None),
    )
    out_specs = (P("member", "region", None), P(None, "region", "member"))
    return jax.shard_map(body, mesh=mesh, in_specs=in_specs, out_specs=out_specs, check_vma=False)
```

```python
import jax
import jax.numpy as jnp
from jax import lax
from jax.experimental import pallas as pl
from jax.experimental.pallas import tpu as pltpu
from jax.sharding import PartitionSpec as P

CYCLES = 2
STEPS = 2
LANES = 128
F32 = jnp.float32
BF16 = jnp.bfloat16
I32 = jnp.int32
PARAMS = pltpu.CompilerParams(vmem_limit_bytes=48 * 1024 * 1024)


def iota(shape, dim):
    return lax.broadcasted_iota(I32, shape, dim)


def whole_spec(shape):
    zeros = (0,) * len(shape)
    return pl.BlockSpec(shape, lambda i: zeros)


def call(kernel, outs, args, specs=None, scratch=(), name=None):
    specs = specs or [whole_spec(a.shape) for a in args]
    return pl.pallas_call(
        kernel,
        out_shape=[jax.ShapeDtypeStruct(s, d) for s, d in outs],
        grid=(1,),
        in_specs=specs,
        out_specs=[whole_spec(s) for s, _ in outs],
        scratch_shapes=[pltpu.VMEM(s, d) for s, d in scratch],
        compiler_params=PARAMS,
        name=name,
    )(*args)


def column_of(row):
    n = row.shape[1]
    square = jnp.broadcast_to(row, (n, n))
    return jnp.sum(jnp.where(iota((n, n), 0) == iota((n, n), 1), square, 0), axis=1, keepdims=True)


def here():
    return lax.axis_index("member")


EDGE_AT = 32
STRIDE = 8


def falling(pairs):
    return [0, *range(pairs - 1, 0, -1)]


def padded(pairs):
    return max(8, pairs)


def make_prepare(members, capacity, parts, tiles):
    width = 2 * STEPS
    pairs = members // 2
    rows = parts * tiles

    def kernel(st0, st1, df0, df1, pb0, pb1, am, slot, *outs):
        notes, trail, keys = outs[:pairs], outs[pairs], outs[pairs + 1]
        m = here()
        lane = iota((1, LANES), 1)
        last = tiles - 1
        trail[...] = jnp.zeros(trail.shape, F32)
        trail[0:1, :] = df1[last:last + 1, :]
        trail[1:2, :] = df0[0:1, :]
        edge = jnp.zeros((1, LANES), F32)
        for p in range(parts):
            for i, t in enumerate((last, 0)):
                source = am[0, p:p + 1, t:t + 1] ^ m
                code = (slot[0, p:p + 1, t:t + 1] * 2 + source % 2) * padded(pairs) + source // 2
                row = 2 + i * parts + p
                trail[row:row + 1, :] = jnp.broadcast_to(code.astype(F32), (1, LANES))
            fields = (st1[p, last:last + 1, :], st0[p, 0:1, :], pb1[0, p, last:last + 1, :], pb0[0, p, 0:1, :])
            for i, x in enumerate(fields):
                to = EDGE_AT + STRIDE * (4 * p + i)
                start = 0 if i % 2 else LANES - width
                moved = pltpu.roll(x.astype(F32), (to - start) % LANES, 1)
                edge = jnp.where((lane >= to) & (lane < to + width), moved, edge)
        before = (iota((tiles, tiles), 0) < iota((tiles, tiles), 1)).astype(F32)
        asked = jnp.zeros((pairs, LANES), F32)
        sources = [[am[c, p:p + 1, :] ^ m for p in range(parts)] for c in range(CYCLES)]
        every = [(iota((members, tiles), 0) == x).astype(F32) for some in sources for x in some]
        earlier_all = jnp.dot(jnp.concatenate(every, axis=0), before, preferred_element_type=F32)
        for c in range(CYCLES):
            seen = jnp.zeros((members, 1), F32)
            for p in range(parts):
                source = sources[c][p]
                at = c * parts + p
                named = every[at]
                earlier = seen + earlier_all[at * members:(at + 1) * members, :]
                rank = jnp.sum(named * earlier, axis=0, keepdims=True).astype(I32)
                seen = seen + jnp.sum(named, axis=1, keepdims=True)
                half = source % 2
                code = half * rows + slot[c, p:p + 1, :] * tiles + iota((1, tiles), 1)
                spot = (iota((LANES, tiles), 0) == (2 * c + half) * capacity + rank).astype(F32)
                pair = jnp.where(iota((pairs, tiles), 0) == source // 2, (code + 1).astype(F32), 0.0)
                asked = asked + lax.dot_general(pair, spot, (((1,), (1,)), ((), ())), preferred_element_type=F32)
                column = column_of(source * capacity + rank)
                keys[c, p * tiles:(p + 1) * tiles, :] = jnp.broadcast_to(column, (tiles, LANES))
        for k in range(pairs):
            notes[k][...] = jnp.where(lane < EDGE_AT, asked[k:k + 1, :] - 1.0, edge)

    return kernel


def halves(mine, theirs):
    half = theirs.shape[0] // 2
    theirs = jnp.concatenate([theirs[half:, :], theirs[:half, :]], axis=0)
    first = jnp.broadcast_to(here() % 2, mine.shape) == 0
    return jnp.where(first, mine, theirs), jnp.where(first, theirs, mine)


def edge_windows(own, below, above, size, parts):
    width = 2 * STEPS

    def field(note, p, i):
        at = EDGE_AT + STRIDE * (4 * p + i)
        start = 0 if i % 2 else LANES - width
        both = jnp.concatenate([note[:size, :], note[size + 8:2 * size + 8, :]], axis=0)
        return pltpu.roll(both, (start - at) % LANES, 1)

    low, high = [], []
    for out, before, after in ((low, below, own), (high, own, above)):
        d = jnp.concatenate([before[size:size + 1, :], after[size + 1:size + 2, :]], axis=1)
        for p in range(parts):
            x = jnp.concatenate([field(before, p, 0), field(after, p, 1)], axis=1)
            x = diffuse(x, d) + jnp.concatenate([field(before, p, 2), field(after, p, 3)], axis=1)
            out.append(x.astype(BF16).astype(F32))
    return jnp.concatenate(low, axis=0), jnp.concatenate(high, axis=0)


def patch(x, first, last):
    tiles = x.shape[0]
    row, lane = iota((tiles, LANES), 0), iota((tiles, LANES), 1)
    head = jnp.where((row == 0) & (lane < STEPS), first, x[:, :LANES])
    tail = jnp.where((row == tiles - 1) & (lane >= LANES - STEPS), last, x[:, -LANES:])
    return jnp.concatenate([head, x[:, LANES:-LANES], tail], axis=1)


def widen(x, left, right):
    tiles = x.shape[0]
    row = iota((tiles, LANES), 0)
    before = jnp.where(row == 0, left, pltpu.roll(x[:, -LANES:], 1, 0))
    after = jnp.where(row == tiles - 1, right, pltpu.roll(x[:, :LANES], tiles - 1, 0))
    return jnp.concatenate([before, x, after], axis=1)


def diffuse(x, d):
    n = x.shape[1]
    for _ in range(STEPS):
        x = x + d * (pltpu.roll(x, 1, 1) - 2.0 * x + pltpu.roll(x, n - 1, 1))
    return x


def pick_rows(wanted, rows):
    m = rows.shape[0]
    n = wanted.shape[0]
    choice = (wanted[:, :m] == iota((n, m), 1)).astype(F32).astype(BF16)
    return jnp.dot(choice, rows, preferred_element_type=F32)


def requested(notes, prior, cycle, rows):
    pairs = len(notes)
    total = pairs * rows
    asked = jnp.concatenate(notes, axis=0)
    spread = jnp.broadcast_to(asked[:, None, :], (pairs, rows, LANES)).reshape(total, LANES)
    mine = iota((total, LANES), 1) == cycle * rows + iota((total, LANES), 0) % rows
    wanted = jnp.sum(jnp.where(mine, spread, 0.0), axis=1, keepdims=True).astype(I32)
    return pick_rows(jnp.broadcast_to(wanted, (total, LANES)), prior)


def make_observe(blocks, per_block, tiles, near):
    count = blocks * per_block

    def kernel(tile, cell, prec, value, pattern, weight, where, terms, local):
        def line(x):
            wide = jnp.concatenate([x] * per_block, axis=1)
            own = iota((per_block, count), 1) // blocks == iota((per_block, count), 0)
            return jnp.sum(jnp.where(own, wide, 0), axis=0, keepdims=True)

        at = line(cell[...])
        row = (at // LANES) * tiles + jnp.concatenate([tile[...]] * per_block, axis=1)
        pick = iota((2, count), 0) == 0
        where[...] = jnp.where(pick, row, at % LANES)
        terms[0:1, :] = line(prec[...])
        for c in range(CYCLES):
            terms[c + 1:c + 2, :] = line(value[c])
        group = iota((tiles, count), 1) % blocks
        total = jnp.zeros((tiles, count), F32)
        for k in range(near):
            total = total + jnp.where(column_of(pattern[k:k + 1, :]) == group, column_of(weight[k:k + 1, :]), 0.0)
        local[...] = total

    return kernel


def assess(prior, where, prec, value, local, parts, tiles, cells):
    blocks = cells // LANES
    rows = tiles * blocks
    count = where.shape[1]
    stacked = jnp.concatenate(
        [jnp.concatenate([x[:, k * LANES:(k + 1) * LANES] for k in range(blocks)], axis=0) for x in prior],
        axis=1,
    )
    choice = (iota((rows, count), 0) == where[0:1, :]).astype(F32).astype(BF16)
    lines = lax.dot_general(stacked, choice, (((0,), (0,)), ((), ())), preferred_element_type=F32)
    lane = iota((LANES, count), 0) == where[1:2, :]
    score = []
    for p in range(parts):
        predicted = jnp.sum(jnp.where(lane, lines[p * LANES:(p + 1) * LANES, :], 0.0), axis=0, keepdims=True)
        miss = value - predicted
        term = 0.5 * (prec * miss * miss)
        score.append(jnp.sum(local * term, axis=1, keepdims=True))
    least = score[0]
    for s in score[1:]:
        least = jnp.minimum(least, s)
    scale = [jnp.exp(least - s) for s in score]
    total = scale[0]
    for s in scale[1:]:
        total = total + s
    weighted = scale[0] * prior[0].astype(F32)
    for s, x in zip(scale[1:], prior[1:]):
        weighted = weighted + s * x.astype(F32)
    return least, total, weighted


def pieces(x):
    high = x.astype(BF16).astype(F32)
    middle = (x - high).astype(BF16).astype(F32)
    low = (x - high - middle).astype(BF16).astype(F32)
    return high, middle, low


def share_of(ref, member, share):
    if share % LANES == 0:
        return ref[:, pl.ds(pl.multiple_of(member * share, LANES), share)]
    return pltpu.roll(ref[...], ref.shape[1] - member * share, 1)[:, :share]


def pack_mean(outs, at, least, total, sums, share, cycle=0, before=None):
    rows = outs[0].shape[0]
    tiles = sums.shape[0]
    groups = tiles // rows
    m = here()
    lane = iota((rows, LANES), 1)
    misc = jnp.zeros((rows, LANES), F32) if before is None else before
    spot = 6 * groups * cycle
    for x in (least, total):
        for piece in pieces(x):
            for g in range(groups):
                misc = jnp.where(lane == spot, piece[g * rows:(g + 1) * rows, :], misc)
                spot += 1
    end = at + groups * share
    for k, out in enumerate(outs):
        block = share_of(sums, m ^ (2 * k), share)
        for g in range(groups):
            out[:, at + g * share:at + (g + 1) * share] = block[g * rows:(g + 1) * rows, :].astype(BF16)
        out[:, end:end + LANES] = misc.astype(BF16)


def unpack_mean(got, at, end, cycle, tiles, share):
    rows = got[0].shape[0]
    groups = tiles // rows
    misc = [x[:, end:end + LANES].astype(F32) for x in got]
    means = []
    for g in range(groups):
        stats = []
        for x in misc:
            pair = []
            for kind in range(2):
                spot = [((2 * cycle + kind) * 3 + piece) * groups + g for piece in range(3)]
                high, middle, low = [x[:, i:i + 1] for i in spot]
                pair.append(high + middle + low)
            stats.append(pair)
        lowest = stats[0][0]
        for least, _ in stats[1:]:
            lowest = jnp.minimum(lowest, least)
        top, bottom = 0.0, 0.0
        for x, (least, total) in zip(got, stats):
            scale = jnp.exp(lowest - least)
            top = top + scale * x[:, at + g * share:at + (g + 1) * share].astype(F32)
            bottom = bottom + scale * total
        means.append(top / bottom)
    return means


def make_first(parts, tiles, cells):
    def kernel(state, diff, pert, after, prior):
        nothing = jnp.zeros((1, LANES), F32)
        d = widen(diff[...], nothing, nothing)
        for p in range(parts):
            x = diffuse(widen(state[p].astype(F32), nothing, nothing), d)
            now = x[:, LANES:LANES + cells] + pert[0, p].astype(F32)
            prior[p * tiles:(p + 1) * tiles, :] = now.astype(BF16)

    return kernel


def make_send(pairs, rows):
    def kernel(own, other, trail, *refs):
        notes, sends, half = refs[:pairs], refs[pairs:2 * pairs], refs[2 * pairs]
        sends = [sends[falling(pairs).index(k)] for k in range(pairs)]
        prior = jnp.concatenate([own[...], other[...]], axis=0)
        sent = requested([x[...] for x in notes], prior, 0, rows)
        for k in range(pairs):
            sends[k][...] = sent[k * rows:(k + 1) * rows, :].astype(BF16)
        size = padded(pairs)
        half[...] = jnp.zeros(half.shape, F32)
        for k in range(pairs):
            half[k:k + 1, :] = notes[k][...]
        half[size:, :] = trail[...]

    return kernel


def make_assess(pairs, parts, tiles, cells, share):
    size = padded(pairs)

    def kernel(own, other, low, high, where, terms, local, second, *refs):
        outs, stats, weighted_out, sums = refs[:pairs], refs[pairs], refs[pairs + 1], refs[pairs + 2]
        fixed = []
        for h, prior in enumerate((own, other)):
            for p in range(parts):
                row = (2 * p + h) * size
                x = prior[p * tiles:(p + 1) * tiles, :].astype(F32)
                x = patch(x, low[row:row + 1, LANES:], high[row:row + 1, :LANES])
                fixed.append(x.astype(BF16))
        least, total, weighted = assess(
            fixed, where[...], terms[0:1, :], terms[1:2, :], local[...], 2 * parts, tiles, cells
        )
        sums[...] = weighted
        pack_mean(outs, 0, least, total, sums, share)
        least, total, weighted = assess(
            [second[p * tiles:(p + 1) * tiles, :] for p in range(parts)],
            where[...], terms[0:1, :], terms[2:3, :], local[...], parts, tiles, cells,
        )
        stats[...] = jnp.where(iota((tiles, LANES), 1) == 0, least, total)
        weighted_out[...] = weighted

    return kernel


def make_second(pairs, parts, tiles, cells):
    size = padded(pairs)

    def kernel(keys, diff, pert, message, mine, theirs, after, *refs):
        got, prior, low_out, high_out = refs[:pairs], refs[pairs], refs[pairs + 1], refs[pairs + 2]
        got = [got[falling(pairs).index(k)] for k in range(pairs)]
        below, above = halves(mine[...], theirs[...])
        low, high = edge_windows(message[...], below, above, size, parts)
        low_out[...] = low
        high_out[...] = high
        below, above = below[size:size + 8, :], above[size:size + 8, :]
        arrived = jnp.concatenate([x[...] for x in got], axis=0)
        moved = pick_rows(keys[0], arrived)
        here_codes = message[size + 2:size + 2 + 2 * parts, :].astype(I32)
        codes = jnp.concatenate([here_codes[parts:], below[2:2 + parts, :].astype(I32)], axis=0)
        start = pick_rows(codes, low.astype(BF16))
        codes = jnp.concatenate([here_codes[:parts], above[2 + parts:2 + 2 * parts, :].astype(I32)], axis=0)
        end = pick_rows(codes, high.astype(BF16))
        d = widen(diff[...], below[0:1, :], above[1:2, :])
        for p in range(parts):
            x = patch(moved[p * tiles:(p + 1) * tiles, :], start[p:p + 1, LANES:], end[p:p + 1, :LANES])
            q = parts + p
            x = widen(x, start[q:q + 1, :LANES], end[q:q + 1, LANES:])
            x = diffuse(x, d)[:, LANES:LANES + cells]
            prior[p * tiles:(p + 1) * tiles, :] = (x + pert[0, p].astype(F32)).astype(BF16)

    return kernel


def make_send_second(pairs, rows, parts, tiles, cells, share):
    def kernel(own, other, where, terms, local, stats, own_sums, *refs):
        notes, kept, outs, sums = refs[:pairs], refs[pairs:2 * pairs], refs[2 * pairs:3 * pairs], refs[3 * pairs]
        outs = [outs[falling(pairs).index(k)] for k in range(pairs)]
        prior = jnp.concatenate([own[...], other[...]], axis=0)
        sent = requested([x[...] for x in notes], prior, 1, rows)
        extra = kept[0].shape[1] - LANES
        for k in range(pairs):
            outs[k][:, :cells] = sent[k * rows:(k + 1) * rows, :].astype(BF16)
            outs[k][:, cells:cells + extra] = kept[k][:, :extra]
        least, total, weighted = assess(
            [other[p * tiles:(p + 1) * tiles, :] for p in range(parts)],
            where[...], terms[0:1, :], terms[2:3, :], local[...], parts, tiles, cells,
        )
        mine = stats[:, 0:1]
        lower = jnp.minimum(least, mine)
        scale, own_scale = jnp.exp(lower - least), jnp.exp(lower - mine)
        total = scale * total + own_scale * stats[:, 1:2]
        sums[...] = scale * weighted + own_scale * own_sums[...]
        least = lower
        before = kept[0][:, extra:].astype(F32)
        pack_mean(outs, cells + extra, least, total, sums, share, 1, before)

    return kernel


def make_last(pairs, rows, parts, tiles, cells):
    def kernel(keys, *refs):
        got, analysis, mean = refs[:pairs], refs[pairs], refs[pairs + 1]
        got = [got[falling(pairs).index(k)] for k in range(pairs)]
        arrived = jnp.concatenate([x[:, :cells] for x in got], axis=0)
        picked = pick_rows(keys[1], arrived)
        for p in range(parts):
            analysis[p] = picked[p * tiles:(p + 1) * tiles, :].astype(BF16)
        share = mean.shape[2]
        extra = tiles // rows * share
        end = cells + CYCLES * extra
        for c in range(CYCLES):
            for g, x in enumerate(unpack_mean(got, cells + c * extra, end, c, tiles, share)):
                mean[c, g * rows:(g + 1) * rows, :] = x

    return kernel


def body(
    state,
    diffusivity,
    model_perturbation,
    obs_values,
    obs_prec,
    obs_tile,
    obs_cell,
    pattern,
    loc_weight,
    anc_member,
    anc_slot,
):
    parts, tiles, cells = state.shape
    members = lax.axis_size("member")
    regions = lax.axis_size("region")
    capacity = max(2, 2 * parts * tiles // members)
    share = cells // members
    pairs = members // 2
    rows = 2 * capacity
    extra = tiles // rows * share + LANES
    blocks, per_block = obs_cell.shape
    count = blocks * per_block
    member_of = anc_member.reshape(CYCLES, parts, tiles)
    slot_of = anc_slot.reshape(CYCLES, parts, tiles)
    near = pattern.shape[1]
    ends = cells // LANES - 1

    def block(shape, at):
        lead = (0,) * (len(shape) - 1)
        return pl.BlockSpec(shape, lambda i: lead + (at,))

    edges = [state, state, diffusivity, diffusivity, model_perturbation, model_perturbation, member_of, slot_of]
    *notes, trail, keys = call(
        make_prepare(members, capacity, parts, tiles),
        [((1, LANES), F32)] * pairs + [((8, LANES), F32), ((CYCLES, parts * tiles, LANES), I32)],
        [pltpu.with_memory_space_constraint(x, pltpu.HBM) for x in edges],
        [
            block((parts, tiles, LANES), 0),
            block((parts, tiles, LANES), ends),
            block((tiles, LANES), 0),
            block((tiles, LANES), ends),
            block((1, parts, tiles, LANES), 0),
            block((1, parts, tiles, LANES), ends),
            whole_spec(member_of.shape),
            whole_spec(slot_of.shape),
        ],
        name="prepare",
    )

    def trade(x):
        return lax.ppermute(x, "member", [(i, i ^ 1) for i in range(members)])

    def exchange(sends, order):
        got = [sends[0]]
        for x, k in list(zip(sends, order))[1:]:
            got.append(lax.ppermute(x, "member", [(i, i ^ (2 * k)) for i in range(members)]))
        return got

    notes = exchange(notes, range(pairs))

    where, terms, local = call(
        make_observe(blocks, per_block, tiles, near),
        [((2, count), I32), ((1 + CYCLES, count), F32), ((tiles, count), F32)],
        [obs_tile[None, :], obs_cell.T, obs_prec.T, jnp.swapaxes(obs_values, 1, 2), pattern.T, loc_weight.T],
        name="observe",
    )

    def noise_spec(c):
        return pl.BlockSpec((1, parts, tiles, cells), lambda i: (c, 0, 0, 0))

    args = [state, diffusivity, model_perturbation, trail]
    specs = [whole_spec(a.shape) for a in args]
    specs[2] = noise_spec(0)
    (prior,) = call(
        make_first(parts, tiles, cells), [((parts * tiles, cells), BF16)], args, specs, name="forecast_first"
    )
    other = trade(prior)
    size = padded(pairs)
    *sends, half = call(
        make_send(pairs, rows),
        [((rows, cells), BF16)] * pairs + [((size + trail.shape[0], LANES), F32)],
        [prior, other, trail, *notes],
        name="send_first",
    )
    got = exchange(sends, falling(pairs))
    message = jnp.concatenate([half, trade(half)], axis=0)
    steps = []
    for i in range(members):
        first, last = (0, regions - 1) if i % 2 == 0 else (1, regions)
        steps += [(i * regions + r, i * regions + r + 1 - 2 * (i % 2)) for r in range(first, last)]
    mine = lax.ppermute(message, ("member", "region"), steps)
    theirs = trade(mine)
    window = ((parts * 2 * size, 2 * LANES), F32)
    sums = [((tiles, cells), F32)]
    args = [keys, diffusivity, model_perturbation, message, mine, theirs, where, *got]
    specs = [whole_spec(a.shape) for a in args]
    specs[2] = noise_spec(1)
    second, low, high = call(
        make_second(pairs, parts, tiles, cells),
        [((parts * tiles, cells), BF16), window, window],
        args,
        specs,
        name="forecast_second",
    )
    *kept, stats, own_sums = call(
        make_assess(pairs, parts, tiles, cells, share),
        [((rows, extra), BF16)] * pairs + [((tiles, LANES), F32), ((tiles, cells), F32)],
        [prior, other, low, high, where, terms, local, second],
        scratch=sums,
        name="assess_first",
    )
    sends = call(
        make_send_second(pairs, rows, parts, tiles, cells, share),
        [((rows, cells + CYCLES * (extra - LANES) + LANES), BF16)] * pairs,
        [second, trade(second), where, terms, local, stats, own_sums, *notes, *kept],
        scratch=sums,
        name="send_second",
    )
    got = exchange(sends, falling(pairs))
    return tuple(
        call(
            make_last(pairs, rows, parts, tiles, cells),
            [(state.shape, BF16), ((CYCLES, tiles, share), F32)],
            [keys, *got],
            name="finish",
        )
    )


def solution(mesh):
    in_specs = (
        P("member", "region", None),
        P("region", None),
        P(None, "member", "region", None),
        P(None, "region", None),
        P("region", None),
        P("region"),
        P("region", None),
        P("region", None),
        P("region", None),
        P(None, "region", "member", None, None),
        P(None, "region", "member", None),
    )
    out_specs = (P("member", "region", None), P(None, "region", "member"))
    return jax.shard_map(body, mesh=mesh, in_specs=in_specs, out_specs=out_specs, check_vma=False)
```
